128 devices in a mesh: tile: 32 (over z, y, core), date: 4 (over x).
Axes of the slice: x: 4, y: 4, z: 4, core: 2. Of those that a mesh axis runs over, the one named last changes fastest.
Arguments:
- complex_images: bfloat16 [8, 32, 32, 2, 10, 1920], P('date', 'tile')
- segment_position_map: int32 [32, 32], P('tile'), may hold values from 0 to 31, each once within a row
- usable_position_total: int32 [32], P('tile'), may hold values from 16 to 32
- interferogram_epochs: int32 [16, 2], replicated, may hold values from 0 to 7, as said below
Outputs:
- coherence: float32 [16, 2, 64, 4096], P('date', None, None, 'tile')
The draws below stay inside these ranges and needn't reach their ends.
Inputs may be any that keep to these rules, and one draw needn't show every extreme that they name: Each row of segment_position_map names every block position once. `interferogram_epochs`: the two dates of a pair differ.
All inputs are finite; a program needn't handle non-finite values.
Results may differ from the reference program's by a relative error of at most 0.0003.
Values may be sent and summed in bfloat16 or wider, within the bound.
No kernel may reach another device: no remote copies, remote signals or barrier semaphores. Data moves between devices by JAX's collectives and lax.ppermute only.
A program may use at most 128 MiB of HBM per device.

```python
import math
import jax
import jax.numpy as jnp
from jax import lax

SEGMENT_HEIGHT = 10
RG_T = 1920
LOOK_RG = 15
LOOK_AZ = 5
EPOCH_TOTAL = 8
SEGMENT_TOTAL = 32
PATCH_TOTAL = 32
PAIRS = 16
LROWS = 64
LCOL = 128
NLCOL = 4096


def draw_complex_images(key, part):
    seeds = jax.random.split(key, 4)
    extent = (EPOCH_TOTAL, SEGMENT_TOTAL, PATCH_TOTAL, 2, SEGMENT_HEIGHT, RG_T)
    common = (1, SEGMENT_TOTAL, PATCH_TOTAL, 2, SEGMENT_HEIGHT, RG_T)
    shared_portion = jax.random.normal(seeds[0], common)
    noise = jax.random.normal(seeds[1], extent)
    weight = jnp.exp(jax.random.uniform(seeds[2], (EPOCH_TOTAL, 1, 1, 1, 1, 1), minval=math.log(0.3), maxval=math.log(2.0)))
    magnitude_entries = jnp.exp(jax.random.uniform(seeds[3], (1, SEGMENT_TOTAL, PATCH_TOTAL, 1, SEGMENT_HEIGHT, RG_T), minval=math.log(0.3), maxval=math.log(3.0)))
    return (magnitude_entries * (shared_portion + weight * noise)).astype(jnp.bfloat16)


def draw_interferogram_epochs(key, part):
    seeds = jax.random.split(key, 2)
    first = jax.random.randint(seeds[0], (PAIRS,), 0, EPOCH_TOTAL)
    offset = jax.random.randint(seeds[1], (PAIRS,), 1, EPOCH_TOTAL)
    second = (first + offset) % EPOCH_TOTAL
    return jnp.stack([first, second], axis=1).astype(jnp.int32)


def touch_ends(values, stream_key, smallest, top_value):
    dims = values.shape
    place = [jax.random.randint(jax.random.fold_in(stream_key, axis), (), 0, dims[axis]) for axis in range(len(dims))]
    values = values.at[tuple(place)].set(smallest)
    longest = dims.index(max(dims))
    place[longest] = (place[longest] + 1) % dims[longest]
    return values.at[tuple(place)].set(top_value)


def setup_inputs(seed: int = 0) -> dict:
    key_list = jax.random.split(jax.random.key(seed), 5)
    complex_images = draw_complex_images(jax.random.fold_in(key_list[4], 71), 0)
    segment_position_map = jax.vmap(lambda own: jax.random.permutation(own, SEGMENT_TOTAL))(jax.random.split(key_list[1], PATCH_TOTAL)).reshape((PATCH_TOTAL, SEGMENT_TOTAL)).astype(jnp.int32)
    usable_position_total = touch_ends(jax.random.randint(key_list[2], (PATCH_TOTAL,), SEGMENT_TOTAL // 2, SEGMENT_TOTAL + 1), jax.random.fold_in(key_list[2], 1), SEGMENT_TOTAL // 2, SEGMENT_TOTAL).astype(jnp.int32)
    interferogram_epochs = draw_interferogram_epochs(jax.random.fold_in(key_list[4], 71), 0)
    return {"complex_images": complex_images, "segment_position_map": segment_position_map, "usable_position_total": usable_position_total, "interferogram_epochs": interferogram_epochs}


EPS = 1e-05

def tile_looks(stack, first_idx, second_idx, valid, box):
    scale = 1.0 / (LOOK_AZ * LOOK_RG)

    def looks(values):
        ranged = jnp.dot(values, box, precision=lax.Precision.HIGHEST, preferred_element_type=jnp.float32)
        extent = ranged.shape
        return ranged.reshape(extent[:-2] + (extent[-2] // LOOK_AZ, LOOK_AZ, extent[-1])).sum(axis=-2) * scale

    def date_power(image):
        image = image.astype(jnp.float32)
        return looks(image[:, 0] * image[:, 0] + image[:, 1] * image[:, 1])
    power = lax.map(date_power, stack)

    def one_pair(indices):
        first = lax.dynamic_index_in_dim(stack, indices[0], 0, keepdims=False).astype(jnp.float32)
        second = lax.dynamic_index_in_dim(stack, indices[1], 0, keepdims=False).astype(jnp.float32)
        cross_re = looks(first[:, 0] * second[:, 0] + first[:, 1] * second[:, 1])
        cross_im = looks(first[:, 1] * second[:, 0] - first[:, 0] * second[:, 1])
        power_first = lax.dynamic_index_in_dim(power, indices[0], 0, keepdims=False)
        power_second = lax.dynamic_index_in_dim(power, indices[1], 0, keepdims=False)
        weight = valid[:, None, None] / jnp.sqrt((power_first + EPS) * (power_second + EPS))
        return jnp.stack([cross_re * weight, cross_im * weight], axis=0)
    return lax.map(one_pair, jnp.stack([first_idx, second_idx], axis=1).astype(jnp.int32))

def reference(complex_images, segment_position_map, usable_position_total, interferogram_epochs):
    box = (jnp.arange(RG_T)[:, None] // LOOK_RG == jnp.arange(LCOL)[None, :]).astype(jnp.float32)

    def one_tile(patch_ordinal):
        stack = lax.dynamic_index_in_dim(complex_images, patch_ordinal, 2, keepdims=False)
        positions = segment_position_map[patch_ordinal]
        valid = (positions < usable_position_total[patch_ordinal]).astype(jnp.float32)
        gamma = tile_looks(stack, interferogram_epochs[:, 0], interferogram_epochs[:, 1], valid, box)
        ranking = jnp.argsort(positions).astype(jnp.int32)
        gamma = jnp.take(gamma, ranking, axis=2)
        return gamma.reshape(PAIRS, 2, LROWS, LCOL)
    result = lax.map(one_tile, jnp.arange(PATCH_TOTAL, dtype=jnp.int32))
    return result.transpose(1, 2, 3, 0, 4).reshape(PAIRS, 2, LROWS, NLCOL)
```

```python
import functools

import jax
import jax.numpy as jnp
from jax import lax
from jax.experimental import pallas as pl
from jax.experimental.pallas import tpu as pltpu
from jax.sharding import PartitionSpec as P

LOOK_RG = 15
LOOK_AZ = 5
EPS = 1e-05
SCALE = 1.0 / (LOOK_AZ * LOOK_RG)
DATES = 8
PAIRS = 16
ITEMS = 8
RG = 1920
LCOL = 128


def look_kernel(info, own, one, two, three, box, out, img, hi, lo, sums):
    group = info[2 * PAIRS]
    for step, block in enumerate((own, one, two, three)):
        base = lax.rem(group + step, 4) * 2
        for date in range(2):
            for line in range(LOOK_AZ):
                img[base + date, line] = block[date, line].astype(jnp.float32)

    def split(values, row):
        upper = values.astype(jnp.bfloat16)
        hi[pl.ds(row, 16), :] = upper
        lo[pl.ds(row, 16), :] = (values - upper.astype(jnp.float32)).astype(jnp.bfloat16)

    def power(half, carry):
        total = []
        for date in range(2):
            acc = jnp.zeros((ITEMS, RG), jnp.float32)
            for line in range(LOOK_AZ):
                re = img[2 * half + date, line, 0:8, :]
                im = img[2 * half + date, line, 8:16, :]
                acc = acc + (re * re + im * im)
            total.append(acc)
        split(jnp.concatenate(total, axis=0), pl.multiple_of(half * 16, 16))
        return carry

    lax.fori_loop(0, DATES // 2, power, 0)

    def cross(k, carry):
        a, b = info[2 * k], info[2 * k + 1]
        acc_re = jnp.zeros((ITEMS, RG), jnp.float32)
        acc_im = jnp.zeros((ITEMS, RG), jnp.float32)
        for line in range(LOOK_AZ):
            re_a, im_a = img[a, line, 0:8, :], img[a, line, 8:16, :]
            re_b, im_b = img[b, line, 0:8, :], img[b, line, 8:16, :]
            acc_re = acc_re + (re_a * re_b + im_a * im_b)
            acc_im = acc_im + (im_a * re_b - re_a * im_b)
        split(jnp.concatenate([acc_re, acc_im], axis=0), pl.multiple_of(64 + k * 16, 16))
        return carry

    lax.fori_loop(0, PAIRS, cross, 0)
    sums[...] = (
        jnp.dot(hi[...], box[...], preferred_element_type=jnp.float32)
        + jnp.dot(lo[...], box[...], preferred_element_type=jnp.float32)
    ) * SCALE

    for owner in range(4):
        rows = []
        for kk in range(4):
            k = owner * 4 + kk
            power_a = sums[pl.ds(pl.multiple_of(info[2 * k] * 8, 8), 8), :]
            power_b = sums[pl.ds(pl.multiple_of(info[2 * k + 1] * 8, 8), 8), :]
            weight = 1.0 / jnp.sqrt((power_a + EPS) * (power_b + EPS))
            rows.append(sums[64 + k * 16 : 72 + k * 16, :] * weight)
            rows.append(sums[72 + k * 16 : 80 + k * 16, :] * weight)
        out[owner] = jnp.swapaxes(jnp.stack(rows, axis=0), 0, 1)


def place_kernel(positions, usable, got, out, rows):
    for block in range(32):
        position = positions[block]
        valid = jnp.where(position < usable[0], 1.0, 0.0).astype(jnp.float32)
        rows[pl.ds(pl.multiple_of(position * 16, 16), 16), :] = got[block] * valid
    for plane in range(8):
        for part in range(8):
            out[plane // 2, plane % 2, part * 8 : part * 8 + 8, :] = rows[
                pl.ds(part * 64 + plane, 8, stride=8), :
            ]


def on_device(complex_images, segment_position_map, usable_position_total, interferogram_epochs):
    group = lax.axis_index("date")
    images = complex_images[:, 0]

    def block_for(step):
        part = lax.dynamic_slice_in_dim(images, lax.rem(group + step, 4) * ITEMS, ITEMS, 1)
        return part.transpose(0, 3, 2, 1, 4).reshape(2, 10, 16, RG)

    def ring(step):
        return [(i, (i + step) % 4) for i in range(4)]

    own = block_for(0)
    two = lax.ppermute(block_for(2), "date", ring(2))
    three = lax.ppermute(block_for(1), "date", ring(1))
    one = lax.ppermute(block_for(3), "date", ring(3))

    box = (
        jnp.arange(RG)[:, None] // LOOK_RG == jnp.arange(LCOL)[None, :]
    ).astype(jnp.bfloat16)
    info = jnp.concatenate(
        [interferogram_epochs.reshape(-1), group.reshape(1)]
    ).astype(jnp.int32)

    block = pl.BlockSpec((2, LOOK_AZ, 16, RG), lambda r, info: (0, r, 0, 0))
    gamma = pl.pallas_call(
        look_kernel,
        out_shape=jax.ShapeDtypeStruct((4, ITEMS, 16, LCOL), jnp.float32),
        grid_spec=pltpu.PrefetchScalarGridSpec(
            num_scalar_prefetch=1,
            grid=(2,),
            in_specs=[block] * 4 + [pl.BlockSpec((RG, LCOL), lambda r, info: (0, 0))],
            out_specs=pl.BlockSpec((4, ITEMS, 8, LCOL), lambda r, info: (0, 0, r, 0)),
            scratch_shapes=[
                pltpu.VMEM((DATES, LOOK_AZ, 16, RG), jnp.float32),
                pltpu.VMEM((320, RG), jnp.bfloat16),
                pltpu.VMEM((320, RG), jnp.bfloat16),
                pltpu.VMEM((320, LCOL), jnp.float32),
            ],
        ),
        compiler_params=pltpu.CompilerParams(vmem_limit_bytes=40 << 20),
    )(info, own, one, two, three, box)

    moved = lax.all_to_all(gamma, "date", split_axis=0, concat_axis=0, tiled=True)
    moved = moved.reshape(32, 16, LCOL)
    got = lax.all_to_all(moved, "tile", split_axis=0, concat_axis=0, tiled=True)

    return pl.pallas_call(
        place_kernel,
        out_shape=jax.ShapeDtypeStruct((4, 2, 64, LCOL), jnp.float32),
        grid_spec=pltpu.PrefetchScalarGridSpec(
            num_scalar_prefetch=2,
            grid=(),
            in_specs=[pl.BlockSpec(memory_space=pltpu.VMEM)],
            out_specs=pl.BlockSpec(memory_space=pltpu.VMEM),
            scratch_shapes=[pltpu.VMEM((512, LCOL), jnp.float32)],
        ),
    )(segment_position_map[0], usable_position_total, got)


def solution(mesh):
    in_specs = (P("date", "tile", None, None, None, None), P("tile", None), P("tile"), P())
    out_specs = P("date", None, None, "tile")
    return jax.shard_map(
        on_device, mesh=mesh, in_specs=in_specs, out_specs=out_specs, check_vma=False
    )
```

```python
import functools

import jax
import jax.numpy as jnp
from jax import lax
from jax.experimental import pallas as pl
from jax.experimental.pallas import tpu as pltpu
from jax.sharding import PartitionSpec as P

LOOK_RG = 15
LOOK_AZ = 5
EPS = 1e-05
SCALE = 1.0 / (LOOK_AZ * LOOK_RG)
DATES = 8
PAIRS = 16
ITEMS = 8
RG = 1920
LCOL = 128
ROWS = 320
SPLIT = 7


def look_kernel(lines, first, last, info, own, one, two, three, box, *rest):
    if first:
        out, img, hi, lo, sums = rest
    else:
        before, out, img, hi, lo, sums = rest
    group = info[2 * PAIRS]
    for step, block in enumerate((own, one, two, three)):
        base = lax.rem(group + step, 4) * 2
        for date in range(2):
            for line in range(lines):
                pixels = jnp.swapaxes(block[:, date, line], 0, 1).reshape(16, RG)
                img[base + date, line] = pixels.astype(jnp.float32)

    def split(values, row):
        upper = values.astype(jnp.bfloat16)
        hi[pl.ds(row, 16), :] = upper
        lo[pl.ds(row, 16), :] = (values - upper.astype(jnp.float32)).astype(jnp.bfloat16)

    def power(half, carry):
        total = []
        for date in range(2):
            acc = jnp.zeros((ITEMS, RG), jnp.float32)
            for line in range(lines):
                re = img[2 * half + date, line, 0:8, :]
                im = img[2 * half + date, line, 8:16, :]
                acc = acc + (re * re + im * im)
            total.append(acc)
        split(jnp.concatenate(total, axis=0), pl.multiple_of(half * 16, 16))
        return carry

    lax.fori_loop(0, DATES // 2, power, 0)

    def cross(k, carry):
        a, b = info[2 * k], info[2 * k + 1]
        acc_re = jnp.zeros((ITEMS, RG), jnp.float32)
        acc_im = jnp.zeros((ITEMS, RG), jnp.float32)
        for line in range(lines):
            re_a, im_a = img[a, line, 0:8, :], img[a, line, 8:16, :]
            re_b, im_b = img[b, line, 0:8, :], img[b, line, 8:16, :]
            acc_re = acc_re + (re_a * re_b + im_a * im_b)
            acc_im = acc_im + (im_a * re_b - re_a * im_b)
        split(jnp.concatenate([acc_re, acc_im], axis=0), pl.multiple_of(64 + k * 16, 16))
        return carry

    lax.fori_loop(0, PAIRS, cross, 0)
    total = jnp.dot(hi[...], box[...], preferred_element_type=jnp.float32) + jnp.dot(
        lo[...], box[...], preferred_element_type=jnp.float32
    )
    if not first:
        total = total + before[...]
    if not last:
        out[...] = total
        return
    sums[...] = total * SCALE

    for owner in range(4):
        rows = []
        for kk in range(4):
            k = owner * 4 + kk
            power_a = sums[pl.ds(pl.multiple_of(info[2 * k] * 8, 8), 8), :]
            power_b = sums[pl.ds(pl.multiple_of(info[2 * k + 1] * 8, 8), 8), :]
            weight = 1.0 / jnp.sqrt((power_a + EPS) * (power_b + EPS))
            rows.append(sums[64 + k * 16 : 72 + k * 16, :] * weight)
            rows.append(sums[72 + k * 16 : 80 + k * 16, :] * weight)
        out[owner] = jnp.swapaxes(jnp.stack(rows, axis=0), 0, 1)


def looks(info, blocks, box, before, last):
    lines = blocks[0].shape[2]
    first = before is None
    vmem = pl.BlockSpec(memory_space=pltpu.VMEM)
    operands = (info, *blocks, box) + (() if first else (before,))
    shape = (4, ITEMS, 8, LCOL) if last else (ROWS, LCOL)
    work = lines * ITEMS * RG * (PAIRS * 8 + DATES * 4) + 4 * ROWS * RG * LCOL
    return pl.pallas_call(
        functools.partial(look_kernel, lines, first, last),
        out_shape=jax.ShapeDtypeStruct(shape, jnp.float32),
        grid_spec=pltpu.PrefetchScalarGridSpec(
            num_scalar_prefetch=1,
            grid=(),
            in_specs=[vmem] * (len(operands) - 1),
            out_specs=vmem,
            scratch_shapes=[
                pltpu.VMEM((DATES, lines, 16, RG), jnp.float32),
                pltpu.VMEM((ROWS, RG), jnp.bfloat16),
                pltpu.VMEM((ROWS, RG), jnp.bfloat16),
                pltpu.VMEM((ROWS, LCOL), jnp.float32),
            ],
        ),
        cost_estimate=pl.CostEstimate(
            flops=work, bytes_accessed=DATES * lines * 16 * RG * 2, transcendentals=0
        ),
        compiler_params=pltpu.CompilerParams(vmem_limit_bytes=24 << 20),
    )(*operands)


def place_kernel(positions, usable, got0, got1, out, rows):
    for block in range(32):
        position = positions[block]
        valid = jnp.where(position < usable[0], 1.0, 0.0).astype(jnp.float32)
        base = pl.multiple_of(position * 16, 16)
        rows[pl.ds(base, 8), :] = got0[block] * valid
        rows[pl.ds(base + 8, 8), :] = got1[block] * valid
    for plane in range(8):
        for part in range(8):
            out[plane // 2, plane % 2, part * 8 : part * 8 + 8, :] = rows[
                pl.ds(part * 64 + plane, 8, stride=8), :
            ]


def cut_direct_kernel(info, images, own, to1, to2, to3, sem):
    group = info[2 * PAIRS]
    copies = []
    for step, out in ((1, to1), (3, to3), (2, to2), (0, own)):
        tiles = pl.ds(lax.rem(group + step, 4) * ITEMS, ITEMS)
        for date in range(2):
            copies.append(
                pltpu.make_async_copy(
                    images.at[date, tiles, 0:LOOK_AZ], out.at[:, date], sem.at[len(copies)]
                )
            )
            copies[-1].start()
    for copy in copies:
        copy.wait()


def cut_tile_kernel(images, after, part_a, part_b, sem):
    del after
    copies = []
    for low, high, out in ((5, SPLIT, part_a), (SPLIT, 10, part_b)):
        for date in range(2):
            copies.append(
                pltpu.make_async_copy(
                    images.at[date, :, low:high], out.at[:, date], sem.at[len(copies)]
                )
            )
            copies[-1].start()
    for copy in copies:
        copy.wait()


def cut_direct(info, images):
    block = jax.ShapeDtypeStruct((ITEMS, 2, LOOK_AZ, 2, RG), jnp.bfloat16)
    anywhere = pl.BlockSpec(memory_space=pl.ANY)
    return pl.pallas_call(
        cut_direct_kernel,
        out_shape=[block] * 4,
        grid_spec=pltpu.PrefetchScalarGridSpec(
            num_scalar_prefetch=1,
            grid=(),
            in_specs=[anywhere],
            out_specs=[anywhere] * 4,
            scratch_shapes=[pltpu.SemaphoreType.DMA((8,))],
        ),
    )(info, images)


def cut_tile(images, after):
    anywhere = pl.BlockSpec(memory_space=pl.ANY)
    return pl.pallas_call(
        cut_tile_kernel,
        out_shape=[
            jax.ShapeDtypeStruct((32, 2, lines, 2, RG), jnp.bfloat16)
            for lines in (SPLIT - 5, 10 - SPLIT)
        ],
        in_specs=[anywhere] * 2,
        out_specs=[anywhere] * 2,
        scratch_shapes=[pltpu.SemaphoreType.DMA((4,))],
    )(images, after)


def meet(own, to1, to2, to3):
    def ring(step):
        return [(i, (i + step) % 4) for i in range(4)]

    three = lax.ppermute(to1, "date", ring(1))
    one = lax.ppermute(to3, "date", ring(3))
    two = lax.ppermute(to2, "date", ring(2))
    return own, one, two, three


def on_device(complex_images, segment_position_map, usable_position_total, interferogram_epochs):
    group = lax.axis_index("date")
    images = complex_images[:, 0].transpose(0, 1, 3, 2, 4)
    info = jnp.concatenate(
        [interferogram_epochs.reshape(-1), group.reshape(1)]
    ).astype(jnp.int32)
    box = (
        jnp.arange(RG)[:, None] // LOOK_RG == jnp.arange(LCOL)[None, :]
    ).astype(jnp.bfloat16)

    def through_tile(part):
        came = lax.all_to_all(part, "tile", split_axis=0, concat_axis=0, tiled=True)
        return [
            lax.dynamic_slice_in_dim(came, lax.rem(group + step, 4) * ITEMS, ITEMS, 0)
            for step in range(4)
        ]

    direct = cut_direct(info, images)
    row0 = meet(*direct)
    part_a, part_b = cut_tile(images, direct[2])
    row1a = meet(*through_tile(part_a))
    row1b = meet(*through_tile(part_b))

    gamma0 = looks(info, row0, box, None, True)
    moved = lax.all_to_all(gamma0, "date", split_axis=0, concat_axis=0, tiled=True)
    got0 = lax.all_to_all(
        moved.reshape(32, 8, LCOL), "tile", split_axis=0, concat_axis=0, tiled=True
    )

    sums1 = looks(info, row1a, box, None, False)
    gamma1 = looks(info, row1b, box, sums1, True)
    got1 = lax.all_to_all(gamma1, "date", split_axis=0, concat_axis=0, tiled=True)

    vmem = pl.BlockSpec(memory_space=pltpu.VMEM)
    return pl.pallas_call(
        place_kernel,
        out_shape=jax.ShapeDtypeStruct((4, 2, 64, LCOL), jnp.float32),
        grid_spec=pltpu.PrefetchScalarGridSpec(
            num_scalar_prefetch=2,
            grid=(),
            in_specs=[vmem, vmem],
            out_specs=vmem,
            scratch_shapes=[pltpu.VMEM((512, LCOL), jnp.float32)],
        ),
    )(segment_position_map[0], usable_position_total, got0, got1.reshape(32, 8, LCOL))


def solution(mesh):
    in_specs = (P("date", "tile", None, None, None, None), P("tile", None), P("tile"), P())
    out_specs = P("date", None, None, "tile")
    return jax.shard_map(
        on_device, mesh=mesh, in_specs=in_specs, out_specs=out_specs, check_vma=False
    )
```

```python
import functools

import jax
import jax.numpy as jnp
from jax import lax
from jax.experimental import pallas as pl
from jax.experimental.pallas import tpu as pltpu
from jax.sharding import PartitionSpec as P

LOOK_RG = 15
LOOK_AZ = 5
EPS = 1e-05
SCALE = 1.0 / (LOOK_AZ * LOOK_RG)
DATES = 8
PAIRS = 16
ITEMS = 8
LINES = 10
RG = 1920
LCOL = 128
ROWS = 320
SPLIT = 8

VMEM = pl.BlockSpec(memory_space=pltpu.VMEM)
HBM = pl.BlockSpec(memory_space=pltpu.HBM)
ANYWHERE = pl.BlockSpec(memory_space=pl.ANY)


def cut_kernel(low, high, info, images, *rest):
    to1, to2, to3, own, sem = rest[-5:]
    group = info[2 * PAIRS]
    copies = []
    for step, out in ((1, to1), (3, to3), (2, to2), (0, own)):
        tiles = pl.ds(lax.rem(group + step, 4) * ITEMS, ITEMS)
        for date in range(2):
            copies.append(
                pltpu.make_async_copy(
                    images.at[date, tiles, low:high], out.at[:, date], sem.at[len(copies)]
                )
            )
            copies[-1].start()
    for copy in copies:
        copy.wait()


def cut(info, images, low, high, after=None):
    block = jax.ShapeDtypeStruct((ITEMS, 2, high - low, 2, RG), jnp.bfloat16)
    operands = (info, images) + (() if after is None else (after,))
    return pl.pallas_call(
        functools.partial(cut_kernel, low, high),
        out_shape=[block] * 4,
        grid_spec=pltpu.PrefetchScalarGridSpec(
            num_scalar_prefetch=1,
            grid=(),
            in_specs=[HBM, ANYWHERE][: len(operands) - 1],
            out_specs=[VMEM] * 4,
            scratch_shapes=[pltpu.SemaphoreType.DMA((8,))],
        ),
        compiler_params=pltpu.CompilerParams(vmem_limit_bytes=8 << 20),
    )(*operands)


def meet(to1, to2, to3, own):
    def ring(step):
        return [(i, (i + step) % 4) for i in range(4)]

    three = lax.ppermute(to1, "date", ring(1))
    one = lax.ppermute(to3, "date", ring(3))
    two = lax.ppermute(to2, "date", ring(2))
    return own, one, two, three


def add_lines(info, blocks, low, high, box, img, hi, lo):
    group = info[2 * PAIRS]
    lines = high - low
    for step, block in enumerate(blocks):
        base = lax.rem(group + step, 4) * 2
        for date in range(2):
            for line in range(lines):
                pixels = jnp.swapaxes(block[:, date, low + line], 0, 1).reshape(16, RG)
                img[base + date, line] = pixels.astype(jnp.float32)

    def split(values, row):
        upper = values.astype(jnp.bfloat16)
        hi[pl.ds(row, 16), :] = upper
        lo[pl.ds(row, 16), :] = (values - upper.astype(jnp.float32)).astype(jnp.bfloat16)

    def power(half, carry):
        total = []
        for date in range(2):
            acc = jnp.zeros((ITEMS, RG), jnp.float32)
            for line in range(lines):
                re = img[2 * half + date, line, 0:8, :]
                im = img[2 * half + date, line, 8:16, :]
                acc = acc + (re * re + im * im)
            total.append(acc)
        split(jnp.concatenate(total, axis=0), pl.multiple_of(half * 16, 16))
        return carry

    lax.fori_loop(0, DATES // 2, power, 0)

    def cross(k, carry):
        a, b = info[2 * k], info[2 * k + 1]
        acc_re = jnp.zeros((ITEMS, RG), jnp.float32)
        acc_im = jnp.zeros((ITEMS, RG), jnp.float32)
        for line in range(lines):
            re_a, im_a = img[a, line, 0:8, :], img[a, line, 8:16, :]
            re_b, im_b = img[b, line, 0:8, :], img[b, line, 8:16, :]
            acc_re = acc_re + (re_a * re_b + im_a * im_b)
            acc_im = acc_im + (im_a * re_b - re_a * im_b)
        split(jnp.concatenate([acc_re, acc_im], axis=0), pl.multiple_of(64 + k * 16, 16))
        return carry

    lax.fori_loop(0, PAIRS, cross, 0)
    return jnp.dot(hi[...], box[...], preferred_element_type=jnp.float32) + jnp.dot(
        lo[...], box[...], preferred_element_type=jnp.float32
    )


def early_kernel(info, own, one, two, three, box, sums0, sums1, img, hi, lo):
    blocks = (own, one, two, three)
    sums0[...] = add_lines(info, blocks, 0, LOOK_AZ, box, img, hi, lo)
    sums1[...] = add_lines(info, blocks, LOOK_AZ, SPLIT, box, img, hi, lo)


def late_kernel(info, own, one, two, three, box, early0, early1, out, img, hi, lo, sums):
    blocks = (own, one, two, three)
    sums[0] = early0[...] * SCALE
    total = add_lines(info, blocks, 0, LINES - SPLIT, box, img, hi, lo)
    sums[1] = (total + early1[...]) * SCALE
    for owner in range(4):
        for look in range(2):
            rows = []
            for kk in range(4):
                k = owner * 4 + kk
                power_a = sums[look, pl.ds(pl.multiple_of(info[2 * k] * 8, 8), 8), :]
                power_b = sums[look, pl.ds(pl.multiple_of(info[2 * k + 1] * 8, 8), 8), :]
                weight = 1.0 / jnp.sqrt((power_a + EPS) * (power_b + EPS))
                rows.append(sums[look, 64 + k * 16 : 72 + k * 16, :] * weight)
                rows.append(sums[look, 72 + k * 16 : 80 + k * 16, :] * weight)
            out[owner, :, look * 8 : look * 8 + 8, :] = jnp.swapaxes(
                jnp.stack(rows, axis=0), 0, 1
            )


def looks(kernel, info, operands, out_shape, lines, scratch=()):
    work = lines * ITEMS * RG * (PAIRS * 8 + DATES * 4) + 4 * ROWS * RG * LCOL
    return pl.pallas_call(
        kernel,
        out_shape=out_shape,
        grid_spec=pltpu.PrefetchScalarGridSpec(
            num_scalar_prefetch=1,
            grid=(),
            in_specs=[VMEM] * len(operands),
            out_specs=jax.tree.map(lambda _: VMEM, out_shape),
            scratch_shapes=[
                pltpu.VMEM((DATES, min(lines, LOOK_AZ), 16, RG), jnp.float32),
                pltpu.VMEM((ROWS, RG), jnp.bfloat16),
                pltpu.VMEM((ROWS, RG), jnp.bfloat16),
                *scratch,
            ],
        ),
        cost_estimate=pl.CostEstimate(
            flops=work, bytes_accessed=DATES * lines * 16 * RG * 2, transcendentals=0
        ),
        compiler_params=pltpu.CompilerParams(vmem_limit_bytes=24 << 20),
    )(info, *operands)


def place_kernel(positions, usable, got, out, rows):
    for block in range(32):
        position = positions[block]
        valid = jnp.where(position < usable[0], 1.0, 0.0).astype(jnp.float32)
        rows[pl.ds(pl.multiple_of(position * 16, 16), 16), :] = got[block] * valid
    for plane in range(8):
        for part in range(8):
            out[plane // 2, plane % 2, part * 8 : part * 8 + 8, :] = rows[
                pl.ds(part * 64 + plane, 8, stride=8), :
            ]


def on_device(complex_images, segment_position_map, usable_position_total, interferogram_epochs):
    group = lax.axis_index("date")
    images = complex_images[:, 0].transpose(0, 1, 3, 2, 4)
    info = jnp.concatenate(
        [interferogram_epochs.reshape(-1), group.reshape(1)]
    ).astype(jnp.int32)
    box = (
        jnp.arange(RG)[:, None] // LOOK_RG == jnp.arange(LCOL)[None, :]
    ).astype(jnp.bfloat16)

    early = meet(*cut(info, images, 0, SPLIT))
    late = meet(*cut(info, images, SPLIT, LINES, early[3]))

    partial = jax.ShapeDtypeStruct((ROWS, LCOL), jnp.float32)
    sums0, sums1 = looks(early_kernel, info, (*early, box), (partial, partial), SPLIT)
    gamma = looks(
        late_kernel,
        info,
        (*late, box, sums0, sums1),
        jax.ShapeDtypeStruct((4, ITEMS, 16, LCOL), jnp.float32),
        LINES - SPLIT,
        (pltpu.VMEM((2, ROWS, LCOL), jnp.float32),),
    )

    moved = lax.all_to_all(gamma, "date", split_axis=0, concat_axis=0, tiled=True)
    got = lax.all_to_all(
        moved.reshape(32, 16, LCOL), "tile", split_axis=0, concat_axis=0, tiled=True
    )
    return pl.pallas_call(
        place_kernel,
        out_shape=jax.ShapeDtypeStruct((4, 2, 64, LCOL), jnp.float32),
        grid_spec=pltpu.PrefetchScalarGridSpec(
            num_scalar_prefetch=2,
            grid=(),
            in_specs=[VMEM],
            out_specs=VMEM,
            scratch_shapes=[pltpu.VMEM((512, LCOL), jnp.float32)],
        ),
        compiler_params=pltpu.CompilerParams(vmem_limit_bytes=4 << 20),
    )(segment_position_map[0], usable_position_total, got)


def solution(mesh):
    in_specs = (P("date", "tile", None, None, None, None), P("tile", None), P("tile"), P())
    out_specs = P("date", None, None, "tile")
    return jax.shard_map(
        on_device, mesh=mesh, in_specs=in_specs, out_specs=out_specs, check_vma=False
    )
```

```python
import functools

import jax
import jax.numpy as jnp
from jax import lax
from jax.experimental import pallas as pl
from jax.experimental.pallas import tpu as pltpu
from jax.sharding import Mesh, PartitionSpec as P

LOOK_RG = 15
LOOK_AZ = 5
EPS = 1e-05
SCALE = 1.0 / (LOOK_AZ * LOOK_RG)
DATES = 8
PAIRS = 16
LINES = 10
RG = 1920
LCOL = 128
ROWS = (DATES + PAIRS) * 8
UNIT = (2, 2, LINES, 2, RG)

VMEM = pl.BlockSpec(memory_space=pltpu.VMEM)
HBM = pl.BlockSpec(memory_space=pltpu.HBM)
TOKEN = jax.ShapeDtypeStruct((8, LCOL), jnp.float32)


def cut_date_kernel(turns, images, *rest):
    to1, to2, to3, own, token, sem = rest[-6:]
    token[...] = jnp.zeros_like(token)
    group, y = lax.axis_index("date"), lax.axis_index("y")
    copies = []
    for step, out in ((1, to1), (3, to3), (2, to2), (0, own)):
        z = lax.rem(group + step, 4)
        for unit, turn in enumerate(turns):
            tiles = pl.ds(z * 8 + lax.rem(y + turn, 4) * 2, 2)
            for date in range(2):
                copies.append(
                    pltpu.make_async_copy(
                        images.at[date, tiles], out.at[unit, :, date], sem.at[len(copies)]
                    )
                )
                copies[-1].start()
    for copy in copies:
        copy.wait()


def cut_date(images, turns, after=None):
    operands = (images,) + (() if after is None else (after,))
    return pl.pallas_call(
        functools.partial(cut_date_kernel, turns),
        out_shape=[jax.ShapeDtypeStruct((len(turns), *UNIT), jnp.bfloat16)] * 4 + [TOKEN],
        in_specs=[HBM, VMEM][: len(operands)],
        out_specs=[VMEM] * 5,
        scratch_shapes=[pltpu.SemaphoreType.DMA((8 * len(turns),))],
        compiler_params=pltpu.CompilerParams(vmem_limit_bytes=48 << 20),
    )(*operands)


def cut_tile_kernel(images, after, out, sem):
    del after
    y = lax.axis_index("y")
    copies = []
    for z in range(4):
        for date in range(2):
            copies.append(
                pltpu.make_async_copy(
                    images.at[date, pl.ds(z * 8 + y * 2, 2)],
                    out.at[2 * z : 2 * z + 2, date],
                    sem.at[len(copies)],
                )
            )
            copies[-1].start()
    for copy in copies:
        copy.wait()


def cut_tile(images, after):
    return pl.pallas_call(
        cut_tile_kernel,
        out_shape=jax.ShapeDtypeStruct((8, 2, LINES, 2, RG), jnp.bfloat16),
        in_specs=[HBM, VMEM],
        out_specs=VMEM,
        scratch_shapes=[pltpu.SemaphoreType.DMA((8,))],
        compiler_params=pltpu.CompilerParams(vmem_limit_bytes=48 << 20),
    )(images, after)


def cut_crossed_kernel(crossed, to1, to2, to3, own, token, sem):
    token[...] = jnp.zeros_like(token)
    group = lax.axis_index("date")
    copies = []
    for step, out in ((1, to1), (3, to3), (2, to2), (0, own)):
        bursts = pl.ds(lax.rem(group + step, 4) * 2, 2)
        copies.append(pltpu.make_async_copy(crossed.at[bursts], out.at[0], sem.at[step]))
        copies[-1].start()
    for copy in copies:
        copy.wait()


def cut_crossed(crossed):
    return pl.pallas_call(
        cut_crossed_kernel,
        out_shape=[jax.ShapeDtypeStruct((1, *UNIT), jnp.bfloat16)] * 4 + [TOKEN],
        in_specs=[HBM],
        out_specs=[VMEM] * 5,
        scratch_shapes=[pltpu.SemaphoreType.DMA((4,))],
        compiler_params=pltpu.CompilerParams(vmem_limit_bytes=8 << 20),
    )(crossed)


def meet(to1, to2, to3, own):
    def ring(step):
        return [(i, (i + step) % 4) for i in range(4)]

    three = lax.ppermute(to1, "date", ring(1))
    one = lax.ppermute(to3, "date", ring(3))
    two = lax.ppermute(to2, "date", ring(2))
    return own, one, two, three


def unit_looks(epochs, blocks, box, img, swp, hi, lo, sums, gamma):
    group = lax.axis_index("date")
    even = lax.broadcasted_iota(jnp.int32, (8, RG), 0) % 2 == 0

    for step, block in enumerate(blocks):
        base = lax.rem(group + step, 4) * 2
        for date in range(2):
            for line in range(LOOK_AZ):
                pixels = jnp.concatenate(
                    [block[:, date, line], block[:, date, LOOK_AZ + line]], axis=0
                )
                pixels = pixels.reshape(8, RG).astype(jnp.float32)
                img[base + date, line] = pixels
                swp[base + date, line] = jnp.where(
                    even, -pltpu.roll(pixels, 7, 0), pltpu.roll(pixels, 1, 0)
                )

    def split(values, row):
        upper = values.astype(jnp.bfloat16)
        hi[pl.ds(row, 16), :] = upper
        lo[pl.ds(row, 16), :] = (values - upper.astype(jnp.float32)).astype(jnp.bfloat16)

    def joined(first, second):
        return jnp.where(
            even, first + pltpu.roll(first, 7, 0), second + pltpu.roll(second, 1, 0)
        )

    def power(half, carry):
        total = []
        for date in range(2):
            acc = jnp.zeros((8, RG), jnp.float32)
            for line in range(LOOK_AZ):
                pixels = img[2 * half + date, line]
                acc = acc + pixels * pixels
            total.append(joined(acc, acc))
        split(jnp.concatenate(total, axis=0), pl.multiple_of(half * 16, 16))
        return carry

    lax.fori_loop(0, DATES // 2, power, 0)

    def cross(half, carry):
        total = []
        for k in (2 * half, 2 * half + 1):
            a, b = epochs[0, k], epochs[1, k]
            same = jnp.zeros((8, RG), jnp.float32)
            other = jnp.zeros((8, RG), jnp.float32)
            for line in range(LOOK_AZ):
                pixels = img[a, line]
                same = same + pixels * img[b, line]
                other = other + pixels * swp[b, line]
            total.append(joined(same, other))
        split(jnp.concatenate(total, axis=0), pl.multiple_of(64 + half * 16, 16))
        return carry

    lax.fori_loop(0, PAIRS // 2, cross, 0)
    sums[...] = (
        jnp.dot(hi[...], box[...], preferred_element_type=jnp.float32)
        + jnp.dot(lo[...], box[...], preferred_element_type=jnp.float32)
    ) * SCALE
    for k in range(PAIRS):
        power_a = sums[pl.ds(pl.multiple_of(epochs[0, k] * 8, 8), 8), :]
        power_b = sums[pl.ds(pl.multiple_of(epochs[1, k] * 8, 8), 8), :]
        weight = 1.0 / jnp.sqrt((power_a + EPS) * (power_b + EPS))
        gamma[8 * k : 8 * k + 8, :] = sums[64 + 8 * k : 72 + 8 * k, :] * weight


def to_owner(gamma, owner, out):
    for item in range(2):
        for look in range(2):
            for part in range(2):
                row = look * 8 + part * 4
                out[item, row : row + 4, :] = gamma[
                    pl.ds(owner * 32 + look * 4 + item * 2 + part, 4, stride=8), :
                ]


def to_owners(gamma, out):
    for owner in range(4):
        to_owner(gamma, owner, out.at[:, owner])


WORK = [
    pltpu.VMEM((DATES, LOOK_AZ, 8, RG), jnp.float32),
    pltpu.VMEM((DATES, LOOK_AZ, 8, RG), jnp.float32),
    pltpu.VMEM((ROWS, RG), jnp.bfloat16),
    pltpu.VMEM((ROWS, RG), jnp.bfloat16),
    pltpu.VMEM((ROWS, LCOL), jnp.float32),
    pltpu.VMEM((PAIRS * 8, LCOL), jnp.float32),
]


def plain_kernel(units, epochs, own, one, two, three, box, out, *work):
    for unit in range(units):
        blocks = [block.at[unit] for block in (own, one, two, three)]
        unit_looks(epochs, blocks, box, *work)
        to_owners(work[-1], out.at[unit])


def last_kernel(epochs, own, one, two, three, box, after, to1, to2, to3, stay, *work):
    del after
    group = lax.axis_index("date")
    unit_looks(epochs, [block.at[0] for block in (own, one, two, three)], box, *work)
    for step, out in ((1, to1), (2, to2), (3, to3), (0, stay)):
        to_owner(work[-1], lax.rem(group + step, 4), out)


def address_kernel(epochs, own, one, two, three, box, early, after, out, token, *work):
    del after
    token[...] = jnp.zeros_like(token)
    y = lax.axis_index("y")
    for turn in (1, 2):
        for item in range(2):
            out[lax.rem(y + turn, 4) * 2 + item] = early[turn - 1, item]
    unit_looks(epochs, [block.at[0] for block in (own, one, two, three)], box, *work)
    to_owners(work[-1], out.at[pl.ds(lax.rem(y + 3, 4) * 2, 2)])


def looks(kernel, epochs, operands, out_shape, out_spec, after=()):
    return pl.pallas_call(
        kernel,
        out_shape=jax.tree.map(
            lambda shape: jax.ShapeDtypeStruct(shape, jnp.float32),
            out_shape,
            is_leaf=lambda shape: isinstance(shape, tuple),
        ),
        grid_spec=pltpu.PrefetchScalarGridSpec(
            num_scalar_prefetch=1,
            grid=(),
            in_specs=[VMEM] * (len(operands) + len(after)),
            out_specs=out_spec,
            scratch_shapes=WORK,
        ),
        cost_estimate=pl.CostEstimate(
            flops=1, bytes_accessed=1, transcendentals=0
        ),
        compiler_params=pltpu.CompilerParams(vmem_limit_bytes=24 << 20),
    )(epochs, *operands, *after)


def place_kernel(positions, usable, other, own, one, two, three, out, rows):
    y, group = lax.axis_index("y"), lax.axis_index("date")

    def put(burst, block):
        position = positions[burst]
        valid = jnp.where(position < usable[0], 1.0, 0.0).astype(jnp.float32)
        rows[pl.ds(pl.multiple_of(position * 16, 16), 16), :] = block * valid

    for turn in (1, 2, 3):
        y_from = lax.rem(y + turn, 4)
        for core in range(2):
            for z in range(4):
                put(z * 8 + y_from * 2 + core, other[y_from * 8 + core * 4 + z])
    for step, block in enumerate((own, one, two, three)):
        for core in range(2):
            put(lax.rem(group + step, 4) * 8 + y * 2 + core, block[core])
    for pair in range(4):
        for part in range(2):
            for eight in range(8):
                out[pair, part, eight * 8 : eight * 8 + 8, :] = rows[
                    pl.ds(eight * 64 + part * 4 + pair, 8, stride=8), :
                ]


def on_device(complex_images, segment_position_map, usable_position_total, interferogram_epochs):
    images = complex_images[:, 0].transpose(0, 1, 3, 2, 4)
    epochs = interferogram_epochs.T
    box = (
        jnp.arange(RG)[:, None] // LOOK_RG == jnp.arange(LCOL)[None, :]
    ).astype(jnp.bfloat16)

    cut_early = cut_date(images, (1, 2))
    cut_late = cut_date(images, (3,), cut_early[4])
    early = meet(*cut_early[:4])
    late = meet(*cut_late[:4])

    crossed = lax.all_to_all(
        cut_tile(images, cut_late[4]), ("z", "core"), split_axis=0, concat_axis=0, tiled=True
    )
    cut_last = cut_crossed(crossed)
    last = meet(*cut_last[:4])

    gamma_early = looks(
        functools.partial(plain_kernel, 2), epochs, (*early, box), (2, 2, 4, 16, LCOL), VMEM
    )
    addressed, computed = looks(
        address_kernel,
        epochs,
        (*late, box, gamma_early),
        [(8, 4, 16, LCOL), TOKEN.shape],
        [VMEM] * 2,
        (cut_last[4],),
    )
    swapped = lax.ppermute(
        addressed.reshape(32, 16, LCOL),
        ("z", "date"),
        [(z * 4 + date, date * 4 + z) for z in range(4) for date in range(4)],
    )
    other = lax.all_to_all(
        swapped, ("y", "core", "date"), split_axis=0, concat_axis=0, tiled=True
    )

    gamma_last = looks(
        last_kernel, epochs, (*last, box), [(2, 16, LCOL)] * 4, [VMEM] * 4, (computed,)
    )
    same = meet(*gamma_last)

    return pl.pallas_call(
        place_kernel,
        out_shape=jax.ShapeDtypeStruct((4, 2, 64, LCOL), jnp.float32),
        grid_spec=pltpu.PrefetchScalarGridSpec(
            num_scalar_prefetch=2,
            grid=(),
            in_specs=[VMEM] * 5,
            out_specs=VMEM,
            scratch_shapes=[pltpu.VMEM((512, LCOL), jnp.float32)],
        ),
        compiler_params=pltpu.CompilerParams(vmem_limit_bytes=4 << 20),
    )(segment_position_map[0], usable_position_total, other, *same)


def solution(mesh):
    fine = Mesh(mesh.devices.reshape(4, 4, 2, 4), ("z", "y", "core", "date"))
    tile = ("z", "y", "core")
    return jax.shard_map(
        on_device,
        mesh=fine,
        in_specs=(P("date", tile, None, None, None, None), P(tile, None), P(tile), P()),
        out_specs=P("date", None, None, tile),
        check_vma=False,
    )
```

```python
import functools

import jax
import jax.numpy as jnp
from jax import lax
from jax.experimental import pallas as pl
from jax.experimental.pallas import tpu as pltpu
from jax.sharding import Mesh, PartitionSpec as P

LOOK_RG = 15
LOOK_AZ = 5
EPS = 1e-05
SCALE = 1.0 / (LOOK_AZ * LOOK_RG)
DATES = 8
PAIRS = 16
ITEMS = 8
RG = 1920
LCOL = 128
ROWS = 320
SPLIT = 8
LINES = 10

VMEM = pl.BlockSpec(memory_space=pltpu.VMEM)
SMEM = pl.BlockSpec(memory_space=pltpu.SMEM)
HBM = pl.BlockSpec(memory_space=pltpu.HBM)
ANYWHERE = pl.BlockSpec(memory_space=pl.ANY)


def cut_kernel(low, high, images, *rest):
    to1, to2, to3, own, sem = rest[-5:]
    group = lax.axis_index("date")
    copies = []
    for step, out in ((1, to1), (3, to3), (2, to2), (0, own)):
        tiles = pl.ds(lax.rem(group + step, 4) * ITEMS, ITEMS)
        for date in range(2):
            copies.append(
                pltpu.make_async_copy(
                    images.at[date, tiles, low:high], out.at[:, date], sem.at[len(copies)]
                )
            )
            copies[-1].start()
    for copy in copies:
        copy.wait()


def cut(images, low, high, after=None):
    block = jax.ShapeDtypeStruct((ITEMS, 2, high - low, 2, RG), jnp.bfloat16)
    operands = (images,) + (() if after is None else (after,))
    return pl.pallas_call(
        functools.partial(cut_kernel, low, high),
        out_shape=[block] * 4,
        in_specs=[HBM, ANYWHERE][: len(operands)],
        out_specs=[VMEM] * 4,
        scratch_shapes=[pltpu.SemaphoreType.DMA((8,))],
        compiler_params=pltpu.CompilerParams(vmem_limit_bytes=8 << 20),
    )(*operands)


def meet(to1, to2, to3, own):
    def ring(step):
        return [(i, (i + step) % 4) for i in range(4)]

    three = lax.ppermute(to1, "date", ring(1))
    one = lax.ppermute(to3, "date", ring(3))
    two = lax.ppermute(to2, "date", ring(2))
    return own, one, two, three


def add_lines(epochs, blocks, low, high, box, img, hi, lo):
    group = lax.axis_index("date")
    lines = high - low
    for step, block in enumerate(blocks):
        base = lax.rem(group + step, 4) * 2
        for date in range(2):
            for line in range(lines):
                pixels = jnp.swapaxes(block[:, date, low + line], 0, 1).reshape(16, RG)
                img[base + date, line] = pixels.astype(jnp.float32)

    def split(values, row):
        upper = values.astype(jnp.bfloat16)
        hi[pl.ds(row, 16), :] = upper
        lo[pl.ds(row, 16), :] = (values - upper.astype(jnp.float32)).astype(jnp.bfloat16)

    def power(half, carry):
        total = []
        for date in range(2):
            acc = jnp.zeros((ITEMS, RG), jnp.float32)
            for line in range(lines):
                re = img[2 * half + date, line, 0:8, :]
                im = img[2 * half + date, line, 8:16, :]
                acc = acc + (re * re + im * im)
            total.append(acc)
        split(jnp.concatenate(total, axis=0), pl.multiple_of(half * 16, 16))
        return carry

    lax.fori_loop(0, DATES // 2, power, 0)

    def cross(k, carry):
        a, b = epochs[0, k], epochs[1, k]
        acc_re = jnp.zeros((ITEMS, RG), jnp.float32)
        acc_im = jnp.zeros((ITEMS, RG), jnp.float32)
        for line in range(lines):
            re_a, im_a = img[a, line, 0:8, :], img[a, line, 8:16, :]
            re_b, im_b = img[b, line, 0:8, :], img[b, line, 8:16, :]
            acc_re = acc_re + (re_a * re_b + im_a * im_b)
            acc_im = acc_im + (im_a * re_b - re_a * im_b)
        split(jnp.concatenate([acc_re, acc_im], axis=0), pl.multiple_of(64 + k * 16, 16))
        return carry

    lax.fori_loop(0, PAIRS, cross, 0)
    return jnp.dot(hi[...], box[...], preferred_element_type=jnp.float32) + jnp.dot(
        lo[...], box[...], preferred_element_type=jnp.float32
    )


def early_kernel(epochs, own, one, two, three, box, sums0, sums1, img, hi, lo):
    blocks = (own, one, two, three)
    sums0[...] = add_lines(epochs, blocks, 0, LOOK_AZ, box, img, hi, lo)
    sums1[...] = add_lines(epochs, blocks, LOOK_AZ, SPLIT, box, img, hi, lo)


def late_kernel(epochs, own, one, two, three, box, early0, early1, table, out, img, hi, lo, sums):
    del table
    sums[0] = early0[...] * SCALE
    total = add_lines(epochs, (own, one, two, three), 0, LINES - SPLIT, box, img, hi, lo)
    sums[1] = (total + early1[...]) * SCALE
    for owner in range(4):
        for look in range(2):
            rows = []
            for kk in range(4):
                k = owner * 4 + kk
                power_a = sums[look, pl.ds(pl.multiple_of(epochs[0, k] * 8, 8), 8), :]
                power_b = sums[look, pl.ds(pl.multiple_of(epochs[1, k] * 8, 8), 8), :]
                weight = 1.0 / jnp.sqrt((power_a + EPS) * (power_b + EPS))
                rows.append(sums[look, 64 + k * 16 : 72 + k * 16, :] * weight)
                rows.append(sums[look, 72 + k * 16 : 80 + k * 16, :] * weight)
            out[:, owner, look * 8 : look * 8 + 8, :] = jnp.swapaxes(
                jnp.stack(rows, axis=0), 0, 1
            )


def looks(kernel, epochs, operands, out_shape, lines, scratch=()):
    work = lines * ITEMS * RG * (PAIRS * 8 + DATES * 4) + 4 * ROWS * RG * LCOL
    return pl.pallas_call(
        kernel,
        out_shape=out_shape,
        grid_spec=pltpu.PrefetchScalarGridSpec(
            num_scalar_prefetch=1,
            grid=(),
            in_specs=[VMEM if x.ndim > 1 else SMEM for x in operands],
            out_specs=jax.tree.map(lambda _: VMEM, out_shape),
            scratch_shapes=[
                pltpu.VMEM((DATES, min(lines, LOOK_AZ), 16, RG), jnp.float32),
                pltpu.VMEM((ROWS, RG), jnp.bfloat16),
                pltpu.VMEM((ROWS, RG), jnp.bfloat16),
                *scratch,
            ],
        ),
        cost_estimate=pl.CostEstimate(
            flops=work, bytes_accessed=DATES * lines * 16 * RG * 2, transcendentals=0
        ),
        compiler_params=pltpu.CompilerParams(vmem_limit_bytes=24 << 20),
    )(epochs, *operands)


def place_kernel(table, got, out, rows):
    for y in range(4):
        for core in range(2):
            for z in range(4):
                position = table[z * 8 + y * 2 + core]
                valid = jnp.where(position < table[32], 1.0, 0.0).astype(jnp.float32)
                rows[pl.ds(pl.multiple_of(position * 16, 16), 16), :] = (
                    got[y * 8 + core * 4 + z] * valid
                )
    for plane in range(8):
        for part in range(8):
            out[plane // 2, plane % 2, part * 8 : part * 8 + 8, :] = rows[
                pl.ds(part * 64 + plane, 8, stride=8), :
            ]


def on_device(complex_images, segment_position_map, usable_position_total, interferogram_epochs):
    images = complex_images[:, 0].transpose(0, 1, 3, 2, 4)
    epochs = interferogram_epochs.T
    table = jnp.concatenate([segment_position_map[0], usable_position_total])
    box = (
        jnp.arange(RG)[:, None] // LOOK_RG == jnp.arange(LCOL)[None, :]
    ).astype(jnp.bfloat16)

    early = meet(*cut(images, 0, SPLIT))
    late = meet(*cut(images, SPLIT, LINES, early[3]))

    partial = jax.ShapeDtypeStruct((ROWS, LCOL), jnp.float32)
    sums0, sums1 = looks(
        early_kernel, epochs, (*early, box), (partial, partial), SPLIT
    )
    gamma = looks(
        late_kernel,
        epochs,
        (*late, box, sums0, sums1, table),
        jax.ShapeDtypeStruct((ITEMS, 4, 16, LCOL), jnp.float32),
        LINES - SPLIT,
        (pltpu.VMEM((2, ROWS, LCOL), jnp.float32),),
    )

    swapped = lax.ppermute(
        gamma.reshape(32, 16, LCOL),
        ("z", "date"),
        [(z * 4 + date, date * 4 + z) for z in range(4) for date in range(4)],
    )
    got = lax.all_to_all(
        swapped, ("y", "core", "date"), split_axis=0, concat_axis=0, tiled=True
    )
    return pl.pallas_call(
        place_kernel,
        out_shape=jax.ShapeDtypeStruct((4, 2, 64, LCOL), jnp.float32),
        grid_spec=pltpu.PrefetchScalarGridSpec(
            num_scalar_prefetch=1,
            grid=(),
            in_specs=[VMEM],
            out_specs=VMEM,
            scratch_shapes=[pltpu.VMEM((512, LCOL), jnp.float32)],
        ),
        compiler_params=pltpu.CompilerParams(vmem_limit_bytes=4 << 20),
    )(table, got)


def solution(mesh):
    fine = Mesh(mesh.devices.reshape(4, 4, 2, 4), ("z", "y", "core", "date"))
    tile = ("z", "y", "core")
    return jax.shard_map(
        on_device,
        mesh=fine,
        in_specs=(P("date", tile, None, None, None, None), P(tile, None), P(tile), P()),
        out_specs=P("date", None, None, tile),
        check_vma=False,
    )
```

```python
import functools

import jax
import jax.numpy as jnp
from jax import lax
from jax.experimental import pallas as pl
from jax.experimental.pallas import tpu as pltpu
from jax.sharding import PartitionSpec as P

LOOK_RG = 15
LOOK_AZ = 5
EPS = 1e-05
SCALE = 1.0 / (LOOK_AZ * LOOK_RG)
DATES = 8
PAIRS = 16
ITEMS = 8
RG = 1920
LCOL = 128
ROWS = 320
SPLIT = 4
HALF = 16

VMEM = pl.BlockSpec(memory_space=pltpu.VMEM)
SMEM = pl.BlockSpec(memory_space=pltpu.SMEM)
HBM = pl.BlockSpec(memory_space=pltpu.HBM)
ANYWHERE = pl.BlockSpec(memory_space=pl.ANY)


def cut_kernel(low, high, images, *rest):
    to1, to2, to3, own, sem = rest[-5:]
    group = lax.axis_index("date")
    copies = []
    for step, out in ((1, to1), (3, to3), (2, to2), (0, own)):
        taker = lax.rem(group + step, 4)
        tiles = pl.ds(lax.rem(taker, 2) * HALF, HALF)
        lines = pl.ds(lax.div(taker, 2) * LOOK_AZ + low, high - low)
        for date in range(2):
            copies.append(
                pltpu.make_async_copy(
                    images.at[date, tiles, lines], out.at[:, date], sem.at[len(copies)]
                )
            )
            copies[-1].start()
    for copy in copies:
        copy.wait()


def cut(images, low, high, after=None):
    block = jax.ShapeDtypeStruct((HALF, 2, high - low, 2, RG), jnp.bfloat16)
    operands = (images,) + (() if after is None else (after,))
    return pl.pallas_call(
        functools.partial(cut_kernel, low, high),
        out_shape=[block] * 4,
        in_specs=[HBM, ANYWHERE][: len(operands)],
        out_specs=[VMEM] * 4,
        scratch_shapes=[pltpu.SemaphoreType.DMA((8,))],
        compiler_params=pltpu.CompilerParams(vmem_limit_bytes=8 << 20),
    )(*operands)


def meet(to1, to2, to3, own):
    def ring(step):
        return [(i, (i + step) % 4) for i in range(4)]

    three = lax.ppermute(to1, "date", ring(1))
    one = lax.ppermute(to3, "date", ring(3))
    two = lax.ppermute(to2, "date", ring(2))
    return own, one, two, three


def add_lines(epochs, blocks, first, lines, box, img, hi, lo):
    group = lax.axis_index("date")
    for step, block in enumerate(blocks):
        base = lax.rem(group + step, 4) * 2
        for date in range(2):
            for line in range(lines):
                pixels = block[first : first + ITEMS, date, line]
                pixels = jnp.swapaxes(pixels, 0, 1).reshape(16, RG)
                img[base + date, line] = pixels.astype(jnp.float32)

    def split(values, row):
        upper = values.astype(jnp.bfloat16)
        hi[pl.ds(row, 16), :] = upper
        lo[pl.ds(row, 16), :] = (values - upper.astype(jnp.float32)).astype(jnp.bfloat16)

    def power(half, carry):
        total = []
        for date in range(2):
            acc = jnp.zeros((ITEMS, RG), jnp.float32)
            for line in range(lines):
                re = img[2 * half + date, line, 0:8, :]
                im = img[2 * half + date, line, 8:16, :]
                acc = acc + (re * re + im * im)
            total.append(acc)
        split(jnp.concatenate(total, axis=0), pl.multiple_of(half * 16, 16))
        return carry

    lax.fori_loop(0, DATES // 2, power, 0)

    def cross(k, carry):
        a, b = epochs[0, k], epochs[1, k]
        acc_re = jnp.zeros((ITEMS, RG), jnp.float32)
        acc_im = jnp.zeros((ITEMS, RG), jnp.float32)
        for line in range(lines):
            re_a, im_a = img[a, line, 0:8, :], img[a, line, 8:16, :]
            re_b, im_b = img[b, line, 0:8, :], img[b, line, 8:16, :]
            acc_re = acc_re + (re_a * re_b + im_a * im_b)
            acc_im = acc_im + (im_a * re_b - re_a * im_b)
        split(jnp.concatenate([acc_re, acc_im], axis=0), pl.multiple_of(64 + k * 16, 16))
        return carry

    lax.fori_loop(0, PAIRS, cross, 0)
    return jnp.dot(hi[...], box[...], preferred_element_type=jnp.float32) + jnp.dot(
        lo[...], box[...], preferred_element_type=jnp.float32
    )


def early_kernel(epochs, own, one, two, three, box, sums, img, hi, lo):
    for part in range(2):
        sums[part] = add_lines(
            epochs, (own, one, two, three), part * ITEMS, SPLIT, box, img, hi, lo
        )


def late_kernel(epochs, own, one, two, three, box, early, table, out, img, hi, lo, sums):
    del table
    start = lax.rem(lax.axis_index("date"), 2) * HALF
    for part in range(2):
        total = add_lines(
            epochs, (own, one, two, three), part * ITEMS, LOOK_AZ - SPLIT, box, img, hi, lo
        )
        sums[...] = (total + early[part]) * SCALE
        for owner in range(4):
            rows = []
            for kk in range(4):
                k = owner * 4 + kk
                power_a = sums[pl.ds(pl.multiple_of(epochs[0, k] * 8, 8), 8), :]
                power_b = sums[pl.ds(pl.multiple_of(epochs[1, k] * 8, 8), 8), :]
                weight = 1.0 / jnp.sqrt((power_a + EPS) * (power_b + EPS))
                rows.append(sums[64 + k * 16 : 72 + k * 16, :] * weight)
                rows.append(sums[72 + k * 16 : 80 + k * 16, :] * weight)
            out[pl.ds(start + part * ITEMS, ITEMS), owner] = jnp.swapaxes(
                jnp.stack(rows, axis=0), 0, 1
            )


def looks(kernel, epochs, operands, out_shape, lines, scratch=()):
    work = lines * HALF * RG * (PAIRS * 8 + DATES * 4) + 4 * ROWS * RG * LCOL
    return pl.pallas_call(
        kernel,
        out_shape=out_shape,
        grid_spec=pltpu.PrefetchScalarGridSpec(
            num_scalar_prefetch=1,
            grid=(),
            in_specs=[VMEM if x.ndim > 1 else SMEM for x in operands],
            out_specs=jax.tree.map(lambda _: VMEM, out_shape),
            scratch_shapes=[
                pltpu.VMEM((DATES, lines, 16, RG), jnp.float32),
                pltpu.VMEM((ROWS, RG), jnp.bfloat16),
                pltpu.VMEM((ROWS, RG), jnp.bfloat16),
                *scratch,
            ],
        ),
        cost_estimate=pl.CostEstimate(
            flops=work, bytes_accessed=DATES * lines * 32 * RG * 2, transcendentals=0
        ),
        compiler_params=pltpu.CompilerParams(vmem_limit_bytes=24 << 20),
    )(epochs, *operands)


def place_kernel(table, got, out, rows):
    half = lax.div(lax.axis_index("tile"), HALF)
    for burst in range(32):
        position = table[burst]
        valid = jnp.where(position < table[32], 1.0, 0.0).astype(jnp.float32)
        base = pl.multiple_of(position * 16, 16)
        rows[pl.ds(base, 8), :] = got[burst, half] * valid
        rows[pl.ds(base + 8, 8), :] = got[burst, 2 + half] * valid
    for plane in range(8):
        for part in range(8):
            out[plane // 2, plane % 2, part * 8 : part * 8 + 8, :] = rows[
                pl.ds(part * 64 + plane, 8, stride=8), :
            ]


def on_device(complex_images, segment_position_map, usable_position_total, interferogram_epochs):
    images = complex_images[:, 0].transpose(0, 1, 3, 2, 4)
    epochs = interferogram_epochs.T
    table = jnp.concatenate([segment_position_map[0], usable_position_total])
    box = (
        jnp.arange(RG)[:, None] // LOOK_RG == jnp.arange(LCOL)[None, :]
    ).astype(jnp.bfloat16)

    early = meet(*cut(images, 0, SPLIT))
    late = meet(*cut(images, SPLIT, LOOK_AZ, early[3]))

    sums = looks(
        early_kernel,
        epochs,
        (*early, box),
        jax.ShapeDtypeStruct((2, ROWS, LCOL), jnp.float32),
        SPLIT,
    )
    gamma = looks(
        late_kernel,
        epochs,
        (*late, box, sums, table),
        jax.ShapeDtypeStruct((32, 4, 8, LCOL), jnp.float32),
        LOOK_AZ - SPLIT,
        (pltpu.VMEM((ROWS, LCOL), jnp.float32),),
    )
    got = lax.all_to_all(
        gamma.reshape(128, 8, LCOL), ("tile", "date"), split_axis=0, concat_axis=0, tiled=True
    ).reshape(32, 4, 8, LCOL)
    return pl.pallas_call(
        place_kernel,
        out_shape=jax.ShapeDtypeStruct((4, 2, 64, LCOL), jnp.float32),
        grid_spec=pltpu.PrefetchScalarGridSpec(
            num_scalar_prefetch=1,
            grid=(),
            in_specs=[VMEM],
            out_specs=VMEM,
            scratch_shapes=[pltpu.VMEM((512, LCOL), jnp.float32)],
        ),
        compiler_params=pltpu.CompilerParams(vmem_limit_bytes=4 << 20),
    )(table, got)


def solution(mesh):
    in_specs = (P("date", "tile", None, None, None, None), P("tile", None), P("tile"), P())
    out_specs = P("date", None, None, "tile")
    return jax.shard_map(
        on_device, mesh=mesh, in_specs=in_specs, out_specs=out_specs, check_vma=False
    )
```

```python
import functools

import jax
import jax.numpy as jnp
from jax import lax
from jax.experimental import pallas as pl
from jax.experimental.pallas import tpu as pltpu
from jax.sharding import PartitionSpec as P

LOOK_RG = 15
LOOK_AZ = 5
EPS = 1e-05
SCALE = 1.0 / (LOOK_AZ * LOOK_RG)
DATES = 8
PAIRS = 16
ITEMS = 8
RG = 1920
LCOL = 128
ROWS = 320
SPLIT = 3
HALF = 16

VMEM = pl.BlockSpec(memory_space=pltpu.VMEM)
SMEM = pl.BlockSpec(memory_space=pltpu.SMEM)
HBM = pl.BlockSpec(memory_space=pltpu.HBM)
ANYWHERE = pl.BlockSpec(memory_space=pl.ANY)


def cut_kernel(parts, images, *rest):
    to1, to2, to3, own, sem = rest[-5:]
    group = lax.axis_index("date")
    copies = []
    for step, out in ((1, to1), (3, to3), (2, to2), (0, own)):
        taker = lax.rem(group + step, 4)
        start, top = lax.rem(taker, 2) * HALF, lax.div(taker, 2) * LOOK_AZ
        filled = 0
        for first, low, high in parts:
            tiles, lines = pl.ds(start + first, ITEMS), pl.ds(top + low, high - low)
            slots = slice(filled, filled + high - low)
            filled += high - low
            for date in range(2):
                copies.append(
                    pltpu.make_async_copy(
                        images.at[date, tiles, lines],
                        out.at[:, date, slots],
                        sem.at[len(copies)],
                    )
                )
                copies[-1].start()
    for copy in copies:
        copy.wait()


def cut(images, parts, after=None):
    slots = sum(high - low for _, low, high in parts)
    block = jax.ShapeDtypeStruct((ITEMS, 2, slots, 2, RG), jnp.bfloat16)
    operands = (images,) + (() if after is None else (after,))
    return pl.pallas_call(
        functools.partial(cut_kernel, parts),
        out_shape=[block] * 4,
        in_specs=[HBM, ANYWHERE][: len(operands)],
        out_specs=[VMEM] * 4,
        scratch_shapes=[pltpu.SemaphoreType.DMA((8 * len(parts),))],
        compiler_params=pltpu.CompilerParams(vmem_limit_bytes=8 << 20),
    )(*operands)


def meet(to1, to2, to3, own):
    def ring(step):
        return [(i, (i + step) % 4) for i in range(4)]

    three = lax.ppermute(to1, "date", ring(1))
    one = lax.ppermute(to3, "date", ring(3))
    two = lax.ppermute(to2, "date", ring(2))
    return own, one, two, three


def add_lines(epochs, blocks, low, high, box, img, hi, lo):
    group = lax.axis_index("date")
    lines = high - low
    for step, block in enumerate(blocks):
        base = lax.rem(group + step, 4) * 2
        for date in range(2):
            for line in range(lines):
                pixels = jnp.swapaxes(block[:, date, low + line], 0, 1).reshape(16, RG)
                img[base + date, line] = pixels.astype(jnp.float32)

    def split(values, row):
        upper = values.astype(jnp.bfloat16)
        hi[pl.ds(row, 16), :] = upper
        lo[pl.ds(row, 16), :] = (values - upper.astype(jnp.float32)).astype(jnp.bfloat16)

    def power(half, carry):
        total = []
        for date in range(2):
            acc = jnp.zeros((ITEMS, RG), jnp.float32)
            for line in range(lines):
                re = img[2 * half + date, line, 0:8, :]
                im = img[2 * half + date, line, 8:16, :]
                acc = acc + (re * re + im * im)
            total.append(acc)
        split(jnp.concatenate(total, axis=0), pl.multiple_of(half * 16, 16))
        return carry

    lax.fori_loop(0, DATES // 2, power, 0)

    def cross(k, carry):
        a, b = epochs[0, k], epochs[1, k]
        acc_re = jnp.zeros((ITEMS, RG), jnp.float32)
        acc_im = jnp.zeros((ITEMS, RG), jnp.float32)
        for line in range(lines):
            re_a, im_a = img[a, line, 0:8, :], img[a, line, 8:16, :]
            re_b, im_b = img[b, line, 0:8, :], img[b, line, 8:16, :]
            acc_re = acc_re + (re_a * re_b + im_a * im_b)
            acc_im = acc_im + (im_a * re_b - re_a * im_b)
        split(jnp.concatenate([acc_re, acc_im], axis=0), pl.multiple_of(64 + k * 16, 16))
        return carry

    lax.fori_loop(0, PAIRS, cross, 0)
    return jnp.dot(hi[...], box[...], preferred_element_type=jnp.float32) + jnp.dot(
        lo[...], box[...], preferred_element_type=jnp.float32
    )


def coherence(epochs, part, sums, out):
    start = lax.rem(lax.axis_index("date"), 2) * HALF + part * ITEMS
    for owner in range(4):
        rows = []
        for kk in range(4):
            k = owner * 4 + kk
            power_a = sums[pl.ds(pl.multiple_of(epochs[0, k] * 8, 8), 8), :]
            power_b = sums[pl.ds(pl.multiple_of(epochs[1, k] * 8, 8), 8), :]
            weight = 1.0 / jnp.sqrt((power_a + EPS) * (power_b + EPS))
            rows.append(sums[64 + k * 16 : 72 + k * 16, :] * weight)
            rows.append(sums[72 + k * 16 : 80 + k * 16, :] * weight)
        out[pl.ds(start, ITEMS), owner] = jnp.swapaxes(jnp.stack(rows, axis=0), 0, 1)


def early_kernel(epochs, own, one, two, three, box, out, later, img, hi, lo, sums):
    blocks = (own, one, two, three)
    sums[...] = add_lines(epochs, blocks, 0, LOOK_AZ, box, img, hi, lo) * SCALE
    coherence(epochs, 0, sums, out)
    later[...] = add_lines(epochs, blocks, LOOK_AZ, LOOK_AZ + SPLIT, box, img, hi, lo)


def late_kernel(epochs, own, one, two, three, box, early, table, given, out, img, hi, lo, sums):
    del table
    del given
    total = add_lines(epochs, (own, one, two, three), 0, LOOK_AZ - SPLIT, box, img, hi, lo)
    sums[...] = (total + early[...]) * SCALE
    coherence(epochs, 1, sums, out)


def looks(kernel, epochs, operands, out_shape, lines, aliases):
    work = lines * ITEMS * RG * (PAIRS * 8 + DATES * 4) + 4 * ROWS * RG * LCOL
    return pl.pallas_call(
        kernel,
        out_shape=out_shape,
        grid_spec=pltpu.PrefetchScalarGridSpec(
            num_scalar_prefetch=1,
            grid=(),
            in_specs=[VMEM if x.ndim > 1 else SMEM for x in operands],
            out_specs=jax.tree.map(lambda _: VMEM, out_shape),
            scratch_shapes=[
                pltpu.VMEM((DATES, min(lines, LOOK_AZ), 16, RG), jnp.float32),
                pltpu.VMEM((ROWS, RG), jnp.bfloat16),
                pltpu.VMEM((ROWS, RG), jnp.bfloat16),
                pltpu.VMEM((ROWS, LCOL), jnp.float32),
            ],
        ),
        input_output_aliases=aliases,
        cost_estimate=pl.CostEstimate(
            flops=work, bytes_accessed=DATES * lines * 16 * RG * 2, transcendentals=0
        ),
        compiler_params=pltpu.CompilerParams(vmem_limit_bytes=24 << 20),
    )(epochs, *operands)


def place_kernel(table, got, out, rows):
    half = lax.div(lax.axis_index("tile"), HALF)
    for burst in range(32):
        position = table[burst]
        valid = jnp.where(position < table[32], 1.0, 0.0).astype(jnp.float32)
        base = pl.multiple_of(position * 16, 16)
        rows[pl.ds(base, 8), :] = got[burst, half] * valid
        rows[pl.ds(base + 8, 8), :] = got[burst, 2 + half] * valid
    for plane in range(8):
        for part in range(8):
            out[plane // 2, plane % 2, part * 8 : part * 8 + 8, :] = rows[
                pl.ds(part * 64 + plane, 8, stride=8), :
            ]


def on_device(complex_images, segment_position_map, usable_position_total, interferogram_epochs):
    images = complex_images[:, 0].transpose(0, 1, 3, 2, 4)
    epochs = interferogram_epochs.T
    table = jnp.concatenate([segment_position_map[0], usable_position_total])
    box = (
        jnp.arange(RG)[:, None] // LOOK_RG == jnp.arange(LCOL)[None, :]
    ).astype(jnp.bfloat16)

    early = meet(*cut(images, ((0, 0, LOOK_AZ), (ITEMS, 0, SPLIT))))
    late = meet(*cut(images, ((ITEMS, SPLIT, LOOK_AZ),), early[3]))

    shape = jax.ShapeDtypeStruct((32, 4, 8, LCOL), jnp.float32)
    partial = jax.ShapeDtypeStruct((ROWS, LCOL), jnp.float32)
    gamma, sums = looks(
        early_kernel, epochs, (*early, box), (shape, partial), LOOK_AZ + SPLIT, {}
    )
    gamma = looks(
        late_kernel, epochs, (*late, box, sums, table, gamma), shape, LOOK_AZ - SPLIT, {8: 0}
    )
    got = lax.all_to_all(
        gamma.reshape(128, 8, LCOL), ("tile", "date"), split_axis=0, concat_axis=0, tiled=True
    ).reshape(32, 4, 8, LCOL)
    return pl.pallas_call(
        place_kernel,
        out_shape=jax.ShapeDtypeStruct((4, 2, 64, LCOL), jnp.float32),
        grid_spec=pltpu.PrefetchScalarGridSpec(
            num_scalar_prefetch=1,
            grid=(),
            in_specs=[VMEM],
            out_specs=VMEM,
            scratch_shapes=[pltpu.VMEM((512, LCOL), jnp.float32)],
        ),
        compiler_params=pltpu.CompilerParams(vmem_limit_bytes=4 << 20),
    )(table, got)


def solution(mesh):
    in_specs = (P("date", "tile", None, None, None, None), P("tile", None), P("tile"), P())
    out_specs = P("date", None, None, "tile")
    return jax.shard_map(
        on_device, mesh=mesh, in_specs=in_specs, out_specs=out_specs, check_vma=False
    )
```

```python
import functools

import jax
import jax.numpy as jnp
from jax import lax
from jax.experimental import pallas as pl
from jax.experimental.pallas import tpu as pltpu
from jax.sharding import PartitionSpec as P

LOOK_RG = 15
LOOK_AZ = 5
EPS = 1e-05
SCALE = 1.0 / (LOOK_AZ * LOOK_RG)
DATES = 8
PAIRS = 16
ITEMS = 8
RG = 1920
LCOL = 128
ROWS = 320
TILES = 32
MAIN = 896
WIDE = 1024
EARLY = ((0, 0, 5), (8, 0, 5), (16, 0, 5), (24, 0, 3))
LATE = ((24, 3, 5),)

VMEM = pl.BlockSpec(memory_space=pltpu.VMEM)
SMEM = pl.BlockSpec(memory_space=pltpu.SMEM)
HBM = pl.BlockSpec(memory_space=pltpu.HBM)
ANYWHERE = pl.BlockSpec(memory_space=pl.ANY)


def cut_kernel(parts, images, *rest):
    to1, to2, to3, own, sem = rest[-5:]
    group = lax.axis_index("date")
    copies = []
    for step, out in ((1, to1), (3, to3), (2, to2), (0, own)):
        taker = lax.rem(group + step, 4)
        top, left = lax.div(taker, 2) * LOOK_AZ, lax.rem(taker, 2) * WIDE
        filled = 0
        for first, low, high in parts:
            lines, slots = pl.ds(top + low, high - low), slice(filled, filled + high - low)
            filled += high - low
            for date in range(2):
                copies.append(
                    pltpu.make_async_copy(
                        images.at[
                            date,
                            first : first + ITEMS,
                            lines,
                            :,
                            pl.ds(pl.multiple_of(left, WIDE), MAIN),
                        ],
                        out.at[:, date, slots],
                        sem.at[len(copies)],
                    )
                )
                copies[-1].start()
    for copy in copies:
        copy.wait()


def cut(images, parts, after=None):
    slots = sum(high - low for _, low, high in parts)
    block = jax.ShapeDtypeStruct((ITEMS, 2, slots, 2, MAIN), jnp.bfloat16)
    operands = (images,) + (() if after is None else (after,))
    return pl.pallas_call(
        functools.partial(cut_kernel, parts),
        out_shape=[block] * 4,
        in_specs=[HBM, ANYWHERE][: len(operands)],
        out_specs=[VMEM] * 4,
        scratch_shapes=[pltpu.SemaphoreType.DMA((8 * len(parts),))],
        compiler_params=pltpu.CompilerParams(vmem_limit_bytes=8 << 20),
    )(*operands)


def cut_middle_kernel(images, to1, to2, to3, own, block, sem):
    copy = pltpu.make_async_copy(images.at[:, :, :, :, MAIN:WIDE], block, sem)
    copy.start()
    copy.wait()
    group = lax.axis_index("date")
    left = lax.broadcasted_iota(jnp.int32, (16, LCOL), 1) < 64
    for step, out in ((1, to1), (3, to3), (2, to2), (0, own)):
        taker = lax.rem(group + step, 4)
        top, half = lax.div(taker, 2) * LOOK_AZ, lax.rem(taker, 2)

        def pack(slot, carry, out=out, top=top, half=half):
            tiles = pl.ds(lax.div(slot, LOOK_AZ) * ITEMS, ITEMS)
            line = top + lax.rem(slot, LOOK_AZ)
            zero = block[0, tiles, line].reshape(16, LCOL).astype(jnp.float32)
            one = block[1, tiles, line].reshape(16, LCOL).astype(jnp.float32)
            first = jnp.where(left, zero, pltpu.roll(one, 64, 1))
            second = jnp.where(left, pltpu.roll(zero, 64, 1), one)
            packed = jnp.where(half == 0, first, second).astype(jnp.bfloat16)
            out[:, slot] = packed.reshape(ITEMS, 2, LCOL)
            return carry

        lax.fori_loop(0, TILES // ITEMS * LOOK_AZ, pack, 0)


def cut_middle(images):
    slots = TILES // ITEMS * LOOK_AZ
    return pl.pallas_call(
        cut_middle_kernel,
        out_shape=[jax.ShapeDtypeStruct((ITEMS, slots, 2, LCOL), jnp.bfloat16)] * 4,
        in_specs=[HBM],
        out_specs=[VMEM] * 4,
        scratch_shapes=[
            pltpu.VMEM((2, TILES, 2 * LOOK_AZ, 2, LCOL), jnp.bfloat16),
            pltpu.SemaphoreType.DMA,
        ],
        compiler_params=pltpu.CompilerParams(vmem_limit_bytes=8 << 20),
    )(images)


def meet(to1, to2, to3, own):
    def ring(step):
        return [(i, (i + step) % 4) for i in range(4)]

    three = lax.ppermute(to1, "date", ring(1))
    one = lax.ppermute(to3, "date", ring(3))
    two = lax.ppermute(to2, "date", ring(2))
    return own, one, two, three


def add_lines(epochs, mains, slot, middles, middle_slot, lines, box, img, hi, lo):
    group = lax.axis_index("date")
    left = lax.broadcasted_iota(jnp.int32, (16, LCOL), 1) < 64
    for step, (main, middle) in enumerate(zip(mains, middles)):
        base = lax.rem(group + step, 4) * 2
        for line in range(lines):
            for date in range(2):
                pixels = jnp.swapaxes(main[:, date, slot + line], 0, 1).reshape(16, MAIN)
                img[base + date, line, :, 0:MAIN] = pixels.astype(jnp.float32)
            packed = jnp.swapaxes(middle[:, middle_slot + line], 0, 1).reshape(16, LCOL)
            packed = packed.astype(jnp.float32)
            img[base, line, :, MAIN:WIDE] = jnp.where(left, packed, 0.0)
            img[base + 1, line, :, MAIN:WIDE] = jnp.where(left, pltpu.roll(packed, 64, 1), 0.0)

    def split(values, row):
        upper = values.astype(jnp.bfloat16)
        hi[pl.ds(row, 16), :] = upper
        lo[pl.ds(row, 16), :] = (values - upper.astype(jnp.float32)).astype(jnp.bfloat16)

    def power(half, carry):
        total = []
        for date in range(2):
            acc = jnp.zeros((ITEMS, WIDE), jnp.float32)
            for line in range(lines):
                re = img[2 * half + date, line, 0:8, :]
                im = img[2 * half + date, line, 8:16, :]
                acc = acc + (re * re + im * im)
            total.append(acc)
        split(jnp.concatenate(total, axis=0), pl.multiple_of(half * 16, 16))
        return carry

    lax.fori_loop(0, DATES // 2, power, 0)

    def cross(k, carry):
        a, b = epochs[0, k], epochs[1, k]
        acc_re = jnp.zeros((ITEMS, WIDE), jnp.float32)
        acc_im = jnp.zeros((ITEMS, WIDE), jnp.float32)
        for line in range(lines):
            re_a, im_a = img[a, line, 0:8, :], img[a, line, 8:16, :]
            re_b, im_b = img[b, line, 0:8, :], img[b, line, 8:16, :]
            acc_re = acc_re + (re_a * re_b + im_a * im_b)
            acc_im = acc_im + (im_a * re_b - re_a * im_b)
        split(jnp.concatenate([acc_re, acc_im], axis=0), pl.multiple_of(64 + k * 16, 16))
        return carry

    lax.fori_loop(0, PAIRS, cross, 0)
    return jnp.dot(hi[...], box[...], preferred_element_type=jnp.float32) + jnp.dot(
        lo[...], box[...], preferred_element_type=jnp.float32
    )


def coherence(epochs, part, sums, out):
    left = lax.broadcasted_iota(jnp.int32, (ITEMS, LCOL), 1) < 64
    for owner in range(4):
        rows = []
        for kk in range(4):
            k = owner * 4 + kk
            power_a = sums[pl.ds(pl.multiple_of(epochs[0, k] * 8, 8), 8), :]
            power_b = sums[pl.ds(pl.multiple_of(epochs[1, k] * 8, 8), 8), :]
            weight = 1.0 / jnp.sqrt((power_a + EPS) * (power_b + EPS))
            cross = jnp.where(
                left, sums[64 + k * 16 : 72 + k * 16, :], sums[72 + k * 16 : 80 + k * 16, :]
            )
            rows.append(cross * weight)
        out[part * ITEMS : (part + 1) * ITEMS, owner] = jnp.swapaxes(
            jnp.stack(rows, axis=0), 0, 1
        )


def early_kernel(epochs, *rest):
    mains, middles, (box, table, out, most, img, hi, lo, sums) = rest[:4], rest[4:8], rest[8:]
    del table
    slot = 0
    for part, (_, low, high) in enumerate(EARLY):
        total = add_lines(
            epochs, mains, slot, middles, part * LOOK_AZ + low, high - low, box, img, hi, lo
        )
        slot += high - low
        if high - low == LOOK_AZ:
            sums[...] = total * SCALE
            coherence(epochs, part, sums, out)
        else:
            most[...] = total


def late_kernel(epochs, *rest):
    mains, middles, (box, most, given, out, img, hi, lo, sums) = rest[:4], rest[4:8], rest[8:]
    del given
    ((_, low, high),) = LATE
    part = len(EARLY) - 1
    total = add_lines(
        epochs, mains, 0, middles, part * LOOK_AZ + low, high - low, box, img, hi, lo
    )
    sums[...] = (total + most[...]) * SCALE
    coherence(epochs, part, sums, out)


def looks(kernel, epochs, operands, out_shape, lines, aliases):
    work = lines * ITEMS * WIDE * (PAIRS * 8 + DATES * 4) + 4 * ROWS * WIDE * LCOL
    return pl.pallas_call(
        kernel,
        out_shape=out_shape,
        grid_spec=pltpu.PrefetchScalarGridSpec(
            num_scalar_prefetch=1,
            grid=(),
            in_specs=[VMEM if x.ndim > 1 else SMEM for x in operands],
            out_specs=jax.tree.map(lambda _: VMEM, out_shape),
            scratch_shapes=[
                pltpu.VMEM((DATES, min(lines, LOOK_AZ), 16, WIDE), jnp.float32),
                pltpu.VMEM((ROWS, WIDE), jnp.bfloat16),
                pltpu.VMEM((ROWS, WIDE), jnp.bfloat16),
                pltpu.VMEM((ROWS, LCOL), jnp.float32),
            ],
        ),
        input_output_aliases=aliases,
        cost_estimate=pl.CostEstimate(
            flops=work, bytes_accessed=DATES * lines * 16 * WIDE * 2, transcendentals=0
        ),
        compiler_params=pltpu.CompilerParams(vmem_limit_bytes=24 << 20),
    )(epochs, *operands)


def place_kernel(table, got, out, rows):
    lane = lax.broadcasted_iota(jnp.int32, (8, LCOL), 1) < 64
    row = lax.broadcasted_iota(jnp.int32, (8, LCOL), 0) < 4
    keep = lane == row
    for burst in range(TILES):
        position = table[burst]
        valid = jnp.where(position < table[TILES], 1.0, 0.0).astype(jnp.float32)
        base = pl.multiple_of(position * 16, 16)
        for look in range(2):
            halves = got[burst * 2 + look]
            crossed = pltpu.roll(pltpu.roll(halves, 64, 1), 4, 0)
            rows[pl.ds(base + look * 8, 8), :] = jnp.where(keep, halves, crossed) * valid
    for pair in range(4):
        for part in range(2):
            for eight in range(8):
                out[pair, part, eight * 8 : eight * 8 + 8, :] = rows[
                    pl.ds(eight * 64 + part * 4 + pair, 8, stride=8), :
                ]


def on_device(complex_images, segment_position_map, usable_position_total, interferogram_epochs):
    images = complex_images[:, 0].transpose(0, 1, 3, 2, 4)
    epochs = interferogram_epochs.T
    table = jnp.concatenate([segment_position_map[0], usable_position_total])

    half = lax.rem(lax.axis_index("date"), 2)
    lane = jnp.arange(WIDE)
    place = jnp.where(lane < MAIN, lane + 64 * half, lane - MAIN * half)
    look = jnp.where(lane < MAIN + 64, place // LOOK_RG, -1)
    box = (look[:, None] == jnp.arange(LCOL)[None, :] % 64).astype(jnp.bfloat16)

    early = meet(*cut(images, EARLY))
    middle = meet(*cut_middle(images))
    late = meet(*cut(images, LATE, early[3]))

    shape = jax.ShapeDtypeStruct((TILES, 4, 4, LCOL), jnp.float32)
    partial = jax.ShapeDtypeStruct((ROWS, LCOL), jnp.float32)
    gamma, most = looks(early_kernel, epochs, (*early, *middle, box, table), (shape, partial), 18, {})
    gamma = looks(late_kernel, epochs, (*late, *middle, box, most, gamma), shape, 2, {11: 0})
    got = lax.all_to_all(
        gamma.reshape(128, 4, LCOL), ("tile", "date"), split_axis=0, concat_axis=0, tiled=True
    ).reshape(64, 8, LCOL)
    return pl.pallas_call(
        place_kernel,
        out_shape=jax.ShapeDtypeStruct((4, 2, 64, LCOL), jnp.float32),
        grid_spec=pltpu.PrefetchScalarGridSpec(
            num_scalar_prefetch=1,
            grid=(),
            in_specs=[VMEM],
            out_specs=VMEM,
            scratch_shapes=[pltpu.VMEM((512, LCOL), jnp.float32)],
        ),
        compiler_params=pltpu.CompilerParams(vmem_limit_bytes=4 << 20),
    )(table, got)


def solution(mesh):
    in_specs = (P("date", "tile", None, None, None, None), P("tile", None), P("tile"), P())
    out_specs = P("date", None, None, "tile")
    return jax.shard_map(
        on_device, mesh=mesh, in_specs=in_specs, out_specs=out_specs, check_vma=False
    )
```

```python
import functools

import jax
import jax.numpy as jnp
from jax import lax
from jax.experimental import pallas as pl
from jax.experimental.pallas import tpu as pltpu
from jax.sharding import PartitionSpec as P

LOOK_RG = 15
LOOK_AZ = 5
EPS = 1e-05
SCALE = 1.0 / (LOOK_AZ * LOOK_RG)
DATES = 8
PAIRS = 16
ITEMS = 8
RG = 1920
LCOL = 128
ROWS = 320
TILES = 32
MAIN = 896
WIDE = 1024
CHUNKS = (((0, 0, 5), (8, 0, 5)), ((16, 0, 5), (24, 0, 3)), ((24, 3, 5),))

VMEM = pl.BlockSpec(memory_space=pltpu.VMEM)
SMEM = pl.BlockSpec(memory_space=pltpu.SMEM)
HBM = pl.BlockSpec(memory_space=pltpu.HBM)
ANYWHERE = pl.BlockSpec(memory_space=pl.ANY)


def cut_kernel(parts, images, *rest):
    to1, to2, to3, own, sem = rest[-5:]
    group = lax.axis_index("date")
    copies = []
    for step, out in ((1, to1), (3, to3), (2, to2), (0, own)):
        taker = lax.rem(group + step, 4)
        top, left = lax.div(taker, 2) * LOOK_AZ, lax.rem(taker, 2) * WIDE
        filled = 0
        for first, low, high in parts:
            lines, slots = pl.ds(top + low, high - low), slice(filled, filled + high - low)
            filled += high - low
            for date in range(2):
                copies.append(
                    pltpu.make_async_copy(
                        images.at[
                            date,
                            first : first + ITEMS,
                            lines,
                            :,
                            pl.ds(pl.multiple_of(left, WIDE), MAIN),
                        ],
                        out.at[:, date, slots],
                        sem.at[len(copies)],
                    )
                )
                copies[-1].start()
    for copy in copies:
        copy.wait()


def cut(images, parts, after=None):
    slots = sum(high - low for _, low, high in parts)
    block = jax.ShapeDtypeStruct((ITEMS, 2, slots, 2, MAIN), jnp.bfloat16)
    operands = (images,) + (() if after is None else (after,))
    return pl.pallas_call(
        functools.partial(cut_kernel, parts),
        out_shape=[block] * 4,
        in_specs=[HBM, ANYWHERE][: len(operands)],
        out_specs=[VMEM] * 4,
        scratch_shapes=[pltpu.SemaphoreType.DMA((8 * len(parts),))],
        compiler_params=pltpu.CompilerParams(vmem_limit_bytes=8 << 20),
    )(*operands)


def cut_middle_kernel(images, *rest):
    to1, to2, to3, own, block, sem = rest[-6:]
    copy = pltpu.make_async_copy(images.at[:, :, :, :, MAIN:WIDE], block, sem)
    copy.start()
    copy.wait()
    group = lax.axis_index("date")
    left = lax.broadcasted_iota(jnp.int32, (16, LCOL), 1) < 64
    for step, out in ((1, to1), (3, to3), (2, to2), (0, own)):
        taker = lax.rem(group + step, 4)
        top, half = lax.div(taker, 2) * LOOK_AZ, lax.rem(taker, 2)

        def pack(slot, carry, out=out, top=top, half=half):
            tiles = pl.ds(lax.div(slot, LOOK_AZ) * ITEMS, ITEMS)
            line = top + lax.rem(slot, LOOK_AZ)
            zero = block[0, tiles, line].reshape(16, LCOL).astype(jnp.float32)
            one = block[1, tiles, line].reshape(16, LCOL).astype(jnp.float32)
            first = jnp.where(left, zero, pltpu.roll(one, 64, 1))
            second = jnp.where(left, pltpu.roll(zero, 64, 1), one)
            packed = jnp.where(half == 0, first, second).astype(jnp.bfloat16)
            out[:, slot] = packed.reshape(ITEMS, 2, LCOL)
            return carry

        lax.fori_loop(0, TILES // ITEMS * LOOK_AZ, pack, 0)


def cut_middle(images, after):
    slots = TILES // ITEMS * LOOK_AZ
    return pl.pallas_call(
        cut_middle_kernel,
        out_shape=[jax.ShapeDtypeStruct((ITEMS, slots, 2, LCOL), jnp.bfloat16)] * 4,
        in_specs=[HBM, ANYWHERE],
        out_specs=[VMEM] * 4,
        scratch_shapes=[
            pltpu.VMEM((2, TILES, 2 * LOOK_AZ, 2, LCOL), jnp.bfloat16),
            pltpu.SemaphoreType.DMA,
        ],
        compiler_params=pltpu.CompilerParams(vmem_limit_bytes=8 << 20),
    )(images, after)


def meet(to1, to2, to3, own):
    def ring(step):
        return [(i, (i + step) % 4) for i in range(4)]

    three = lax.ppermute(to1, "date", ring(1))
    one = lax.ppermute(to3, "date", ring(3))
    two = lax.ppermute(to2, "date", ring(2))
    return own, one, two, three


def add_lines(epochs, mains, slot, middles, middle_slot, lines, box, img, hi, lo):
    group = lax.axis_index("date")
    left = lax.broadcasted_iota(jnp.int32, (16, LCOL), 1) < 64
    for step, (main, middle) in enumerate(zip(mains, middles)):
        base = lax.rem(group + step, 4) * 2
        for line in range(lines):
            for date in range(2):
                pixels = jnp.swapaxes(main[:, date, slot + line], 0, 1).reshape(16, MAIN)
                img[base + date, line, :, 0:MAIN] = pixels.astype(jnp.float32)
            packed = jnp.swapaxes(middle[:, middle_slot + line], 0, 1).reshape(16, LCOL)
            packed = packed.astype(jnp.float32)
            img[base, line, :, MAIN:WIDE] = jnp.where(left, packed, 0.0)
            img[base + 1, line, :, MAIN:WIDE] = jnp.where(left, pltpu.roll(packed, 64, 1), 0.0)

    def split(values, row):
        upper = values.astype(jnp.bfloat16)
        hi[pl.ds(row, 16), :] = upper
        lo[pl.ds(row, 16), :] = (values - upper.astype(jnp.float32)).astype(jnp.bfloat16)

    def power(half, carry):
        total = []
        for date in range(2):
            acc = jnp.zeros((ITEMS, WIDE), jnp.float32)
            for line in range(lines):
                re = img[2 * half + date, line, 0:8, :]
                im = img[2 * half + date, line, 8:16, :]
                acc = acc + (re * re + im * im)
            total.append(acc)
        split(jnp.concatenate(total, axis=0), pl.multiple_of(half * 16, 16))
        return carry

    lax.fori_loop(0, DATES // 2, power, 0)

    def cross(k, carry):
        a, b = epochs[0, k], epochs[1, k]
        acc_re = jnp.zeros((ITEMS, WIDE), jnp.float32)
        acc_im = jnp.zeros((ITEMS, WIDE), jnp.float32)
        for line in range(lines):
            re_a, im_a = img[a, line, 0:8, :], img[a, line, 8:16, :]
            re_b, im_b = img[b, line, 0:8, :], img[b, line, 8:16, :]
            acc_re = acc_re + (re_a * re_b + im_a * im_b)
            acc_im = acc_im + (im_a * re_b - re_a * im_b)
        split(jnp.concatenate([acc_re, acc_im], axis=0), pl.multiple_of(64 + k * 16, 16))
        return carry

    lax.fori_loop(0, PAIRS, cross, 0)
    return jnp.dot(hi[...], box[...], preferred_element_type=jnp.float32) + jnp.dot(
        lo[...], box[...], preferred_element_type=jnp.float32
    )


def coherence(epochs, part, sums, out):
    left = lax.broadcasted_iota(jnp.int32, (ITEMS, LCOL), 1) < 64
    for owner in range(4):
        rows = []
        for kk in range(4):
            k = owner * 4 + kk
            power_a = sums[pl.ds(pl.multiple_of(epochs[0, k] * 8, 8), 8), :]
            power_b = sums[pl.ds(pl.multiple_of(epochs[1, k] * 8, 8), 8), :]
            weight = 1.0 / jnp.sqrt((power_a + EPS) * (power_b + EPS))
            cross = jnp.where(
                left, sums[64 + k * 16 : 72 + k * 16, :], sums[72 + k * 16 : 80 + k * 16, :]
            )
            rows.append(cross * weight)
        out[part * ITEMS : (part + 1) * ITEMS, owner] = jnp.swapaxes(
            jnp.stack(rows, axis=0), 0, 1
        )


def looks_kernel(chunk, epochs, *rest):
    mains, middles, (box, *rest), work = rest[:4], rest[4:8], rest[8:-4], rest[-4:]
    sums = work[-1]
    if chunk == 0:
        table, out = rest
        del table
    elif chunk == 1:
        given, out, most = rest
        del given
    else:
        most, given, out = rest
        del given
    slot = 0
    for first, low, high in CHUNKS[chunk]:
        part = first // ITEMS
        total = add_lines(
            epochs, mains, slot, middles, part * LOOK_AZ + low, high - low, box, *work[:-1]
        )
        slot += high - low
        if low > 0:
            total = total + most[...]
        if high < LOOK_AZ:
            most[...] = total
        else:
            sums[...] = total * SCALE
            coherence(epochs, part, sums, out)


def looks(chunk, epochs, operands, out_shape, aliases):
    lines = sum(high - low for _, low, high in CHUNKS[chunk])
    work = lines * ITEMS * WIDE * (PAIRS * 8 + DATES * 4) + 4 * ROWS * WIDE * LCOL
    return pl.pallas_call(
        functools.partial(looks_kernel, chunk),
        out_shape=out_shape,
        grid_spec=pltpu.PrefetchScalarGridSpec(
            num_scalar_prefetch=1,
            grid=(),
            in_specs=[VMEM if x.ndim > 1 else SMEM for x in operands],
            out_specs=jax.tree.map(lambda _: VMEM, out_shape),
            scratch_shapes=[
                pltpu.VMEM((DATES, min(lines, LOOK_AZ), 16, WIDE), jnp.float32),
                pltpu.VMEM((ROWS, WIDE), jnp.bfloat16),
                pltpu.VMEM((ROWS, WIDE), jnp.bfloat16),
                pltpu.VMEM((ROWS, LCOL), jnp.float32),
            ],
        ),
        input_output_aliases=aliases,
        cost_estimate=pl.CostEstimate(
            flops=work, bytes_accessed=DATES * lines * 16 * WIDE * 2, transcendentals=0
        ),
        compiler_params=pltpu.CompilerParams(vmem_limit_bytes=24 << 20),
    )(epochs, *operands)


def place_kernel(table, got, out, rows):
    lane = lax.broadcasted_iota(jnp.int32, (8, LCOL), 1) < 64
    row = lax.broadcasted_iota(jnp.int32, (8, LCOL), 0) < 4
    keep = lane == row
    for burst in range(TILES):
        position = table[burst]
        valid = jnp.where(position < table[TILES], 1.0, 0.0).astype(jnp.float32)
        base = pl.multiple_of(position * 16, 16)
        for look in range(2):
            halves = got[burst * 2 + look]
            crossed = pltpu.roll(pltpu.roll(halves, 64, 1), 4, 0)
            rows[pl.ds(base + look * 8, 8), :] = jnp.where(keep, halves, crossed) * valid
    for pair in range(4):
        for part in range(2):
            for eight in range(8):
                out[pair, part, eight * 8 : eight * 8 + 8, :] = rows[
                    pl.ds(eight * 64 + part * 4 + pair, 8, stride=8), :
                ]


def on_device(complex_images, segment_position_map, usable_position_total, interferogram_epochs):
    images = complex_images[:, 0].transpose(0, 1, 3, 2, 4)
    epochs = interferogram_epochs.T
    table = jnp.concatenate([segment_position_map[0], usable_position_total])

    half = lax.rem(lax.axis_index("date"), 2)
    lane = jnp.arange(WIDE)
    place = jnp.where(lane < MAIN, lane + 64 * half, lane - MAIN * half)
    look = jnp.where(lane < MAIN + 64, place // LOOK_RG, -1)
    box = (look[:, None] == jnp.arange(LCOL)[None, :] % 64).astype(jnp.bfloat16)

    cut0 = cut(images, CHUNKS[0])
    cut_between = cut_middle(images, cut0[1])
    cut1 = cut(images, CHUNKS[1], cut_between[1])
    chunk0, middle, chunk1 = meet(*cut0), meet(*cut_between), meet(*cut1)
    chunk2 = meet(*cut(images, CHUNKS[2], chunk0[3]))

    shape = jax.ShapeDtypeStruct((TILES, 4, 4, LCOL), jnp.float32)
    partial = jax.ShapeDtypeStruct((ROWS, LCOL), jnp.float32)
    gamma = looks(0, epochs, (*chunk0, *middle, box, table), shape, {})
    gamma, most = looks(1, epochs, (*chunk1, *middle, box, gamma), (shape, partial), {10: 0})
    gamma = looks(2, epochs, (*chunk2, *middle, box, most, gamma), shape, {11: 0})
    got = lax.all_to_all(
        gamma.reshape(128, 4, LCOL), ("tile", "date"), split_axis=0, concat_axis=0, tiled=True
    ).reshape(64, 8, LCOL)
    return pl.pallas_call(
        place_kernel,
        out_shape=jax.ShapeDtypeStruct((4, 2, 64, LCOL), jnp.float32),
        grid_spec=pltpu.PrefetchScalarGridSpec(
            num_scalar_prefetch=1,
            grid=(),
            in_specs=[VMEM],
            out_specs=VMEM,
            scratch_shapes=[pltpu.VMEM((512, LCOL), jnp.float32)],
        ),
        compiler_params=pltpu.CompilerParams(vmem_limit_bytes=4 << 20),
    )(table, got)


def solution(mesh):
    in_specs = (P("date", "tile", None, None, None, None), P("tile", None), P("tile"), P())
    out_specs = P("date", None, None, "tile")
    return jax.shard_map(
        on_device, mesh=mesh, in_specs=in_specs, out_specs=out_specs, check_vma=False
    )
```

```python
import functools

import jax
import jax.numpy as jnp
from jax import lax
from jax.experimental import pallas as pl
from jax.experimental.pallas import tpu as pltpu
from jax.sharding import PartitionSpec as P

LOOK_RG = 15
LOOK_AZ = 5
EPS = 1e-05
SCALE = 1.0 / (LOOK_AZ * LOOK_RG)
DATES = 8
PAIRS = 16
ITEMS = 8
RG = 1920
LCOL = 128
ROWS = 320
CHUNKS = ((0, 0, 5), (8, 0, 4), (8, 4, 5))
HALF = 16

VMEM = pl.BlockSpec(memory_space=pltpu.VMEM)
SMEM = pl.BlockSpec(memory_space=pltpu.SMEM)
HBM = pl.BlockSpec(memory_space=pltpu.HBM)
ANYWHERE = pl.BlockSpec(memory_space=pl.ANY)


def cut_kernel(chunk, images, *rest):
    to1, to2, to3, own, sem = rest[-5:]
    first, low, high = chunk
    group = lax.axis_index("date")
    copies = []
    for step, out in ((1, to1), (3, to3), (2, to2), (0, own)):
        taker = lax.rem(group + step, 4)
        tiles = pl.ds(lax.rem(taker, 2) * HALF + first, ITEMS)
        lines = pl.ds(lax.div(taker, 2) * LOOK_AZ + low, high - low)
        for date in range(2):
            copies.append(
                pltpu.make_async_copy(
                    images.at[date, tiles, lines], out.at[:, date], sem.at[len(copies)]
                )
            )
            copies[-1].start()
    for copy in copies:
        copy.wait()


def cut(images, chunk, after=None):
    _, low, high = chunk
    block = jax.ShapeDtypeStruct((ITEMS, 2, high - low, 2, RG), jnp.bfloat16)
    operands = (images,) + (() if after is None else (after,))
    return pl.pallas_call(
        functools.partial(cut_kernel, chunk),
        out_shape=[block] * 4,
        in_specs=[HBM, ANYWHERE][: len(operands)],
        out_specs=[VMEM] * 4,
        scratch_shapes=[pltpu.SemaphoreType.DMA((8,))],
        compiler_params=pltpu.CompilerParams(vmem_limit_bytes=8 << 20),
    )(*operands)


def meet(to1, to2, to3, own):
    def ring(step):
        return [(i, (i + step) % 4) for i in range(4)]

    three = lax.ppermute(to1, "date", ring(1))
    one = lax.ppermute(to3, "date", ring(3))
    two = lax.ppermute(to2, "date", ring(2))
    return own, one, two, three


def add_lines(epochs, blocks, box, img, hi, lo):
    group = lax.axis_index("date")
    lines = blocks[0].shape[2]
    for step, block in enumerate(blocks):
        base = lax.rem(group + step, 4) * 2
        for date in range(2):
            for line in range(lines):
                pixels = jnp.swapaxes(block[:, date, line], 0, 1).reshape(16, RG)
                img[base + date, line] = pixels.astype(jnp.float32)

    def split(values, row):
        upper = values.astype(jnp.bfloat16)
        hi[pl.ds(row, 16), :] = upper
        lo[pl.ds(row, 16), :] = (values - upper.astype(jnp.float32)).astype(jnp.bfloat16)

    def power(half, carry):
        total = []
        for date in range(2):
            acc = jnp.zeros((ITEMS, RG), jnp.float32)
            for line in range(lines):
                re = img[2 * half + date, line, 0:8, :]
                im = img[2 * half + date, line, 8:16, :]
                acc = acc + (re * re + im * im)
            total.append(acc)
        split(jnp.concatenate(total, axis=0), pl.multiple_of(half * 16, 16))
        return carry

    lax.fori_loop(0, DATES // 2, power, 0)

    def cross(k, carry):
        a, b = epochs[0, k], epochs[1, k]
        acc_re = jnp.zeros((ITEMS, RG), jnp.float32)
        acc_im = jnp.zeros((ITEMS, RG), jnp.float32)
        for line in range(lines):
            re_a, im_a = img[a, line, 0:8, :], img[a, line, 8:16, :]
            re_b, im_b = img[b, line, 0:8, :], img[b, line, 8:16, :]
            acc_re = acc_re + (re_a * re_b + im_a * im_b)
            acc_im = acc_im + (im_a * re_b - re_a * im_b)
        split(jnp.concatenate([acc_re, acc_im], axis=0), pl.multiple_of(64 + k * 16, 16))
        return carry

    lax.fori_loop(0, PAIRS, cross, 0)
    return jnp.dot(hi[...], box[...], preferred_element_type=jnp.float32) + jnp.dot(
        lo[...], box[...], preferred_element_type=jnp.float32
    )


def coherence(epochs, part, sums, out):
    start = lax.rem(lax.axis_index("date"), 2) * HALF + part * ITEMS
    for owner in range(4):
        rows = []
        for kk in range(4):
            k = owner * 4 + kk
            power_a = sums[pl.ds(pl.multiple_of(epochs[0, k] * 8, 8), 8), :]
            power_b = sums[pl.ds(pl.multiple_of(epochs[1, k] * 8, 8), 8), :]
            weight = 1.0 / jnp.sqrt((power_a + EPS) * (power_b + EPS))
            rows.append(sums[64 + k * 16 : 72 + k * 16, :] * weight)
            rows.append(sums[72 + k * 16 : 80 + k * 16, :] * weight)
        out[pl.ds(start, ITEMS), owner] = jnp.swapaxes(jnp.stack(rows, axis=0), 0, 1)


def whole_kernel(epochs, own, one, two, three, box, table, out, img, hi, lo, sums):
    del table
    sums[...] = add_lines(epochs, (own, one, two, three), box, img, hi, lo) * SCALE
    coherence(epochs, 0, sums, out)


def most_kernel(epochs, own, one, two, three, box, after, later, img, hi, lo, sums):
    del after, sums
    later[...] = add_lines(epochs, (own, one, two, three), box, img, hi, lo)


def last_kernel(epochs, own, one, two, three, box, most, given, out, img, hi, lo, sums):
    del given
    total = add_lines(epochs, (own, one, two, three), box, img, hi, lo)
    sums[...] = (total + most[...]) * SCALE
    coherence(epochs, 1, sums, out)


def looks(kernel, epochs, operands, out_shape, lines, aliases={}):
    work = lines * ITEMS * RG * (PAIRS * 8 + DATES * 4) + 4 * ROWS * RG * LCOL
    return pl.pallas_call(
        kernel,
        out_shape=out_shape,
        grid_spec=pltpu.PrefetchScalarGridSpec(
            num_scalar_prefetch=1,
            grid=(),
            in_specs=[VMEM if x.ndim > 1 else SMEM for x in operands],
            out_specs=jax.tree.map(lambda _: VMEM, out_shape),
            scratch_shapes=[
                pltpu.VMEM((DATES, lines, 16, RG), jnp.float32),
                pltpu.VMEM((ROWS, RG), jnp.bfloat16),
                pltpu.VMEM((ROWS, RG), jnp.bfloat16),
                pltpu.VMEM((ROWS, LCOL), jnp.float32),
            ],
        ),
        input_output_aliases=aliases,
        cost_estimate=pl.CostEstimate(
            flops=work, bytes_accessed=DATES * lines * 16 * RG * 2, transcendentals=0
        ),
        compiler_params=pltpu.CompilerParams(vmem_limit_bytes=24 << 20),
    )(epochs, *operands)


def place_kernel(table, got, out, rows):
    half = lax.div(lax.axis_index("tile"), HALF)
    for burst in range(32):
        position = table[burst]
        valid = jnp.where(position < table[32], 1.0, 0.0).astype(jnp.float32)
        base = pl.multiple_of(position * 16, 16)
        rows[pl.ds(base, 8), :] = got[burst, half] * valid
        rows[pl.ds(base + 8, 8), :] = got[burst, 2 + half] * valid
    for plane in range(8):
        for part in range(8):
            out[plane // 2, plane % 2, part * 8 : part * 8 + 8, :] = rows[
                pl.ds(part * 64 + plane, 8, stride=8), :
            ]


def on_device(complex_images, segment_position_map, usable_position_total, interferogram_epochs):
    images = complex_images[:, 0].transpose(0, 1, 3, 2, 4)
    epochs = interferogram_epochs.T
    table = jnp.concatenate([segment_position_map[0], usable_position_total])
    box = (
        jnp.arange(RG)[:, None] // LOOK_RG == jnp.arange(LCOL)[None, :]
    ).astype(jnp.bfloat16)

    first = meet(*cut(images, CHUNKS[0]))
    second = meet(*cut(images, CHUNKS[1], first[3]))
    third = meet(*cut(images, CHUNKS[2], first[2]))

    shape = jax.ShapeDtypeStruct((32, 4, 8, LCOL), jnp.float32)
    partial = jax.ShapeDtypeStruct((ROWS, LCOL), jnp.float32)
    gamma = looks(whole_kernel, epochs, (*first, box, table), shape, 5)
    most = looks(most_kernel, epochs, (*second, box, gamma), partial, 4)
    gamma = looks(last_kernel, epochs, (*third, box, most, gamma), shape, 1, {7: 0})
    got = lax.all_to_all(
        gamma.reshape(128, 8, LCOL), ("tile", "date"), split_axis=0, concat_axis=0, tiled=True
    ).reshape(32, 4, 8, LCOL)
    return pl.pallas_call(
        place_kernel,
        out_shape=jax.ShapeDtypeStruct((4, 2, 64, LCOL), jnp.float32),
        grid_spec=pltpu.PrefetchScalarGridSpec(
            num_scalar_prefetch=1,
            grid=(),
            in_specs=[VMEM],
            out_specs=VMEM,
            scratch_shapes=[pltpu.VMEM((512, LCOL), jnp.float32)],
        ),
        compiler_params=pltpu.CompilerParams(vmem_limit_bytes=4 << 20),
    )(table, got)


def solution(mesh):
    in_specs = (P("date", "tile", None, None, None, None), P("tile", None), P("tile"), P())
    out_specs = P("date", None, None, "tile")
    return jax.shard_map(
        on_device, mesh=mesh, in_specs=in_specs, out_specs=out_specs, check_vma=False
    )
```

```python
import functools

import jax
import jax.numpy as jnp
from jax import lax
from jax.experimental import pallas as pl
from jax.experimental.pallas import tpu as pltpu
from jax.sharding import PartitionSpec as P

LOOK_RG = 15
LOOK_AZ = 5
EPS = 1e-05
SCALE = 1.0 / (LOOK_AZ * LOOK_RG)
DATES = 8
PAIRS = 16
ITEMS = 8
RG = 1920
LCOL = 128
ROWS = 320
CHUNKS = ((0, 0, 5), (8, 0, 4), (8, 4, 5))
HALF = 16

VMEM = pl.BlockSpec(memory_space=pltpu.VMEM)
SMEM = pl.BlockSpec(memory_space=pltpu.SMEM)
HBM = pl.BlockSpec(memory_space=pltpu.HBM)
ANYWHERE = pl.BlockSpec(memory_space=pl.ANY)


def cut_kernel(chunk, images, *rest):
    to1, to2, to3, own, sem = rest[-5:]
    first, low, high = chunk
    group = lax.axis_index("date")
    copies = []
    for step, out in ((1, to1), (3, to3), (2, to2), (0, own)):
        taker = lax.rem(group + step, 4)
        tiles = pl.ds(lax.rem(taker, 2) * HALF + first, ITEMS)
        lines = pl.ds(lax.div(taker, 2) * LOOK_AZ + low, high - low)
        for date in range(2):
            copies.append(
                pltpu.make_async_copy(
                    images.at[date, tiles, lines], out.at[:, date], sem.at[len(copies)]
                )
            )
            copies[-1].start()
    for copy in copies:
        copy.wait()


def cut(images, chunk, after=None):
    _, low, high = chunk
    block = jax.ShapeDtypeStruct((ITEMS, 2, high - low, 2, RG), jnp.bfloat16)
    operands = (images,) + (() if after is None else (after,))
    return pl.pallas_call(
        functools.partial(cut_kernel, chunk),
        out_shape=[block] * 4,
        in_specs=[HBM, ANYWHERE][: len(operands)],
        out_specs=[VMEM] * 4,
        scratch_shapes=[pltpu.SemaphoreType.DMA((8,))],
        compiler_params=pltpu.CompilerParams(vmem_limit_bytes=8 << 20),
    )(*operands)


def meet(to1, to2, to3, own):
    def ring(step):
        return [(i, (i + step) % 4) for i in range(4)]

    three = lax.ppermute(to1, "date", ring(1))
    one = lax.ppermute(to3, "date", ring(3))
    two = lax.ppermute(to2, "date", ring(2))
    return own, one, two, three


def add_lines(epochs, blocks, box, img, hi, lo):
    group = lax.axis_index("date")
    lines = blocks[0].shape[2]
    for step, block in enumerate(blocks):
        base = lax.rem(group + step, 4) * 2
        for date in range(2):
            for line in range(lines):
                pixels = jnp.swapaxes(block[:, date, line], 0, 1).reshape(16, RG)
                img[base + date, line] = pixels.astype(jnp.float32)

    def split(values, row):
        upper = values.astype(jnp.bfloat16)
        hi[pl.ds(row, 16), :] = upper
        lo[pl.ds(row, 16), :] = (values - upper.astype(jnp.float32)).astype(jnp.bfloat16)

    def power(half, carry):
        total = []
        for date in range(2):
            acc = jnp.zeros((ITEMS, RG), jnp.float32)
            for line in range(lines):
                re = img[2 * half + date, line, 0:8, :]
                im = img[2 * half + date, line, 8:16, :]
                acc = acc + (re * re + im * im)
            total.append(acc)
        split(jnp.concatenate(total, axis=0), pl.multiple_of(half * 16, 16))
        return carry

    lax.fori_loop(0, DATES // 2, power, 0)

    def cross(k, carry):
        a, b = epochs[0, k], epochs[1, k]
        acc_re = jnp.zeros((ITEMS, RG), jnp.float32)
        acc_im = jnp.zeros((ITEMS, RG), jnp.float32)
        for line in range(lines):
            re_a, im_a = img[a, line, 0:8, :], img[a, line, 8:16, :]
            re_b, im_b = img[b, line, 0:8, :], img[b, line, 8:16, :]
            acc_re = acc_re + (re_a * re_b + im_a * im_b)
            acc_im = acc_im + (im_a * re_b - re_a * im_b)
        split(jnp.concatenate([acc_re, acc_im], axis=0), pl.multiple_of(64 + k * 16, 16))
        return carry

    lax.fori_loop(0, PAIRS, cross, 0)
    return jnp.dot(hi[...], box[...], preferred_element_type=jnp.float32) + jnp.dot(
        lo[...], box[...], preferred_element_type=jnp.float32
    )


def coherence(epochs, part, sums, out):
    start = lax.rem(lax.axis_index("date"), 2) * HALF + part * ITEMS
    for owner in range(4):
        rows = []
        for kk in range(4):
            k = owner * 4 + kk
            power_a = sums[pl.ds(pl.multiple_of(epochs[0, k] * 8, 8), 8), :]
            power_b = sums[pl.ds(pl.multiple_of(epochs[1, k] * 8, 8), 8), :]
            weight = 1.0 / jnp.sqrt((power_a + EPS) * (power_b + EPS))
            rows.append(sums[64 + k * 16 : 72 + k * 16, :] * weight)
            rows.append(sums[72 + k * 16 : 80 + k * 16, :] * weight)
        out[pl.ds(start, ITEMS), owner] = jnp.swapaxes(jnp.stack(rows, axis=0), 0, 1)


def whole_kernel(epochs, own, one, two, three, box, table, out, img, hi, lo, sums):
    del table
    sums[...] = add_lines(epochs, (own, one, two, three), box, img, hi, lo) * SCALE
    coherence(epochs, 0, sums, out)


def most_kernel(epochs, own, one, two, three, box, after, later, img, hi, lo, sums):
    del after, sums
    later[...] = add_lines(epochs, (own, one, two, three), box, img, hi, lo)


def last_kernel(epochs, own, one, two, three, box, most, given, out, img, hi, lo, sums):
    del given
    total = add_lines(epochs, (own, one, two, three), box, img, hi, lo)
    sums[...] = (total + most[...]) * SCALE
    coherence(epochs, 1, sums, out)


def looks(kernel, epochs, operands, out_shape, lines, aliases={}):
    work = lines * ITEMS * RG * (PAIRS * 8 + DATES * 4) + 4 * ROWS * RG * LCOL
    return pl.pallas_call(
        kernel,
        out_shape=out_shape,
        grid_spec=pltpu.PrefetchScalarGridSpec(
            num_scalar_prefetch=1,
            grid=(),
            in_specs=[VMEM if x.ndim > 1 else SMEM for x in operands],
            out_specs=jax.tree.map(lambda _: VMEM, out_shape),
            scratch_shapes=[
                pltpu.VMEM((DATES, lines, 16, RG), jnp.float32),
                pltpu.VMEM((ROWS, RG), jnp.bfloat16),
                pltpu.VMEM((ROWS, RG), jnp.bfloat16),
                pltpu.VMEM((ROWS, LCOL), jnp.float32),
            ],
        ),
        input_output_aliases=aliases,
        cost_estimate=pl.CostEstimate(
            flops=work, bytes_accessed=DATES * lines * 16 * RG * 2, transcendentals=0
        ),
        compiler_params=pltpu.CompilerParams(vmem_limit_bytes=24 << 20),
    )(epochs, *operands)


def place_kernel(table, got, out, rows):
    half = lax.div(lax.axis_index("tile"), HALF)
    for burst in range(32):
        position = table[burst]
        valid = jnp.where(position < table[32], 1.0, 0.0).astype(jnp.float32)
        base = pl.multiple_of(position * 16, 16)
        rows[pl.ds(base, 8), :] = got[burst, half] * valid
        rows[pl.ds(base + 8, 8), :] = got[burst, 2 + half] * valid
    for plane in range(8):
        for part in range(8):
            out[plane // 2, plane % 2, part * 8 : part * 8 + 8, :] = rows[
                pl.ds(part * 64 + plane, 8, stride=8), :
            ]


def on_device(complex_images, segment_position_map, usable_position_total, interferogram_epochs):
    images = complex_images[:, 0].transpose(0, 1, 3, 2, 4)
    epochs = interferogram_epochs.T
    table = jnp.concatenate([segment_position_map[0], usable_position_total])
    box = (
        jnp.arange(RG)[:, None] // LOOK_RG == jnp.arange(LCOL)[None, :]
    ).astype(jnp.bfloat16)

    first = meet(*cut(images, CHUNKS[0]))
    second = meet(*cut(images, CHUNKS[1], first[3]))

    shape = jax.ShapeDtypeStruct((32, 4, 8, LCOL), jnp.float32)
    partial = jax.ShapeDtypeStruct((ROWS, LCOL), jnp.float32)
    gamma = looks(whole_kernel, epochs, (*first, box, table), shape, 5)
    third = meet(*cut(images, CHUNKS[2], gamma))
    most = looks(most_kernel, epochs, (*second, box, gamma), partial, 4)
    gamma = looks(last_kernel, epochs, (*third, box, most, gamma), shape, 1, {7: 0})
    got = lax.all_to_all(
        gamma.reshape(128, 8, LCOL), ("tile", "date"), split_axis=0, concat_axis=0, tiled=True
    ).reshape(32, 4, 8, LCOL)
    return pl.pallas_call(
        place_kernel,
        out_shape=jax.ShapeDtypeStruct((4, 2, 64, LCOL), jnp.float32),
        grid_spec=pltpu.PrefetchScalarGridSpec(
            num_scalar_prefetch=1,
            grid=(),
            in_specs=[VMEM],
            out_specs=VMEM,
            scratch_shapes=[pltpu.VMEM((512, LCOL), jnp.float32)],
        ),
        compiler_params=pltpu.CompilerParams(vmem_limit_bytes=4 << 20),
    )(table, got)


def solution(mesh):
    in_specs = (P("date", "tile", None, None, None, None), P("tile", None), P("tile"), P())
    out_specs = P("date", None, None, "tile")
    return jax.shard_map(
        on_device, mesh=mesh, in_specs=in_specs, out_specs=out_specs, check_vma=False
    )
```

```python
import functools

import jax
import jax.numpy as jnp
from jax import lax
from jax.experimental import pallas as pl
from jax.experimental.pallas import tpu as pltpu
from jax.sharding import PartitionSpec as P

LOOK_RG = 15
LOOK_AZ = 5
EPS = 1e-05
SCALE = 1.0 / (LOOK_AZ * LOOK_RG)
DATES = 8
PAIRS = 16
ITEMS = 8
RG = 1920
LCOL = 128
ROWS = 320
CHUNKS = ((0, 0, 5), (8, 0, 4), (8, 4, 5))
HALF = 16

VMEM = pl.BlockSpec(memory_space=pltpu.VMEM)
SMEM = pl.BlockSpec(memory_space=pltpu.SMEM)
HBM = pl.BlockSpec(memory_space=pltpu.HBM)
ANYWHERE = pl.BlockSpec(memory_space=pl.ANY)


def cut_kernel(chunk, steps, images, *rest):
    *outs, sem = rest[-1 - len(steps) :]
    first, low, high = chunk
    group = lax.axis_index("date")
    copies = []
    for step, out in zip(steps, outs):
        taker = lax.rem(group + step, 4)
        tiles = pl.ds(lax.rem(taker, 2) * HALF + first, ITEMS)
        lines = pl.ds(lax.div(taker, 2) * LOOK_AZ + low, high - low)
        for date in range(2):
            copies.append(
                pltpu.make_async_copy(
                    images.at[date, tiles, lines], out.at[:, date], sem.at[len(copies)]
                )
            )
            copies[-1].start()
    for copy in copies:
        copy.wait()


def cut(images, chunk, after=None, steps=(1, 2, 3, 0), limit=8):
    _, low, high = chunk
    block = jax.ShapeDtypeStruct((ITEMS, 2, high - low, 2, RG), jnp.bfloat16)
    operands = (images,) + (() if after is None else (after,))
    return pl.pallas_call(
        functools.partial(cut_kernel, chunk, steps),
        out_shape=[block] * len(steps),
        in_specs=[HBM, ANYWHERE][: len(operands)],
        out_specs=[VMEM] * len(steps),
        scratch_shapes=[pltpu.SemaphoreType.DMA((2 * len(steps),))],
        compiler_params=pltpu.CompilerParams(vmem_limit_bytes=limit << 20),
    )(*operands)


def meet(to1, to2, to3, own):
    def ring(step):
        return [(i, (i + step) % 4) for i in range(4)]

    three = lax.ppermute(to1, "date", ring(1))
    one = lax.ppermute(to3, "date", ring(3))
    two = lax.ppermute(to2, "date", ring(2))
    return own, one, two, three


def add_lines(epochs, blocks, box, img, hi, lo):
    group = lax.axis_index("date")
    lines = blocks[0].shape[2]
    for step, block in enumerate(blocks):
        base = lax.rem(group + step, 4) * 2
        for date in range(2):
            for line in range(lines):
                pixels = jnp.swapaxes(block[:, date, line], 0, 1).reshape(16, RG)
                img[base + date, line] = pixels.astype(jnp.float32)

    def split(values, row):
        upper = values.astype(jnp.bfloat16)
        hi[pl.ds(row, 16), :] = upper
        lo[pl.ds(row, 16), :] = (values - upper.astype(jnp.float32)).astype(jnp.bfloat16)

    def power(half, carry):
        total = []
        for date in range(2):
            acc = jnp.zeros((ITEMS, RG), jnp.float32)
            for line in range(lines):
                re = img[2 * half + date, line, 0:8, :]
                im = img[2 * half + date, line, 8:16, :]
                acc = acc + (re * re + im * im)
            total.append(acc)
        split(jnp.concatenate(total, axis=0), pl.multiple_of(half * 16, 16))
        return carry

    lax.fori_loop(0, DATES // 2, power, 0)

    def cross(k, carry):
        a, b = epochs[0, k], epochs[1, k]
        acc_re = jnp.zeros((ITEMS, RG), jnp.float32)
        acc_im = jnp.zeros((ITEMS, RG), jnp.float32)
        for line in range(lines):
            re_a, im_a = img[a, line, 0:8, :], img[a, line, 8:16, :]
            re_b, im_b = img[b, line, 0:8, :], img[b, line, 8:16, :]
            acc_re = acc_re + (re_a * re_b + im_a * im_b)
            acc_im = acc_im + (im_a * re_b - re_a * im_b)
        split(jnp.concatenate([acc_re, acc_im], axis=0), pl.multiple_of(64 + k * 16, 16))
        return carry

    lax.fori_loop(0, PAIRS, cross, 0)
    return jnp.dot(hi[...], box[...], preferred_element_type=jnp.float32) + jnp.dot(
        lo[...], box[...], preferred_element_type=jnp.float32
    )


def coherence(epochs, part, sums, out):
    start = lax.rem(lax.axis_index("date"), 2) * HALF + part * ITEMS
    for owner in range(4):
        rows = []
        for kk in range(4):
            k = owner * 4 + kk
            power_a = sums[pl.ds(pl.multiple_of(epochs[0, k] * 8, 8), 8), :]
            power_b = sums[pl.ds(pl.multiple_of(epochs[1, k] * 8, 8), 8), :]
            weight = 1.0 / jnp.sqrt((power_a + EPS) * (power_b + EPS))
            rows.append(sums[64 + k * 16 : 72 + k * 16, :] * weight)
            rows.append(sums[72 + k * 16 : 80 + k * 16, :] * weight)
        out[pl.ds(start, ITEMS), owner] = jnp.swapaxes(jnp.stack(rows, axis=0), 0, 1)


def whole_kernel(epochs, own, one, two, three, box, table, out, img, hi, lo, sums):
    del table
    sums[...] = add_lines(epochs, (own, one, two, three), box, img, hi, lo) * SCALE
    coherence(epochs, 0, sums, out)


def most_kernel(epochs, own, one, two, three, box, after, later, img, hi, lo, sums):
    del after, sums
    later[...] = add_lines(epochs, (own, one, two, three), box, img, hi, lo)


def last_kernel(epochs, own, one, two, three, box, most, given, out, img, hi, lo, sums):
    del given
    total = add_lines(epochs, (own, one, two, three), box, img, hi, lo)
    sums[...] = (total + most[...]) * SCALE
    coherence(epochs, 1, sums, out)


def looks(kernel, epochs, operands, out_shape, lines, aliases={}):
    work = lines * ITEMS * RG * (PAIRS * 8 + DATES * 4) + 4 * ROWS * RG * LCOL
    return pl.pallas_call(
        kernel,
        out_shape=out_shape,
        grid_spec=pltpu.PrefetchScalarGridSpec(
            num_scalar_prefetch=1,
            grid=(),
            in_specs=[VMEM if x.ndim > 1 else SMEM for x in operands],
            out_specs=jax.tree.map(lambda _: VMEM, out_shape),
            scratch_shapes=[
                pltpu.VMEM((DATES, lines, 16, RG), jnp.float32),
                pltpu.VMEM((ROWS, RG), jnp.bfloat16),
                pltpu.VMEM((ROWS, RG), jnp.bfloat16),
                pltpu.VMEM((ROWS, LCOL), jnp.float32),
            ],
        ),
        input_output_aliases=aliases,
        cost_estimate=pl.CostEstimate(
            flops=work, bytes_accessed=DATES * lines * 16 * RG * 2, transcendentals=0
        ),
        compiler_params=pltpu.CompilerParams(vmem_limit_bytes=24 << 20),
    )(epochs, *operands)


def place_kernel(table, got, out, rows):
    half = lax.div(lax.axis_index("tile"), HALF)
    for burst in range(32):
        position = table[burst]
        valid = jnp.where(position < table[32], 1.0, 0.0).astype(jnp.float32)
        base = pl.multiple_of(position * 16, 16)
        rows[pl.ds(base, 8), :] = got[burst, half] * valid
        rows[pl.ds(base + 8, 8), :] = got[burst, 2 + half] * valid
    for plane in range(8):
        for part in range(8):
            out[plane // 2, plane % 2, part * 8 : part * 8 + 8, :] = rows[
                pl.ds(part * 64 + plane, 8, stride=8), :
            ]


def on_device(complex_images, segment_position_map, usable_position_total, interferogram_epochs):
    images = complex_images[:, 0].transpose(0, 1, 3, 2, 4)
    epochs = interferogram_epochs.T
    table = jnp.concatenate([segment_position_map[0], usable_position_total])
    box = (
        jnp.arange(RG)[:, None] // LOOK_RG == jnp.arange(LCOL)[None, :]
    ).astype(jnp.bfloat16)

    (to1,) = cut(images, CHUNKS[0], None, (1,), 56)
    (to3,) = cut(images, CHUNKS[0], None, (3,), 56)
    (to2,) = cut(images, CHUNKS[0], None, (2,), 56)
    _, one, two, three = meet(to1, to2, to3, to1)
    (own,) = cut(images, CHUNKS[0], three, (0,))
    first = (own, one, two, three)
    second = meet(*cut(images, CHUNKS[1], first[3]))

    shape = jax.ShapeDtypeStruct((32, 4, 8, LCOL), jnp.float32)
    partial = jax.ShapeDtypeStruct((ROWS, LCOL), jnp.float32)
    gamma = looks(whole_kernel, epochs, (*first, box, table), shape, 5)
    third = meet(*cut(images, CHUNKS[2], gamma))
    most = looks(most_kernel, epochs, (*second, box, gamma), partial, 4)
    gamma = looks(last_kernel, epochs, (*third, box, most, gamma), shape, 1, {7: 0})
    got = lax.all_to_all(
        gamma.reshape(128, 8, LCOL), ("tile", "date"), split_axis=0, concat_axis=0, tiled=True
    ).reshape(32, 4, 8, LCOL)
    return pl.pallas_call(
        place_kernel,
        out_shape=jax.ShapeDtypeStruct((4, 2, 64, LCOL), jnp.float32),
        grid_spec=pltpu.PrefetchScalarGridSpec(
            num_scalar_prefetch=1,
            grid=(),
            in_specs=[VMEM],
            out_specs=VMEM,
            scratch_shapes=[pltpu.VMEM((512, LCOL), jnp.float32)],
        ),
        compiler_params=pltpu.CompilerParams(vmem_limit_bytes=4 << 20),
    )(table, got)


def solution(mesh):
    in_specs = (P("date", "tile", None, None, None, None), P("tile", None), P("tile"), P())
    out_specs = P("date", None, None, "tile")
    return jax.shard_map(
        on_device, mesh=mesh, in_specs=in_specs, out_specs=out_specs, check_vma=False
    )
```

```python
import functools

import jax
import jax.numpy as jnp
from jax import lax
from jax.experimental import pallas as pl
from jax.experimental.pallas import tpu as pltpu
from jax.sharding import PartitionSpec as P

LOOK_RG = 15
LOOK_AZ = 5
EPS = 1e-05
SCALE = 1.0 / (LOOK_AZ * LOOK_RG)
DATES = 8
PAIRS = 16
ITEMS = 8
RG = 1920
LCOL = 128
ROWS = 320
CHUNKS = ((0, 0, 5), (8, 0, 4), (8, 4, 5))
HALF = 16

VMEM = pl.BlockSpec(memory_space=pltpu.VMEM)
SMEM = pl.BlockSpec(memory_space=pltpu.SMEM)
HBM = pl.BlockSpec(memory_space=pltpu.HBM)
ANYWHERE = pl.BlockSpec(memory_space=pl.ANY)


def cut_kernel(chunk, steps, images, *rest):
    *outs, sem = rest[-1 - len(steps) :]
    first, low, high = chunk
    group = lax.axis_index("date")
    copies = []
    for step, out in zip(steps, outs):
        taker = lax.rem(group + step, 4)
        start = lax.rem(taker, 2) * HALF + first
        lines = pl.ds(lax.div(taker, 2) * LOOK_AZ + low, high - low)
        for tile in range(ITEMS):
            for date in range(2):
                copies.append(
                    pltpu.make_async_copy(
                        images.at[date, start + tile, lines],
                        out.at[tile, date],
                        sem.at[len(copies)],
                    )
                )
                copies[-1].start()
    for copy in copies:
        copy.wait()


def cut(images, chunk, after=None, steps=(1, 2, 3, 0), limit=8):
    _, low, high = chunk
    block = jax.ShapeDtypeStruct((ITEMS, 2, high - low, 2, RG), jnp.bfloat16)
    operands = (images,) + (() if after is None else (after,))
    return pl.pallas_call(
        functools.partial(cut_kernel, chunk, steps),
        out_shape=[block] * len(steps),
        in_specs=[HBM, ANYWHERE][: len(operands)],
        out_specs=[VMEM] * len(steps),
        scratch_shapes=[pltpu.SemaphoreType.DMA((2 * ITEMS * len(steps),))],
        compiler_params=pltpu.CompilerParams(vmem_limit_bytes=limit << 20),
    )(*operands)


def meet(to1, to2, to3, own):
    def ring(step):
        return [(i, (i + step) % 4) for i in range(4)]

    three = lax.ppermute(to1, "date", ring(1))
    one = lax.ppermute(to3, "date", ring(3))
    two = lax.ppermute(to2, "date", ring(2))
    return own, one, two, three


def add_lines(epochs, blocks, box, img, hi, lo):
    group = lax.axis_index("date")
    lines = blocks[0].shape[2]
    for step, block in enumerate(blocks):
        base = lax.rem(group + step, 4) * 2
        for date in range(2):
            for line in range(lines):
                pixels = jnp.swapaxes(block[:, date, line], 0, 1).reshape(16, RG)
                img[base + date, line] = pixels.astype(jnp.float32)

    def split(values, row):
        upper = values.astype(jnp.bfloat16)
        hi[pl.ds(row, 16), :] = upper
        lo[pl.ds(row, 16), :] = (values - upper.astype(jnp.float32)).astype(jnp.bfloat16)

    def power(half, carry):
        total = []
        for date in range(2):
            acc = jnp.zeros((ITEMS, RG), jnp.float32)
            for line in range(lines):
                re = img[2 * half + date, line, 0:8, :]
                im = img[2 * half + date, line, 8:16, :]
                acc = acc + (re * re + im * im)
            total.append(acc)
        split(jnp.concatenate(total, axis=0), pl.multiple_of(half * 16, 16))
        return carry

    lax.fori_loop(0, DATES // 2, power, 0)

    def cross(k, carry):
        a, b = epochs[0, k], epochs[1, k]
        acc_re = jnp.zeros((ITEMS, RG), jnp.float32)
        acc_im = jnp.zeros((ITEMS, RG), jnp.float32)
        for line in range(lines):
            re_a, im_a = img[a, line, 0:8, :], img[a, line, 8:16, :]
            re_b, im_b = img[b, line, 0:8, :], img[b, line, 8:16, :]
            acc_re = acc_re + (re_a * re_b + im_a * im_b)
            acc_im = acc_im + (im_a * re_b - re_a * im_b)
        split(jnp.concatenate([acc_re, acc_im], axis=0), pl.multiple_of(64 + k * 16, 16))
        return carry

    lax.fori_loop(0, PAIRS, cross, 0)
    return jnp.dot(hi[...], box[...], preferred_element_type=jnp.float32) + jnp.dot(
        lo[...], box[...], preferred_element_type=jnp.float32
    )


def coherence(epochs, part, sums, out):
    start = lax.rem(lax.axis_index("date"), 2) * HALF + part * ITEMS
    for owner in range(4):
        rows = []
        for kk in range(4):
            k = owner * 4 + kk
            power_a = sums[pl.ds(pl.multiple_of(epochs[0, k] * 8, 8), 8), :]
            power_b = sums[pl.ds(pl.multiple_of(epochs[1, k] * 8, 8), 8), :]
            weight = 1.0 / jnp.sqrt((power_a + EPS) * (power_b + EPS))
            rows.append(sums[64 + k * 16 : 72 + k * 16, :] * weight)
            rows.append(sums[72 + k * 16 : 80 + k * 16, :] * weight)
        out[pl.ds(start, ITEMS), owner] = jnp.swapaxes(jnp.stack(rows, axis=0), 0, 1)


def whole_kernel(epochs, own, one, two, three, box, table, out, img, hi, lo, sums):
    del table
    sums[...] = add_lines(epochs, (own, one, two, three), box, img, hi, lo) * SCALE
    coherence(epochs, 0, sums, out)


def most_kernel(epochs, own, one, two, three, box, after, later, img, hi, lo, sums):
    del after, sums
    later[...] = add_lines(epochs, (own, one, two, three), box, img, hi, lo)


def last_kernel(epochs, own, one, two, three, box, most, given, out, img, hi, lo, sums):
    del given
    total = add_lines(epochs, (own, one, two, three), box, img, hi, lo)
    sums[...] = (total + most[...]) * SCALE
    coherence(epochs, 1, sums, out)


def looks(kernel, epochs, operands, out_shape, lines, aliases={}):
    work = lines * ITEMS * RG * (PAIRS * 8 + DATES * 4) + 4 * ROWS * RG * LCOL
    return pl.pallas_call(
        kernel,
        out_shape=out_shape,
        grid_spec=pltpu.PrefetchScalarGridSpec(
            num_scalar_prefetch=1,
            grid=(),
            in_specs=[VMEM if x.ndim > 1 else SMEM for x in operands],
            out_specs=jax.tree.map(lambda _: VMEM, out_shape),
            scratch_shapes=[
                pltpu.VMEM((DATES, lines, 16, RG), jnp.float32),
                pltpu.VMEM((ROWS, RG), jnp.bfloat16),
                pltpu.VMEM((ROWS, RG), jnp.bfloat16),
                pltpu.VMEM((ROWS, LCOL), jnp.float32),
            ],
        ),
        input_output_aliases=aliases,
        cost_estimate=pl.CostEstimate(
            flops=work, bytes_accessed=DATES * lines * 16 * RG * 2, transcendentals=0
        ),
        compiler_params=pltpu.CompilerParams(vmem_limit_bytes=24 << 20),
    )(epochs, *operands)


def place_kernel(table, got, out, rows):
    half = lax.div(lax.axis_index("tile"), HALF)
    for burst in range(32):
        position = table[burst]
        valid = jnp.where(position < table[32], 1.0, 0.0).astype(jnp.float32)
        base = pl.multiple_of(position * 16, 16)
        rows[pl.ds(base, 8), :] = got[burst, half] * valid
        rows[pl.ds(base + 8, 8), :] = got[burst, 2 + half] * valid
    for plane in range(8):
        for part in range(8):
            out[plane // 2, plane % 2, part * 8 : part * 8 + 8, :] = rows[
                pl.ds(part * 64 + plane, 8, stride=8), :
            ]


def on_device(complex_images, segment_position_map, usable_position_total, interferogram_epochs):
    images = complex_images[:, 0].transpose(0, 1, 3, 2, 4)
    epochs = interferogram_epochs.T
    table = jnp.concatenate([segment_position_map[0], usable_position_total])
    box = (
        jnp.arange(RG)[:, None] // LOOK_RG == jnp.arange(LCOL)[None, :]
    ).astype(jnp.bfloat16)

    (to1,) = cut(images, CHUNKS[0], None, (1,), 56)
    (to3,) = cut(images, CHUNKS[0], None, (3,), 56)
    (to2,) = cut(images, CHUNKS[0], None, (2,), 56)
    _, one, two, three = meet(to1, to2, to3, to1)
    (own,) = cut(images, CHUNKS[0], three, (0,))
    first = (own, one, two, three)
    second = meet(*cut(images, CHUNKS[1], first[3]))

    shape = jax.ShapeDtypeStruct((32, 4, 8, LCOL), jnp.float32)
    partial = jax.ShapeDtypeStruct((ROWS, LCOL), jnp.float32)
    gamma = looks(whole_kernel, epochs, (*first, box, table), shape, 5)
    third = meet(*cut(images, CHUNKS[2], gamma))
    most = looks(most_kernel, epochs, (*second, box, gamma), partial, 4)
    gamma = looks(last_kernel, epochs, (*third, box, most, gamma), shape, 1, {7: 0})
    got = lax.all_to_all(
        gamma.reshape(128, 8, LCOL), ("tile", "date"), split_axis=0, concat_axis=0, tiled=True
    ).reshape(32, 4, 8, LCOL)
    return pl.pallas_call(
        place_kernel,
        out_shape=jax.ShapeDtypeStruct((4, 2, 64, LCOL), jnp.float32),
        grid_spec=pltpu.PrefetchScalarGridSpec(
            num_scalar_prefetch=1,
            grid=(),
            in_specs=[VMEM],
            out_specs=VMEM,
            scratch_shapes=[pltpu.VMEM((512, LCOL), jnp.float32)],
        ),
        compiler_params=pltpu.CompilerParams(vmem_limit_bytes=4 << 20),
    )(table, got)


def solution(mesh):
    in_specs = (P("date", "tile", None, None, None, None), P("tile", None), P("tile"), P())
    out_specs = P("date", None, None, "tile")
    return jax.shard_map(
        on_device, mesh=mesh, in_specs=in_specs, out_specs=out_specs, check_vma=False
    )
```

```python
import functools

import jax
import jax.numpy as jnp
from jax import lax
from jax.experimental import pallas as pl
from jax.experimental.pallas import tpu as pltpu
from jax.sharding import PartitionSpec as P

LOOK_RG = 15
LOOK_AZ = 5
EPS = 1e-05
SCALE = 1.0 / (LOOK_AZ * LOOK_RG)
DATES = 8
PAIRS = 16
ITEMS = 8
RG = 1920
LCOL = 128
ROWS = 320
CHUNKS = ((0, 0, 5), (8, 0, 4), (8, 4, 5))
HALF = 16

VMEM = pl.BlockSpec(memory_space=pltpu.VMEM)
SMEM = pl.BlockSpec(memory_space=pltpu.SMEM)
HBM = pl.BlockSpec(memory_space=pltpu.HBM)
ANYWHERE = pl.BlockSpec(memory_space=pl.ANY)


def cut_kernel(chunk, images, *rest):
    to1, to2, to3, own, sem = rest[-5:]
    first, low, high = chunk
    group = lax.axis_index("date")
    copies = []
    for step, out in ((1, to1), (3, to3), (2, to2), (0, own)):
        taker = lax.rem(group + step, 4)
        tiles = pl.ds(lax.rem(taker, 2) * HALF + first, ITEMS)
        lines = pl.ds(lax.div(taker, 2) * LOOK_AZ + low, high - low)
        for date in range(2):
            copies.append(
                pltpu.make_async_copy(
                    images.at[date, tiles, lines], out.at[:, date], sem.at[len(copies)]
                )
            )
            copies[-1].start()
    for copy in copies:
        copy.wait()


def cut(images, chunk, after=None):
    _, low, high = chunk
    block = jax.ShapeDtypeStruct((ITEMS, 2, high - low, 2, RG), jnp.bfloat16)
    operands = (images,) + (() if after is None else (after,))
    return pl.pallas_call(
        functools.partial(cut_kernel, chunk),
        out_shape=[block] * 4,
        in_specs=[HBM, ANYWHERE][: len(operands)],
        out_specs=[VMEM] * 4,
        scratch_shapes=[pltpu.SemaphoreType.DMA((8,))],
        compiler_params=pltpu.CompilerParams(vmem_limit_bytes=8 << 20),
    )(*operands)


def meet(to1, to2, to3, own):
    def ring(step):
        return [(i, (i + step) % 4) for i in range(4)]

    three = lax.ppermute(to1, "date", ring(1))
    one = lax.ppermute(to3, "date", ring(3))
    two = lax.ppermute(to2, "date", ring(2))
    return own, one, two, three


def add_lines(epochs, blocks, box, img, terms):
    group = lax.axis_index("date")
    lines = blocks[0].shape[2]
    for step, block in enumerate(blocks):
        base = lax.rem(group + step, 4) * 2
        for date in range(2):
            for line in range(lines):
                pixels = jnp.swapaxes(block[:, date, line], 0, 1).reshape(16, RG)
                img[base + date, line] = pixels.astype(jnp.float32)

    def split(values, row):
        upper = values.astype(jnp.bfloat16)
        terms[pl.ds(row, 16), :] = upper
        terms[pl.ds(ROWS + row, 16), :] = (values - upper.astype(jnp.float32)).astype(
            jnp.bfloat16
        )

    def power(half, carry):
        total = []
        for date in range(2):
            acc = jnp.zeros((ITEMS, RG), jnp.float32)
            for line in range(lines):
                re = img[2 * half + date, line, 0:8, :]
                im = img[2 * half + date, line, 8:16, :]
                acc = acc + (re * re + im * im)
            total.append(acc)
        split(jnp.concatenate(total, axis=0), pl.multiple_of(half * 16, 16))
        return carry

    lax.fori_loop(0, DATES // 2, power, 0)

    def cross(k, carry):
        a, b = epochs[0, k], epochs[1, k]
        acc_re = jnp.zeros((ITEMS, RG), jnp.float32)
        acc_im = jnp.zeros((ITEMS, RG), jnp.float32)
        for line in range(lines):
            re_a, im_a = img[a, line, 0:8, :], img[a, line, 8:16, :]
            re_b, im_b = img[b, line, 0:8, :], img[b, line, 8:16, :]
            acc_re = acc_re + (re_a * re_b + im_a * im_b)
            acc_im = acc_im + (im_a * re_b - re_a * im_b)
        split(jnp.concatenate([acc_re, acc_im], axis=0), pl.multiple_of(64 + k * 16, 16))
        return carry

    lax.fori_loop(0, PAIRS, cross, 0)
    both = jnp.dot(terms[...], box[...], preferred_element_type=jnp.float32)
    return both[:ROWS] + both[ROWS:]


def coherence(epochs, part, sums, out):
    start = lax.rem(lax.axis_index("date"), 2) * HALF + part * ITEMS
    for owner in range(4):
        rows = []
        for kk in range(4):
            k = owner * 4 + kk
            power_a = sums[pl.ds(pl.multiple_of(epochs[0, k] * 8, 8), 8), :]
            power_b = sums[pl.ds(pl.multiple_of(epochs[1, k] * 8, 8), 8), :]
            weight = 1.0 / jnp.sqrt((power_a + EPS) * (power_b + EPS))
            rows.append(sums[64 + k * 16 : 72 + k * 16, :] * weight)
            rows.append(sums[72 + k * 16 : 80 + k * 16, :] * weight)
        out[pl.ds(start, ITEMS), owner] = jnp.swapaxes(jnp.stack(rows, axis=0), 0, 1)


def whole_kernel(epochs, own, one, two, three, box, table, out, img, terms, sums):
    del table
    sums[...] = add_lines(epochs, (own, one, two, three), box, img, terms) * SCALE
    coherence(epochs, 0, sums, out)


def most_kernel(epochs, own, one, two, three, box, after, later, img, terms, sums):
    del after, sums
    later[...] = add_lines(epochs, (own, one, two, three), box, img, terms)


def last_kernel(epochs, own, one, two, three, box, most, given, out, img, terms, sums):
    del given
    total = add_lines(epochs, (own, one, two, three), box, img, terms)
    sums[...] = (total + most[...]) * SCALE
    coherence(epochs, 1, sums, out)


def looks(kernel, epochs, operands, out_shape, lines, aliases={}):
    work = lines * ITEMS * RG * (PAIRS * 8 + DATES * 4) + 4 * ROWS * RG * LCOL
    return pl.pallas_call(
        kernel,
        out_shape=out_shape,
        grid_spec=pltpu.PrefetchScalarGridSpec(
            num_scalar_prefetch=1,
            grid=(),
            in_specs=[VMEM if x.ndim > 1 else SMEM for x in operands],
            out_specs=jax.tree.map(lambda _: VMEM, out_shape),
            scratch_shapes=[
                pltpu.VMEM((DATES, lines, 16, RG), jnp.float32),
                pltpu.VMEM((2 * ROWS, RG), jnp.bfloat16),
                pltpu.VMEM((ROWS, LCOL), jnp.float32),
            ],
        ),
        input_output_aliases=aliases,
        cost_estimate=pl.CostEstimate(
            flops=work, bytes_accessed=DATES * lines * 16 * RG * 2, transcendentals=0
        ),
        compiler_params=pltpu.CompilerParams(vmem_limit_bytes=24 << 20),
    )(epochs, *operands)


def place_kernel(table, got, out, rows):
    half = lax.div(lax.axis_index("tile"), HALF)
    for burst in range(32):
        position = table[burst]
        valid = jnp.where(position < table[32], 1.0, 0.0).astype(jnp.float32)
        base = pl.multiple_of(position * 16, 16)
        rows[pl.ds(base, 8), :] = got[burst, half] * valid
        rows[pl.ds(base + 8, 8), :] = got[burst, 2 + half] * valid
    for plane in range(8):
        for part in range(8):
            out[plane // 2, plane % 2, part * 8 : part * 8 + 8, :] = rows[
                pl.ds(part * 64 + plane, 8, stride=8), :
            ]


def on_device(complex_images, segment_position_map, usable_position_total, interferogram_epochs):
    images = complex_images[:, 0].transpose(0, 1, 3, 2, 4)
    epochs = interferogram_epochs.T
    table = jnp.concatenate([segment_position_map[0], usable_position_total])
    box = (
        jnp.arange(RG)[:, None] // LOOK_RG == jnp.arange(LCOL)[None, :]
    ).astype(jnp.bfloat16)

    first = meet(*cut(images, CHUNKS[0]))
    second = meet(*cut(images, CHUNKS[1], first[3]))

    shape = jax.ShapeDtypeStruct((32, 4, 8, LCOL), jnp.float32)
    partial = jax.ShapeDtypeStruct((ROWS, LCOL), jnp.float32)
    gamma = looks(whole_kernel, epochs, (*first, box, table), shape, 5)
    third = meet(*cut(images, CHUNKS[2], gamma))
    most = looks(most_kernel, epochs, (*second, box, gamma), partial, 4)
    gamma = looks(last_kernel, epochs, (*third, box, most, gamma), shape, 1, {7: 0})
    got = lax.all_to_all(
        gamma.reshape(128, 8, LCOL), ("tile", "date"), split_axis=0, concat_axis=0, tiled=True
    ).reshape(32, 4, 8, LCOL)
    return pl.pallas_call(
        place_kernel,
        out_shape=jax.ShapeDtypeStruct((4, 2, 64, LCOL), jnp.float32),
        grid_spec=pltpu.PrefetchScalarGridSpec(
            num_scalar_prefetch=1,
            grid=(),
            in_specs=[VMEM],
            out_specs=VMEM,
            scratch_shapes=[pltpu.VMEM((512, LCOL), jnp.float32)],
        ),
        compiler_params=pltpu.CompilerParams(vmem_limit_bytes=4 << 20),
    )(table, got)


def solution(mesh):
    in_specs = (P("date", "tile", None, None, None, None), P("tile", None), P("tile"), P())
    out_specs = P("date", None, None, "tile")
    return jax.shard_map(
        on_device, mesh=mesh, in_specs=in_specs, out_specs=out_specs, check_vma=False
    )
```

```python
import functools

import jax
import jax.numpy as jnp
from jax import lax
from jax.experimental import pallas as pl
from jax.experimental.pallas import tpu as pltpu
from jax.sharding import PartitionSpec as P

LOOK_RG = 15
LOOK_AZ = 5
EPS = 1e-05
SCALE = 1.0 / (LOOK_AZ * LOOK_RG)
DATES = 8
PAIRS = 16
ITEMS = 8
RG = 1920
LCOL = 128
ROWS = 320
TILES = 32
MAIN = 896
WIDE = 1024
CHUNKS = (((0, 0, 5), (8, 0, 5)), ((16, 0, 5), (24, 0, 4)), ((24, 4, 5),))

VMEM = pl.BlockSpec(memory_space=pltpu.VMEM)
SMEM = pl.BlockSpec(memory_space=pltpu.SMEM)
HBM = pl.BlockSpec(memory_space=pltpu.HBM)
ANYWHERE = pl.BlockSpec(memory_space=pl.ANY)


def slots_of(parts):
    return sum(high - low for _, low, high in parts)


def cut_kernel(parts, middle, images, *rest):
    to1, to2, to3, own, block, middle_sem, sem = rest[-7:]
    if middle:
        first = parts[0][0]
        fetch = pltpu.make_async_copy(
            images.at[:, first : first + 2 * ITEMS, :, :, MAIN:WIDE], block, middle_sem
        )
        fetch.start()
    group = lax.axis_index("date")
    takers = [
        (lax.rem(group + step, 4), out)
        for step, out in ((1, to1), (3, to3), (2, to2), (0, own))
    ]
    copies = []
    for taker, out in takers:
        top, left = lax.div(taker, 2) * LOOK_AZ, lax.rem(taker, 2) * WIDE
        filled = 0
        for first, low, high in parts:
            lines, slots = pl.ds(top + low, high - low), slice(filled, filled + high - low)
            filled += high - low
            for date in range(2):
                copies.append(
                    pltpu.make_async_copy(
                        images.at[
                            date,
                            first : first + ITEMS,
                            lines,
                            :,
                            pl.ds(pl.multiple_of(left, WIDE), MAIN),
                        ],
                        out.at[:, date, slots],
                        sem.at[len(copies)],
                    )
                )
                copies[-1].start()
    if middle:
        fetch.wait()
    for copy in copies:
        copy.wait()
    if middle:
        source = lax.broadcasted_iota(jnp.int32, (LCOL, LCOL), 0)
        lane = lax.broadcasted_iota(jnp.int32, (LCOL, LCOL), 1)
        rows = 2 * ITEMS * LOOK_AZ * 2
        for taker, out in takers:
            top, half = lax.div(taker, 2) * LOOK_AZ, lax.rem(taker, 2)
            packed = jnp.zeros((rows, LCOL), jnp.float32)
            for date in range(2):
                moved = lane + 64 * half - 64 * date
                pick = jnp.where((source == moved) & ((lane < 64) == (date == 0)), 1.0, 0.0)
                samples = block[date, :, pl.ds(top, LOOK_AZ)].reshape(rows, LCOL)
                packed = packed + jnp.dot(
                    samples, pick.astype(jnp.bfloat16), preferred_element_type=jnp.float32
                )
            packed = packed.astype(jnp.bfloat16).reshape(2 * ITEMS, LOOK_AZ, 2, LCOL)
            for index in range(2 * LOOK_AZ):
                part, line = index // LOOK_AZ, index % LOOK_AZ
                lanes = slice(index % 7 * LCOL, (index % 7 + 1) * LCOL)
                out[:, index // 7, slots_of(parts), :, lanes] = packed[
                    part * ITEMS : (part + 1) * ITEMS, line
                ]


def cut(images, parts, middle, after=None):
    block = jax.ShapeDtypeStruct((ITEMS, 2, slots_of(parts) + middle, 2, MAIN), jnp.bfloat16)
    operands = (images,) + (() if after is None else (after,))
    return pl.pallas_call(
        functools.partial(cut_kernel, parts, middle),
        out_shape=[block] * 4,
        in_specs=[HBM, ANYWHERE][: len(operands)],
        out_specs=[VMEM] * 4,
        scratch_shapes=[
            pltpu.VMEM((2, 2 * ITEMS, 2 * LOOK_AZ, 2, LCOL), jnp.bfloat16),
            pltpu.SemaphoreType.DMA,
            pltpu.SemaphoreType.DMA((8 * len(parts),)),
        ],
        compiler_params=pltpu.CompilerParams(vmem_limit_bytes=8 << 20),
    )(*operands)


def meet(to1, to2, to3, own):
    def ring(step):
        return [(i, (i + step) % 4) for i in range(4)]

    three = lax.ppermute(to1, "date", ring(1))
    one = lax.ppermute(to3, "date", ring(3))
    two = lax.ppermute(to2, "date", ring(2))
    return own, one, two, three


def add_lines(epochs, mains, slot, middles, spare, index, lines, box, img, hi, lo):
    group = lax.axis_index("date")
    left = lax.broadcasted_iota(jnp.int32, (16, LCOL), 1) < 64
    for step, (main, middle) in enumerate(zip(mains, middles)):
        base = lax.rem(group + step, 4) * 2
        for line in range(lines):
            for date in range(2):
                pixels = jnp.swapaxes(main[:, date, slot + line], 0, 1).reshape(16, MAIN)
                img[base + date, line, :, 0:MAIN] = pixels.astype(jnp.float32)
            lanes = slice((index + line) % 7 * LCOL, ((index + line) % 7 + 1) * LCOL)
            packed = middle[:, (index + line) // 7, spare, :, lanes]
            packed = jnp.swapaxes(packed, 0, 1).reshape(16, LCOL)
            packed = packed.astype(jnp.float32)
            img[base, line, :, MAIN:WIDE] = jnp.where(left, packed, 0.0)
            img[base + 1, line, :, MAIN:WIDE] = jnp.where(left, pltpu.roll(packed, 64, 1), 0.0)

    def split(values, row):
        upper = values.astype(jnp.bfloat16)
        hi[pl.ds(row, 16), :] = upper
        lo[pl.ds(row, 16), :] = (values - upper.astype(jnp.float32)).astype(jnp.bfloat16)

    def power(half, carry):
        total = []
        for date in range(2):
            acc = jnp.zeros((ITEMS, WIDE), jnp.float32)
            for line in range(lines):
                re = img[2 * half + date, line, 0:8, :]
                im = img[2 * half + date, line, 8:16, :]
                acc = acc + (re * re + im * im)
            total.append(acc)
        split(jnp.concatenate(total, axis=0), pl.multiple_of(half * 16, 16))
        return carry

    lax.fori_loop(0, DATES // 2, power, 0)

    def cross(k, carry):
        a, b = epochs[0, k], epochs[1, k]
        acc_re = jnp.zeros((ITEMS, WIDE), jnp.float32)
        acc_im = jnp.zeros((ITEMS, WIDE), jnp.float32)
        for line in range(lines):
            re_a, im_a = img[a, line, 0:8, :], img[a, line, 8:16, :]
            re_b, im_b = img[b, line, 0:8, :], img[b, line, 8:16, :]
            acc_re = acc_re + (re_a * re_b + im_a * im_b)
            acc_im = acc_im + (im_a * re_b - re_a * im_b)
        split(jnp.concatenate([acc_re, acc_im], axis=0), pl.multiple_of(64 + k * 16, 16))
        return carry

    lax.fori_loop(0, PAIRS, cross, 0)
    return jnp.dot(hi[...], box[...], preferred_element_type=jnp.float32) + jnp.dot(
        lo[...], box[...], preferred_element_type=jnp.float32
    )


def coherence(epochs, part, sums, out):
    left = lax.broadcasted_iota(jnp.int32, (ITEMS, LCOL), 1) < 64
    for owner in range(4):
        rows = []
        for kk in range(4):
            k = owner * 4 + kk
            power_a = sums[pl.ds(pl.multiple_of(epochs[0, k] * 8, 8), 8), :]
            power_b = sums[pl.ds(pl.multiple_of(epochs[1, k] * 8, 8), 8), :]
            weight = 1.0 / jnp.sqrt((power_a + EPS) * (power_b + EPS))
            cross = jnp.where(
                left, sums[64 + k * 16 : 72 + k * 16, :], sums[72 + k * 16 : 80 + k * 16, :]
            )
            rows.append(cross * weight)
        out[part * ITEMS : (part + 1) * ITEMS, owner] = jnp.swapaxes(
            jnp.stack(rows, axis=0), 0, 1
        )


def looks_kernel(chunk, epochs, *rest):
    mains, rest, (img, hi, lo, sums) = rest[:4], rest[4:-4], rest[-4:]
    middles = mains
    if chunk == 0:
        box, _, out = rest
    elif chunk == 1:
        box, _, out, most = rest
    else:
        middles, (box, most, _, out) = rest[:4], rest[4:]
    spare = slots_of(CHUNKS[min(chunk, 1)])
    slot = 0
    for first, low, high in CHUNKS[chunk]:
        part = first // ITEMS
        total = add_lines(
            epochs,
            mains,
            slot,
            middles,
            spare,
            part % 2 * LOOK_AZ + low,
            high - low,
            box,
            img,
            hi,
            lo,
        )
        slot += high - low
        if low > 0:
            total = total + most[...]
        if high < LOOK_AZ:
            most[...] = total
        else:
            sums[...] = total * SCALE
            coherence(epochs, part, sums, out)


def looks(chunk, epochs, operands, out_shape, aliases):
    lines = sum(high - low for _, low, high in CHUNKS[chunk])
    work = lines * ITEMS * WIDE * (PAIRS * 8 + DATES * 4) + 4 * ROWS * WIDE * LCOL
    return pl.pallas_call(
        functools.partial(looks_kernel, chunk),
        out_shape=out_shape,
        grid_spec=pltpu.PrefetchScalarGridSpec(
            num_scalar_prefetch=1,
            grid=(),
            in_specs=[VMEM if x.ndim > 1 else SMEM for x in operands],
            out_specs=jax.tree.map(lambda _: VMEM, out_shape),
            scratch_shapes=[
                pltpu.VMEM((DATES, min(lines, LOOK_AZ), 16, WIDE), jnp.float32),
                pltpu.VMEM((ROWS, WIDE), jnp.bfloat16),
                pltpu.VMEM((ROWS, WIDE), jnp.bfloat16),
                pltpu.VMEM((ROWS, LCOL), jnp.float32),
            ],
        ),
        input_output_aliases=aliases,
        cost_estimate=pl.CostEstimate(
            flops=work, bytes_accessed=DATES * lines * 16 * WIDE * 2, transcendentals=0
        ),
        compiler_params=pltpu.CompilerParams(vmem_limit_bytes=24 << 20),
    )(epochs, *operands)


def place_kernel(table, got, out, rows):
    lane = lax.broadcasted_iota(jnp.int32, (8, LCOL), 1) < 64
    row = lax.broadcasted_iota(jnp.int32, (8, LCOL), 0) < 4
    keep = lane == row
    for burst in range(TILES):
        position = table[burst]
        valid = jnp.where(position < table[TILES], 1.0, 0.0).astype(jnp.float32)
        base = pl.multiple_of(position * 16, 16)
        for look in range(2):
            halves = got[burst * 2 + look]
            crossed = pltpu.roll(pltpu.roll(halves, 64, 1), 4, 0)
            rows[pl.ds(base + look * 8, 8), :] = jnp.where(keep, halves, crossed) * valid
    for pair in range(4):
        for part in range(2):
            for eight in range(8):
                out[pair, part, eight * 8 : eight * 8 + 8, :] = rows[
                    pl.ds(eight * 64 + part * 4 + pair, 8, stride=8), :
                ]


def on_device(complex_images, segment_position_map, usable_position_total, interferogram_epochs):
    images = complex_images[:, 0].transpose(0, 1, 3, 2, 4)
    epochs = interferogram_epochs.T
    table = jnp.concatenate([segment_position_map[0], usable_position_total])

    half = lax.rem(lax.axis_index("date"), 2)
    lane = jnp.arange(WIDE)
    place = jnp.where(lane < MAIN, lane + 64 * half, lane - MAIN * half)
    look = jnp.where(lane < MAIN + 64, place // LOOK_RG, -1)
    box = (look[:, None] == jnp.arange(LCOL)[None, :] % 64).astype(jnp.bfloat16)

    chunk0 = meet(*cut(images, CHUNKS[0], 1))
    chunk1 = meet(*cut(images, CHUNKS[1], 1, chunk0[3]))

    shape = jax.ShapeDtypeStruct((TILES, 4, 4, LCOL), jnp.float32)
    partial = jax.ShapeDtypeStruct((ROWS, LCOL), jnp.float32)
    gamma = looks(0, epochs, (*chunk0, box, table), shape, {})
    chunk2 = meet(*cut(images, CHUNKS[2], 0, gamma))
    gamma, most = looks(1, epochs, (*chunk1, box, gamma), (shape, partial), {6: 0})
    gamma = looks(2, epochs, (*chunk2, *chunk1, box, most, gamma), shape, {11: 0})
    got = lax.all_to_all(
        gamma.reshape(128, 4, LCOL), ("tile", "date"), split_axis=0, concat_axis=0, tiled=True
    ).reshape(64, 8, LCOL)
    return pl.pallas_call(
        place_kernel,
        out_shape=jax.ShapeDtypeStruct((4, 2, 64, LCOL), jnp.float32),
        grid_spec=pltpu.PrefetchScalarGridSpec(
            num_scalar_prefetch=1,
            grid=(),
            in_specs=[VMEM],
            out_specs=VMEM,
            scratch_shapes=[pltpu.VMEM((512, LCOL), jnp.float32)],
        ),
        compiler_params=pltpu.CompilerParams(vmem_limit_bytes=4 << 20),
    )(table, got)


def solution(mesh):
    in_specs = (P("date", "tile", None, None, None, None), P("tile", None), P("tile"), P())
    out_specs = P("date", None, None, "tile")
    return jax.shard_map(
        on_device, mesh=mesh, in_specs=in_specs, out_specs=out_specs, check_vma=False
    )
```

```python
import functools

import jax
import jax.numpy as jnp
from jax import lax
from jax.experimental import pallas as pl
from jax.experimental.pallas import tpu as pltpu
from jax.sharding import PartitionSpec as P

LOOK_RG = 15
LOOK_AZ = 5
EPS = 1e-05
SCALE = 1.0 / (LOOK_AZ * LOOK_RG)
DATES = 8
PAIRS = 16
ITEMS = 8
RG = 1920
LCOL = 128
ROWS = 320
TILES = 32
MAIN = 896
WIDE = 1024
CHUNKS = (((0, 0, 5), (8, 0, 5)), ((16, 0, 5), (24, 0, 4)), ((24, 4, 5),))

VMEM = pl.BlockSpec(memory_space=pltpu.VMEM)
SMEM = pl.BlockSpec(memory_space=pltpu.SMEM)
HBM = pl.BlockSpec(memory_space=pltpu.HBM)
ANYWHERE = pl.BlockSpec(memory_space=pl.ANY)


def slots_of(parts):
    return sum(high - low for _, low, high in parts)


def cut_kernel(parts, middle, images, *rest):
    to1, to2, to3, own, block, middle_sem, sem = rest[-7:]
    if middle:
        first = parts[0][0]
        fetch = pltpu.make_async_copy(
            images.at[:, first : first + 2 * ITEMS, :, :, MAIN:WIDE], block, middle_sem
        )
        fetch.start()
    group = lax.axis_index("date")
    takers = [
        (lax.rem(group + step, 4), out)
        for step, out in ((1, to1), (3, to3), (2, to2), (0, own))
    ]
    copies = []
    for taker, out in takers:
        top, left = lax.div(taker, 2) * LOOK_AZ, lax.rem(taker, 2) * WIDE
        filled = 0
        for first, low, high in parts:
            lines, slots = pl.ds(top + low, high - low), slice(filled, filled + high - low)
            filled += high - low
            for date in range(2):
                copies.append(
                    pltpu.make_async_copy(
                        images.at[
                            date,
                            first : first + ITEMS,
                            lines,
                            :,
                            pl.ds(pl.multiple_of(left, WIDE), MAIN),
                        ],
                        out.at[:, date, slots],
                        sem.at[len(copies)],
                    )
                )
                copies[-1].start()
    if middle:
        fetch.wait()
    for copy in copies:
        copy.wait()
    if middle:
        source = lax.broadcasted_iota(jnp.int32, (LCOL, LCOL), 0)
        lane = lax.broadcasted_iota(jnp.int32, (LCOL, LCOL), 1)
        rows = 2 * ITEMS * LOOK_AZ * 2
        for taker, out in takers:
            top, half = lax.div(taker, 2) * LOOK_AZ, lax.rem(taker, 2)
            packed = jnp.zeros((rows, LCOL), jnp.float32)
            for date in range(2):
                moved = lane + 64 * half - 64 * date
                pick = jnp.where((source == moved) & ((lane < 64) == (date == 0)), 1.0, 0.0)
                samples = block[date, :, pl.ds(top, LOOK_AZ)].reshape(rows, LCOL)
                packed = packed + jnp.dot(
                    samples, pick.astype(jnp.bfloat16), preferred_element_type=jnp.float32
                )
            packed = packed.astype(jnp.bfloat16).reshape(2 * ITEMS, LOOK_AZ, 2, LCOL)
            for index in range(2 * LOOK_AZ):
                part, line = index // LOOK_AZ, index % LOOK_AZ
                lanes = slice(index % 7 * LCOL, (index % 7 + 1) * LCOL)
                out[:, index // 7, slots_of(parts), :, lanes] = packed[
                    part * ITEMS : (part + 1) * ITEMS, line
                ]


def cut(images, parts, middle, after=None):
    block = jax.ShapeDtypeStruct((ITEMS, 2, slots_of(parts) + middle, 2, MAIN), jnp.bfloat16)
    operands = (images,) + (() if after is None else (after,))
    return pl.pallas_call(
        functools.partial(cut_kernel, parts, middle),
        out_shape=[block] * 4,
        in_specs=[HBM, ANYWHERE][: len(operands)],
        out_specs=[VMEM] * 4,
        scratch_shapes=[
            pltpu.VMEM((2, 2 * ITEMS, 2 * LOOK_AZ, 2, LCOL), jnp.bfloat16),
            pltpu.SemaphoreType.DMA,
            pltpu.SemaphoreType.DMA((8 * len(parts),)),
        ],
        compiler_params=pltpu.CompilerParams(vmem_limit_bytes=8 << 20),
    )(*operands)


def meet(to1, to2, to3, own):
    def ring(step):
        return [(i, (i + step) % 4) for i in range(4)]

    three = lax.ppermute(to1, "date", ring(1))
    one = lax.ppermute(to3, "date", ring(3))
    two = lax.ppermute(to2, "date", ring(2))
    return own, one, two, three


def add_lines(epochs, mains, slot, middles, spare, index, lines, box, img, hi, lo):
    group = lax.axis_index("date")
    left = lax.broadcasted_iota(jnp.int32, (16, LCOL), 1) < 64
    for step, (main, middle) in enumerate(zip(mains, middles)):
        base = lax.rem(group + step, 4) * 2
        for line in range(lines):
            for date in range(2):
                pixels = jnp.swapaxes(main[:, date, slot + line], 0, 1).reshape(16, MAIN)
                img[base + date, line, :, 0:MAIN] = pixels.astype(jnp.float32)
            lanes = slice((index + line) % 7 * LCOL, ((index + line) % 7 + 1) * LCOL)
            packed = middle[:, (index + line) // 7, spare, :, lanes]
            packed = jnp.swapaxes(packed, 0, 1).reshape(16, LCOL)
            packed = packed.astype(jnp.float32)
            img[base, line, :, MAIN:WIDE] = jnp.where(left, packed, 0.0)
            img[base + 1, line, :, MAIN:WIDE] = jnp.where(left, pltpu.roll(packed, 64, 1), 0.0)

    def split(values, row):
        upper = values.astype(jnp.bfloat16)
        hi[pl.ds(row, 16), :] = upper
        lo[pl.ds(row, 16), :] = (values - upper.astype(jnp.float32)).astype(jnp.bfloat16)

    def power(half, carry):
        total = []
        for date in range(2):
            acc = jnp.zeros((ITEMS, WIDE), jnp.float32)
            for line in range(lines):
                re = img[2 * half + date, line, 0:8, :]
                im = img[2 * half + date, line, 8:16, :]
                acc = acc + (re * re + im * im)
            total.append(acc)
        split(jnp.concatenate(total, axis=0), pl.multiple_of(half * 16, 16))
        return carry

    lax.fori_loop(0, DATES // 2, power, 0)

    def cross(k, carry):
        a, b = epochs[0, k], epochs[1, k]
        acc_re = jnp.zeros((ITEMS, WIDE), jnp.float32)
        acc_im = jnp.zeros((ITEMS, WIDE), jnp.float32)
        for line in range(lines):
            re_a, im_a = img[a, line, 0:8, :], img[a, line, 8:16, :]
            re_b, im_b = img[b, line, 0:8, :], img[b, line, 8:16, :]
            acc_re = acc_re + (re_a * re_b + im_a * im_b)
            acc_im = acc_im + (im_a * re_b - re_a * im_b)
        split(jnp.concatenate([acc_re, acc_im], axis=0), pl.multiple_of(64 + k * 16, 16))
        return carry

    lax.fori_loop(0, PAIRS, cross, 0)
    return jnp.dot(hi[...], box[...], preferred_element_type=jnp.float32) + jnp.dot(
        lo[...], box[...], preferred_element_type=jnp.float32
    )


def coherence(epochs, part, sums, out):
    left = lax.broadcasted_iota(jnp.int32, (ITEMS, LCOL), 1) < 64
    for owner in range(4):
        rows = []
        for kk in range(4):
            k = owner * 4 + kk
            power_a = sums[pl.ds(pl.multiple_of(epochs[0, k] * 8, 8), 8), :]
            power_b = sums[pl.ds(pl.multiple_of(epochs[1, k] * 8, 8), 8), :]
            weight = 1.0 / jnp.sqrt((power_a + EPS) * (power_b + EPS))
            cross = jnp.where(
                left, sums[64 + k * 16 : 72 + k * 16, :], sums[72 + k * 16 : 80 + k * 16, :]
            )
            rows.append(cross * weight)
        out[part * ITEMS : (part + 1) * ITEMS, owner] = jnp.swapaxes(
            jnp.stack(rows, axis=0), 0, 1
        )


def looks_kernel(chunk, epochs, *rest):
    mains, rest, (img, hi, lo, sums) = rest[:4], rest[4:-4], rest[-4:]
    middles = mains
    if chunk == 0:
        box, _, out = rest
    elif chunk == 1:
        box, _, out, most = rest
    else:
        middles, (box, most, _, out) = rest[:4], rest[4:]
    spare = slots_of(CHUNKS[min(chunk, 1)])
    slot = 0
    for first, low, high in CHUNKS[chunk]:
        part = first // ITEMS
        total = add_lines(
            epochs,
            mains,
            slot,
            middles,
            spare,
            part % 2 * LOOK_AZ + low,
            high - low,
            box,
            img,
            hi,
            lo,
        )
        slot += high - low
        if low > 0:
            total = total + most[...]
        if high < LOOK_AZ:
            most[...] = total
        else:
            sums[...] = total * SCALE
            coherence(epochs, part, sums, out)


def looks(chunk, epochs, operands, out_shape, aliases):
    lines = sum(high - low for _, low, high in CHUNKS[chunk])
    work = lines * ITEMS * WIDE * (PAIRS * 8 + DATES * 4) + 4 * ROWS * WIDE * LCOL
    return pl.pallas_call(
        functools.partial(looks_kernel, chunk),
        out_shape=out_shape,
        grid_spec=pltpu.PrefetchScalarGridSpec(
            num_scalar_prefetch=1,
            grid=(),
            in_specs=[VMEM if x.ndim > 1 else SMEM for x in operands],
            out_specs=jax.tree.map(lambda _: VMEM, out_shape),
            scratch_shapes=[
                pltpu.VMEM((DATES, min(lines, LOOK_AZ), 16, WIDE), jnp.float32),
                pltpu.VMEM((ROWS, WIDE), jnp.bfloat16),
                pltpu.VMEM((ROWS, WIDE), jnp.bfloat16),
                pltpu.VMEM((ROWS, LCOL), jnp.float32),
            ],
        ),
        input_output_aliases=aliases,
        cost_estimate=pl.CostEstimate(
            flops=work, bytes_accessed=DATES * lines * 16 * WIDE * 2, transcendentals=0
        ),
        compiler_params=pltpu.CompilerParams(vmem_limit_bytes=24 << 20),
    )(epochs, *operands)


def place_kernel(table, got, out, rows):
    lane = lax.broadcasted_iota(jnp.int32, (8, LCOL), 1) < 64
    row = lax.broadcasted_iota(jnp.int32, (8, LCOL), 0) < 4
    keep = lane == row
    for burst in range(TILES):
        position = table[burst]
        valid = jnp.where(position < table[TILES], 1.0, 0.0).astype(jnp.float32)
        base = pl.multiple_of(position * 16, 16)
        for look in range(2):
            halves = got[burst * 2 + look]
            crossed = pltpu.roll(pltpu.roll(halves, 64, 1), 4, 0)
            rows[pl.ds(base + look * 8, 8), :] = jnp.where(keep, halves, crossed) * valid
    for pair in range(4):
        for part in range(2):
            for eight in range(8):
                out[pair, part, eight * 8 : eight * 8 + 8, :] = rows[
                    pl.ds(eight * 64 + part * 4 + pair, 8, stride=8), :
                ]


def on_device(complex_images, segment_position_map, usable_position_total, interferogram_epochs):
    images = complex_images[:, 0].transpose(0, 1, 3, 2, 4)
    epochs = interferogram_epochs.T
    table = jnp.concatenate([segment_position_map[0], usable_position_total])

    half = lax.rem(lax.axis_index("date"), 2)
    lane = jnp.arange(WIDE)
    place = jnp.where(lane < MAIN, lane + 64 * half, lane - MAIN * half)
    look = jnp.where(lane < MAIN + 64, place // LOOK_RG, -1)
    box = (look[:, None] == jnp.arange(LCOL)[None, :] % 64).astype(jnp.bfloat16)

    chunk0 = meet(*cut(images, CHUNKS[0], 1))
    chunk1 = meet(*cut(images, CHUNKS[1], 1, chunk0[0]))

    shape = jax.ShapeDtypeStruct((TILES, 4, 4, LCOL), jnp.float32)
    partial = jax.ShapeDtypeStruct((ROWS, LCOL), jnp.float32)
    gamma = looks(0, epochs, (*chunk0, box, table), shape, {})
    chunk2 = meet(*cut(images, CHUNKS[2], 0, gamma))
    gamma, most = looks(1, epochs, (*chunk1, box, gamma), (shape, partial), {6: 0})
    gamma = looks(2, epochs, (*chunk2, *chunk1, box, most, gamma), shape, {11: 0})
    got = lax.all_to_all(
        gamma.reshape(128, 4, LCOL), ("tile", "date"), split_axis=0, concat_axis=0, tiled=True
    ).reshape(64, 8, LCOL)
    return pl.pallas_call(
        place_kernel,
        out_shape=jax.ShapeDtypeStruct((4, 2, 64, LCOL), jnp.float32),
        grid_spec=pltpu.PrefetchScalarGridSpec(
            num_scalar_prefetch=1,
            grid=(),
            in_specs=[VMEM],
            out_specs=VMEM,
            scratch_shapes=[pltpu.VMEM((512, LCOL), jnp.float32)],
        ),
        compiler_params=pltpu.CompilerParams(vmem_limit_bytes=4 << 20),
    )(table, got)


def solution(mesh):
    in_specs = (P("date", "tile", None, None, None, None), P("tile", None), P("tile"), P())
    out_specs = P("date", None, None, "tile")
    return jax.shard_map(
        on_device, mesh=mesh, in_specs=in_specs, out_specs=out_specs, check_vma=False
    )
```

```python
import functools

import jax
import jax.numpy as jnp
from jax import lax
from jax.experimental import pallas as pl
from jax.experimental.pallas import tpu as pltpu
from jax.sharding import PartitionSpec as P

LOOK_RG = 15
LOOK_AZ = 5
EPS = 1e-05
SCALE = 1.0 / (LOOK_AZ * LOOK_RG)
DATES = 8
PAIRS = 16
ITEMS = 8
RG = 1920
LCOL = 128
ROWS = 320
CHUNKS = ((0, 0, 5), (8, 0, 4), (8, 4, 5))
HALF = 16

VMEM = pl.BlockSpec(memory_space=pltpu.VMEM)
SMEM = pl.BlockSpec(memory_space=pltpu.SMEM)
HBM = pl.BlockSpec(memory_space=pltpu.HBM)
ANYWHERE = pl.BlockSpec(memory_space=pl.ANY)


def cut_kernel(chunk, images, *rest):
    to1, to2, to3, own, sem = rest[-5:]
    first, low, high = chunk
    group = lax.axis_index("date")
    copies = []
    for step, out in ((1, to1), (3, to3), (2, to2), (0, own)):
        taker = lax.rem(group + step, 4)
        tiles = pl.ds(lax.rem(taker, 2) * HALF + first, ITEMS)
        lines = pl.ds(lax.div(taker, 2) * LOOK_AZ + low, high - low)
        for date in range(2):
            copies.append(
                pltpu.make_async_copy(
                    images.at[date, tiles, lines], out.at[:, date], sem.at[len(copies)]
                )
            )
            copies[-1].start()
    for copy in copies:
        copy.wait()


def cut(images, chunk, after=None):
    _, low, high = chunk
    block = jax.ShapeDtypeStruct((ITEMS, 2, high - low, 2, RG), jnp.bfloat16)
    operands = (images,) + (() if after is None else (after,))
    return pl.pallas_call(
        functools.partial(cut_kernel, chunk),
        out_shape=[block] * 4,
        in_specs=[HBM, ANYWHERE][: len(operands)],
        out_specs=[VMEM] * 4,
        scratch_shapes=[pltpu.SemaphoreType.DMA((8,))],
        compiler_params=pltpu.CompilerParams(vmem_limit_bytes=8 << 20),
    )(*operands)


def meet(to1, to2, to3, own):
    def ring(step):
        return [(i, (i + step) % 4) for i in range(4)]

    three = lax.ppermute(to1, "date", ring(1))
    one = lax.ppermute(to3, "date", ring(3))
    two = lax.ppermute(to2, "date", ring(2))
    return own, one, two, three


def add_lines(epochs, blocks, box, img, hi, lo):
    group = lax.axis_index("date")
    lines = blocks[0].shape[2]
    for step, block in enumerate(blocks):
        base = lax.rem(group + step, 4) * 2
        for date in range(2):
            for line in range(lines):
                pixels = jnp.swapaxes(block[:, date, line], 0, 1).reshape(16, RG)
                img[base + date, line] = pixels.astype(jnp.float32)

    def split(values, row):
        upper = values.astype(jnp.bfloat16)
        hi[pl.ds(row, 16), :] = upper
        lo[pl.ds(row, 16), :] = (values - upper.astype(jnp.float32)).astype(jnp.bfloat16)

    def power(half, carry):
        total = []
        for date in range(2):
            acc = jnp.zeros((ITEMS, RG), jnp.float32)
            for line in range(lines):
                re = img[2 * half + date, line, 0:8, :]
                im = img[2 * half + date, line, 8:16, :]
                acc = acc + (re * re + im * im)
            total.append(acc)
        split(jnp.concatenate(total, axis=0), pl.multiple_of(half * 16, 16))
        return carry

    lax.fori_loop(0, DATES // 2, power, 0, unroll=True)

    def cross(k, carry):
        a, b = epochs[0, k], epochs[1, k]
        acc_re = jnp.zeros((ITEMS, RG), jnp.float32)
        acc_im = jnp.zeros((ITEMS, RG), jnp.float32)
        for line in range(lines):
            re_a, im_a = img[a, line, 0:8, :], img[a, line, 8:16, :]
            re_b, im_b = img[b, line, 0:8, :], img[b, line, 8:16, :]
            acc_re = acc_re + (re_a * re_b + im_a * im_b)
            acc_im = acc_im + (im_a * re_b - re_a * im_b)
        split(jnp.concatenate([acc_re, acc_im], axis=0), pl.multiple_of(64 + k * 16, 16))
        return carry

    lax.fori_loop(0, PAIRS, cross, 0, unroll=4)
    return jnp.dot(hi[...], box[...], preferred_element_type=jnp.float32) + jnp.dot(
        lo[...], box[...], preferred_element_type=jnp.float32
    )


def coherence(epochs, part, sums, out):
    start = lax.rem(lax.axis_index("date"), 2) * HALF + part * ITEMS
    for owner in range(4):
        rows = []
        for kk in range(4):
            k = owner * 4 + kk
            power_a = sums[pl.ds(pl.multiple_of(epochs[0, k] * 8, 8), 8), :]
            power_b = sums[pl.ds(pl.multiple_of(epochs[1, k] * 8, 8), 8), :]
            weight = 1.0 / jnp.sqrt((power_a + EPS) * (power_b + EPS))
            rows.append(sums[64 + k * 16 : 72 + k * 16, :] * weight)
            rows.append(sums[72 + k * 16 : 80 + k * 16, :] * weight)
        out[pl.ds(start, ITEMS), owner] = jnp.swapaxes(jnp.stack(rows, axis=0), 0, 1)


def whole_kernel(epochs, own, one, two, three, box, table, out, img, hi, lo, sums):
    del table
    sums[...] = add_lines(epochs, (own, one, two, three), box, img, hi, lo) * SCALE
    coherence(epochs, 0, sums, out)


def most_kernel(epochs, own, one, two, three, box, after, later, img, hi, lo, sums):
    del after, sums
    later[...] = add_lines(epochs, (own, one, two, three), box, img, hi, lo)


def last_kernel(epochs, own, one, two, three, box, most, given, out, img, hi, lo, sums):
    del given
    total = add_lines(epochs, (own, one, two, three), box, img, hi, lo)
    sums[...] = (total + most[...]) * SCALE
    coherence(epochs, 1, sums, out)


def looks(kernel, epochs, operands, out_shape, lines, aliases={}):
    work = lines * ITEMS * RG * (PAIRS * 8 + DATES * 4) + 4 * ROWS * RG * LCOL
    return pl.pallas_call(
        kernel,
        out_shape=out_shape,
        grid_spec=pltpu.PrefetchScalarGridSpec(
            num_scalar_prefetch=1,
            grid=(),
            in_specs=[VMEM if x.ndim > 1 else SMEM for x in operands],
            out_specs=jax.tree.map(lambda _: VMEM, out_shape),
            scratch_shapes=[
                pltpu.VMEM((DATES, lines, 16, RG), jnp.float32),
                pltpu.VMEM((ROWS, RG), jnp.bfloat16),
                pltpu.VMEM((ROWS, RG), jnp.bfloat16),
                pltpu.VMEM((ROWS, LCOL), jnp.float32),
            ],
        ),
        input_output_aliases=aliases,
        cost_estimate=pl.CostEstimate(
            flops=work, bytes_accessed=DATES * lines * 16 * RG * 2, transcendentals=0
        ),
        compiler_params=pltpu.CompilerParams(vmem_limit_bytes=24 << 20),
    )(epochs, *operands)


def place_kernel(table, got, out, rows):
    half = lax.div(lax.axis_index("tile"), HALF)
    for burst in range(32):
        position = table[burst]
        valid = jnp.where(position < table[32], 1.0, 0.0).astype(jnp.float32)
        base = pl.multiple_of(position * 16, 16)
        rows[pl.ds(base, 8), :] = got[burst, half] * valid
        rows[pl.ds(base + 8, 8), :] = got[burst, 2 + half] * valid
    for plane in range(8):
        for part in range(8):
            out[plane // 2, plane % 2, part * 8 : part * 8 + 8, :] = rows[
                pl.ds(part * 64 + plane, 8, stride=8), :
            ]


def on_device(complex_images, segment_position_map, usable_position_total, interferogram_epochs):
    images = complex_images[:, 0].transpose(0, 1, 3, 2, 4)
    epochs = interferogram_epochs.T
    table = jnp.concatenate([segment_position_map[0], usable_position_total])
    box = (
        jnp.arange(RG)[:, None] // LOOK_RG == jnp.arange(LCOL)[None, :]
    ).astype(jnp.bfloat16)

    first = meet(*cut(images, CHUNKS[0]))
    second = meet(*cut(images, CHUNKS[1], first[3]))

    shape = jax.ShapeDtypeStruct((32, 4, 8, LCOL), jnp.float32)
    partial = jax.ShapeDtypeStruct((ROWS, LCOL), jnp.float32)
    gamma = looks(whole_kernel, epochs, (*first, box, table), shape, 5)
    third = meet(*cut(images, CHUNKS[2], gamma))
    most = looks(most_kernel, epochs, (*second, box, gamma), partial, 4)
    gamma = looks(last_kernel, epochs, (*third, box, most, gamma), shape, 1, {7: 0})
    got = lax.all_to_all(
        gamma.reshape(128, 8, LCOL), ("tile", "date"), split_axis=0, concat_axis=0, tiled=True
    ).reshape(32, 4, 8, LCOL)
    return pl.pallas_call(
        place_kernel,
        out_shape=jax.ShapeDtypeStruct((4, 2, 64, LCOL), jnp.float32),
        grid_spec=pltpu.PrefetchScalarGridSpec(
            num_scalar_prefetch=1,
            grid=(),
            in_specs=[VMEM],
            out_specs=VMEM,
            scratch_shapes=[pltpu.VMEM((512, LCOL), jnp.float32)],
        ),
        compiler_params=pltpu.CompilerParams(vmem_limit_bytes=4 << 20),
    )(table, got)


def solution(mesh):
    in_specs = (P("date", "tile", None, None, None, None), P("tile", None), P("tile"), P())
    out_specs = P("date", None, None, "tile")
    return jax.shard_map(
        on_device, mesh=mesh, in_specs=in_specs, out_specs=out_specs, check_vma=False
    )
```

```python
import functools

import jax
import jax.numpy as jnp
from jax import lax
from jax.experimental import pallas as pl
from jax.experimental.pallas import tpu as pltpu
from jax.sharding import PartitionSpec as P

LOOK_RG = 15
LOOK_AZ = 5
EPS = 1e-05
SCALE = 1.0 / (LOOK_AZ * LOOK_RG)
DATES = 8
PAIRS = 16
ITEMS = 8
RG = 1920
LCOL = 128
ROWS = 320
CHUNKS = ((0, 0, 5), (8, 0, 4), (8, 4, 5))
HALF = 16

VMEM = pl.BlockSpec(memory_space=pltpu.VMEM)
SMEM = pl.BlockSpec(memory_space=pltpu.SMEM)
HBM = pl.BlockSpec(memory_space=pltpu.HBM)
ANYWHERE = pl.BlockSpec(memory_space=pl.ANY)


def cut_kernel(chunk, images, *rest):
    to1, to2, to3, own, sem = rest[-5:]
    first, low, high = chunk
    group = lax.axis_index("date")
    copies = []
    for step, out in ((1, to1), (3, to3), (2, to2), (0, own)):
        taker = lax.rem(group + step, 4)
        tiles = pl.ds(lax.rem(taker, 2) * HALF + first, ITEMS)
        lines = pl.ds(lax.div(taker, 2) * LOOK_AZ + low, high - low)
        for date in range(2):
            copies.append(
                pltpu.make_async_copy(
                    images.at[date, tiles, lines], out.at[:, date], sem.at[len(copies)]
                )
            )
            copies[-1].start()
    for copy in copies:
        copy.wait()


def cut(images, chunk, after=None):
    _, low, high = chunk
    block = jax.ShapeDtypeStruct((ITEMS, 2, high - low, 2, RG), jnp.bfloat16)
    operands = (images,) + (() if after is None else (after,))
    return pl.pallas_call(
        functools.partial(cut_kernel, chunk),
        out_shape=[block] * 4,
        in_specs=[HBM, ANYWHERE][: len(operands)],
        out_specs=[VMEM] * 4,
        scratch_shapes=[pltpu.SemaphoreType.DMA((8,))],
        compiler_params=pltpu.CompilerParams(vmem_limit_bytes=8 << 20),
    )(*operands)


def meet(to1, to2, to3, own):
    def ring(step):
        return [(i, (i + step) % 4) for i in range(4)]

    three = lax.ppermute(to1, "date", ring(1))
    one = lax.ppermute(to3, "date", ring(3))
    two = lax.ppermute(to2, "date", ring(2))
    return own, one, two, three


def add_lines(epochs, blocks, box, img, hi, lo):
    group = lax.axis_index("date")
    lines = blocks[0].shape[2]
    for step, block in enumerate(blocks):
        base = lax.rem(group + step, 4) * 2
        for date in range(2):
            for line in range(lines):
                pixels = jnp.swapaxes(block[:, date, line], 0, 1).reshape(16, RG)
                img[base + date, line] = pixels.astype(jnp.float32)

    def split(values, row):
        upper = values.astype(jnp.bfloat16)
        hi[pl.ds(row, 16), :] = upper
        lo[pl.ds(row, 16), :] = (values - upper.astype(jnp.float32)).astype(jnp.bfloat16)

    def power(half, carry):
        total = []
        for date in range(2):
            acc = jnp.zeros((ITEMS, RG), jnp.float32)
            for line in range(lines):
                re = img[2 * half + date, line, 0:8, :]
                im = img[2 * half + date, line, 8:16, :]
                acc = acc + (re * re + im * im)
            total.append(acc)
        split(jnp.concatenate(total, axis=0), pl.multiple_of(half * 16, 16))
        return carry

    lax.fori_loop(0, DATES // 2, power, 0)

    def cross(k, carry):
        a, b = epochs[0, k], epochs[1, k]
        acc_re = jnp.zeros((ITEMS, RG), jnp.float32)
        acc_im = jnp.zeros((ITEMS, RG), jnp.float32)
        for line in range(lines):
            re_a, im_a = img[a, line, 0:8, :], img[a, line, 8:16, :]
            re_b, im_b = img[b, line, 0:8, :], img[b, line, 8:16, :]
            acc_re = acc_re + (re_a * re_b + im_a * im_b)
            acc_im = acc_im + (im_a * re_b - re_a * im_b)
        split(jnp.concatenate([acc_re, acc_im], axis=0), pl.multiple_of(64 + k * 16, 16))
        return carry

    lax.fori_loop(0, PAIRS, cross, 0)
    return jnp.dot(hi[...], box[...], preferred_element_type=jnp.float32) + jnp.dot(
        lo[...], box[...], preferred_element_type=jnp.float32
    )


def coherence(epochs, part, sums, out):
    start = lax.rem(lax.axis_index("date"), 2) * HALF + part * ITEMS
    for owner in range(4):
        rows = []
        for kk in range(4):
            k = owner * 4 + kk
            power_a = sums[pl.ds(pl.multiple_of(epochs[0, k] * 8, 8), 8), :]
            power_b = sums[pl.ds(pl.multiple_of(epochs[1, k] * 8, 8), 8), :]
            weight = 1.0 / jnp.sqrt((power_a + EPS) * (power_b + EPS))
            rows.append(sums[64 + k * 16 : 72 + k * 16, :] * weight)
            rows.append(sums[72 + k * 16 : 80 + k * 16, :] * weight)
        out[owner, pl.ds(start, ITEMS)] = jnp.swapaxes(jnp.stack(rows, axis=0), 0, 1)


def whole_kernel(epochs, own, one, two, three, box, table, out, img, hi, lo, sums):
    del table
    sums[...] = add_lines(epochs, (own, one, two, three), box, img, hi, lo) * SCALE
    coherence(epochs, 0, sums, out)


def most_kernel(epochs, own, one, two, three, box, after, later, img, hi, lo, sums):
    del after, sums
    later[...] = add_lines(epochs, (own, one, two, three), box, img, hi, lo)


def last_kernel(epochs, own, one, two, three, box, most, given, out, img, hi, lo, sums):
    del given
    total = add_lines(epochs, (own, one, two, three), box, img, hi, lo)
    sums[...] = (total + most[...]) * SCALE
    coherence(epochs, 1, sums, out)


def looks(kernel, epochs, operands, out_shape, lines, aliases={}):
    work = lines * ITEMS * RG * (PAIRS * 8 + DATES * 4) + 4 * ROWS * RG * LCOL
    return pl.pallas_call(
        kernel,
        out_shape=out_shape,
        grid_spec=pltpu.PrefetchScalarGridSpec(
            num_scalar_prefetch=1,
            grid=(),
            in_specs=[VMEM if x.ndim > 1 else SMEM for x in operands],
            out_specs=jax.tree.map(lambda _: VMEM, out_shape),
            scratch_shapes=[
                pltpu.VMEM((DATES, lines, 16, RG), jnp.float32),
                pltpu.VMEM((ROWS, RG), jnp.bfloat16),
                pltpu.VMEM((ROWS, RG), jnp.bfloat16),
                pltpu.VMEM((ROWS, LCOL), jnp.float32),
            ],
        ),
        input_output_aliases=aliases,
        cost_estimate=pl.CostEstimate(
            flops=work, bytes_accessed=DATES * lines * 16 * RG * 2, transcendentals=0
        ),
        compiler_params=pltpu.CompilerParams(vmem_limit_bytes=24 << 20),
    )(epochs, *operands)


def place_kernel(table, got, out, rows):
    half = lax.div(lax.axis_index("tile"), HALF)
    for burst in range(32):
        position = table[burst]
        valid = jnp.where(position < table[32], 1.0, 0.0).astype(jnp.float32)
        base = pl.multiple_of(position * 16, 16)
        rows[pl.ds(base, 8), :] = got[half, burst] * valid
        rows[pl.ds(base + 8, 8), :] = got[2 + half, burst] * valid
    for plane in range(8):
        for part in range(8):
            out[plane // 2, plane % 2, part * 8 : part * 8 + 8, :] = rows[
                pl.ds(part * 64 + plane, 8, stride=8), :
            ]


def on_device(complex_images, segment_position_map, usable_position_total, interferogram_epochs):
    images = complex_images[:, 0].transpose(0, 1, 3, 2, 4)
    epochs = interferogram_epochs.T
    table = jnp.concatenate([segment_position_map[0], usable_position_total])
    box = (
        jnp.arange(RG)[:, None] // LOOK_RG == jnp.arange(LCOL)[None, :]
    ).astype(jnp.bfloat16)

    first = meet(*cut(images, CHUNKS[0]))
    second = meet(*cut(images, CHUNKS[1], first[3]))

    shape = jax.ShapeDtypeStruct((4, 32, 8, LCOL), jnp.float32)
    partial = jax.ShapeDtypeStruct((ROWS, LCOL), jnp.float32)
    gamma = looks(whole_kernel, epochs, (*first, box, table), shape, 5)
    third = meet(*cut(images, CHUNKS[2], gamma))
    most = looks(most_kernel, epochs, (*second, box, gamma), partial, 4)
    gamma = looks(last_kernel, epochs, (*third, box, most, gamma), shape, 1, {7: 0})
    got = lax.all_to_all(
        gamma.reshape(128, 8, LCOL), ("date", "tile"), split_axis=0, concat_axis=0, tiled=True
    ).reshape(4, 32, 8, LCOL)
    return pl.pallas_call(
        place_kernel,
        out_shape=jax.ShapeDtypeStruct((4, 2, 64, LCOL), jnp.float32),
        grid_spec=pltpu.PrefetchScalarGridSpec(
            num_scalar_prefetch=1,
            grid=(),
            in_specs=[VMEM],
            out_specs=VMEM,
            scratch_shapes=[pltpu.VMEM((512, LCOL), jnp.float32)],
        ),
        compiler_params=pltpu.CompilerParams(vmem_limit_bytes=4 << 20),
    )(table, got)


def solution(mesh):
    in_specs = (P("date", "tile", None, None, None, None), P("tile", None), P("tile"), P())
    out_specs = P("date", None, None, "tile")
    return jax.shard_map(
        on_device, mesh=mesh, in_specs=in_specs, out_specs=out_specs, check_vma=False
    )
```

```python
import functools

import jax
import jax.numpy as jnp
from jax import lax
from jax.experimental import pallas as pl
from jax.experimental.pallas import tpu as pltpu
from jax.sharding import PartitionSpec as P

LOOK_RG = 15
LOOK_AZ = 5
EPS = 1e-05
SCALE = 1.0 / (LOOK_AZ * LOOK_RG)
DATES = 8
PAIRS = 16
ITEMS = 8
RG = 1920
LCOL = 128
ROWS = 320
CHUNKS = ((0, 0, 5), (8, 0, 4), (8, 4, 5))
HALF = 16

VMEM = pl.BlockSpec(memory_space=pltpu.VMEM)
SMEM = pl.BlockSpec(memory_space=pltpu.SMEM)
HBM = pl.BlockSpec(memory_space=pltpu.HBM)
ANYWHERE = pl.BlockSpec(memory_space=pl.ANY)


def cut_kernel(chunk, images, *rest):
    to1, to2, to3, own, sem = rest[-5:]
    first, low, high = chunk
    group = lax.axis_index("date")
    copies = []
    for step, out in ((1, to1), (3, to3), (2, to2), (0, own)):
        taker = lax.rem(group + step, 4)
        tiles = pl.ds(lax.rem(taker, 2) * HALF + first, ITEMS)
        lines = pl.ds(lax.div(taker, 2) * LOOK_AZ + low, high - low)
        for date in range(2):
            copies.append(
                pltpu.make_async_copy(
                    images.at[date, tiles, lines], out.at[:, date], sem.at[len(copies)]
                )
            )
            copies[-1].start()
    for copy in copies:
        copy.wait()


def cut(images, chunk, after=None):
    _, low, high = chunk
    block = jax.ShapeDtypeStruct((ITEMS, 2, high - low, 2, RG), jnp.bfloat16)
    operands = (images,) + (() if after is None else (after,))
    return pl.pallas_call(
        functools.partial(cut_kernel, chunk),
        out_shape=[block] * 4,
        in_specs=[HBM, ANYWHERE][: len(operands)],
        out_specs=[VMEM] * 4,
        scratch_shapes=[pltpu.SemaphoreType.DMA((8,))],
        compiler_params=pltpu.CompilerParams(vmem_limit_bytes=8 << 20),
    )(*operands)


def meet(to1, to2, to3, own):
    def ring(step):
        return [(i, (i + step) % 4) for i in range(4)]

    three = lax.ppermute(to1, "date", ring(1))
    one = lax.ppermute(to3, "date", ring(3))
    two = lax.ppermute(to2, "date", ring(2))
    return own, one, two, three


def add_lines(epochs, blocks, box, img, hi, lo):
    group = lax.axis_index("date")
    lines = blocks[0].shape[2]
    for step, block in enumerate(blocks):
        base = lax.rem(group + step, 4) * 2
        for date in range(2):
            for line in range(lines):
                pixels = jnp.swapaxes(block[:, date, line], 0, 1).reshape(16, RG)
                img[base + date, line] = pixels.astype(jnp.float32)

    def split(values, row):
        upper = values.astype(jnp.bfloat16)
        hi[pl.ds(row, 16), :] = upper
        lo[pl.ds(row, 16), :] = (values - upper.astype(jnp.float32)).astype(jnp.bfloat16)

    def power(half, carry):
        total = []
        for date in range(2):
            acc = jnp.zeros((ITEMS, RG), jnp.float32)
            for line in range(lines):
                re = img[2 * half + date, line, 0:8, :]
                im = img[2 * half + date, line, 8:16, :]
                acc = acc + (re * re + im * im)
            total.append(acc)
        split(jnp.concatenate(total, axis=0), pl.multiple_of(half * 16, 16))
        return carry

    lax.fori_loop(0, DATES // 2, power, 0)

    def cross(k, carry):
        a, b = epochs[0, k], epochs[1, k]
        acc_re = jnp.zeros((ITEMS, RG), jnp.float32)
        acc_im = jnp.zeros((ITEMS, RG), jnp.float32)
        for line in range(lines):
            re_a, im_a = img[a, line, 0:8, :], img[a, line, 8:16, :]
            re_b, im_b = img[b, line, 0:8, :], img[b, line, 8:16, :]
            acc_re = acc_re + (re_a * re_b + im_a * im_b)
            acc_im = acc_im + (im_a * re_b - re_a * im_b)
        split(jnp.concatenate([acc_re, acc_im], axis=0), pl.multiple_of(64 + k * 16, 16))
        return carry

    lax.fori_loop(0, PAIRS, cross, 0)
    return jnp.dot(hi[...], box[...], preferred_element_type=jnp.float32) + jnp.dot(
        lo[...], box[...], preferred_element_type=jnp.float32
    )


def coherence(epochs, part, sums, out):
    start = lax.rem(lax.axis_index("date"), 2) * HALF + part * ITEMS
    for owner in range(4):
        rows = []
        for kk in range(4):
            k = owner * 4 + kk
            power_a = sums[pl.ds(pl.multiple_of(epochs[0, k] * 8, 8), 8), :]
            power_b = sums[pl.ds(pl.multiple_of(epochs[1, k] * 8, 8), 8), :]
            weight = lax.rsqrt((power_a + EPS) * (power_b + EPS))
            rows.append(sums[64 + k * 16 : 72 + k * 16, :] * weight)
            rows.append(sums[72 + k * 16 : 80 + k * 16, :] * weight)
        out[owner, pl.ds(start, ITEMS)] = jnp.swapaxes(jnp.stack(rows, axis=0), 0, 1)


def whole_kernel(epochs, own, one, two, three, box, table, out, img, hi, lo, sums):
    del table
    sums[...] = add_lines(epochs, (own, one, two, three), box, img, hi, lo) * SCALE
    coherence(epochs, 0, sums, out)


def most_kernel(epochs, own, one, two, three, box, after, later, img, hi, lo, sums):
    del after, sums
    later[...] = add_lines(epochs, (own, one, two, three), box, img, hi, lo)


def last_kernel(epochs, own, one, two, three, box, most, given, out, img, hi, lo, sums):
    del given
    total = add_lines(epochs, (own, one, two, three), box, img, hi, lo)
    sums[...] = (total + most[...]) * SCALE
    coherence(epochs, 1, sums, out)


def looks(kernel, epochs, operands, out_shape, lines, aliases={}):
    work = lines * ITEMS * RG * (PAIRS * 8 + DATES * 4) + 4 * ROWS * RG * LCOL
    return pl.pallas_call(
        kernel,
        out_shape=out_shape,
        grid_spec=pltpu.PrefetchScalarGridSpec(
            num_scalar_prefetch=1,
            grid=(),
            in_specs=[VMEM if x.ndim > 1 else SMEM for x in operands],
            out_specs=jax.tree.map(lambda _: VMEM, out_shape),
            scratch_shapes=[
                pltpu.VMEM((DATES, lines, 16, RG), jnp.float32),
                pltpu.VMEM((ROWS, RG), jnp.bfloat16),
                pltpu.VMEM((ROWS, RG), jnp.bfloat16),
                pltpu.VMEM((ROWS, LCOL), jnp.float32),
            ],
        ),
        input_output_aliases=aliases,
        cost_estimate=pl.CostEstimate(
            flops=work, bytes_accessed=DATES * lines * 16 * RG * 2, transcendentals=0
        ),
        compiler_params=pltpu.CompilerParams(vmem_limit_bytes=24 << 20),
    )(epochs, *operands)


def place_kernel(table, got, out, rows):
    half = lax.div(lax.axis_index("tile"), HALF)
    pair = pl.program_id(0)

    @pl.when(pair == 0)
    def _():
        for burst in range(32):
            position = table[burst]
            valid = jnp.where(position < table[32], 1.0, 0.0).astype(jnp.float32)
            base = pl.multiple_of(position * 16, 16)
            rows[pl.ds(base, 8), :] = got[half, burst] * valid
            rows[pl.ds(base + 8, 8), :] = got[2 + half, burst] * valid

    for part in range(2):
        for eight in range(8):
            out[0, part, eight * 8 : eight * 8 + 8, :] = rows[
                pl.ds(eight * 64 + pair * 2 + part, 8, stride=8), :
            ]


def on_device(complex_images, segment_position_map, usable_position_total, interferogram_epochs):
    images = complex_images[:, 0].transpose(0, 1, 3, 2, 4)
    epochs = interferogram_epochs.T
    table = jnp.concatenate([segment_position_map[0], usable_position_total])
    box = (
        jnp.arange(RG)[:, None] // LOOK_RG == jnp.arange(LCOL)[None, :]
    ).astype(jnp.bfloat16)

    first = meet(*cut(images, CHUNKS[0]))
    second = meet(*cut(images, CHUNKS[1], first[3]))

    shape = jax.ShapeDtypeStruct((4, 32, 8, LCOL), jnp.float32)
    partial = jax.ShapeDtypeStruct((ROWS, LCOL), jnp.float32)
    gamma = looks(whole_kernel, epochs, (*first, box, table), shape, 5)
    third = meet(*cut(images, CHUNKS[2], gamma))
    most = looks(most_kernel, epochs, (*second, box, gamma), partial, 4)
    gamma = looks(last_kernel, epochs, (*third, box, most, gamma), shape, 1, {7: 0})
    got = lax.all_to_all(
        gamma.reshape(128, 8, LCOL), ("date", "tile"), split_axis=0, concat_axis=0, tiled=True
    ).reshape(4, 32, 8, LCOL)
    return pl.pallas_call(
        place_kernel,
        out_shape=jax.ShapeDtypeStruct((4, 2, 64, LCOL), jnp.float32),
        grid_spec=pltpu.PrefetchScalarGridSpec(
            num_scalar_prefetch=1,
            grid=(4,),
            in_specs=[VMEM],
            out_specs=pl.BlockSpec((1, 2, 64, LCOL), lambda pair, table: (pair, 0, 0, 0)),
            scratch_shapes=[pltpu.VMEM((512, LCOL), jnp.float32)],
        ),
        compiler_params=pltpu.CompilerParams(vmem_limit_bytes=4 << 20),
    )(table, got)


def solution(mesh):
    in_specs = (P("date", "tile", None, None, None, None), P("tile", None), P("tile"), P())
    out_specs = P("date", None, None, "tile")
    return jax.shard_map(
        on_device, mesh=mesh, in_specs=in_specs, out_specs=out_specs, check_vma=False
    )
```

```python
import functools

import jax
import jax.numpy as jnp
from jax import lax
from jax.experimental import pallas as pl
from jax.experimental.pallas import tpu as pltpu
from jax.sharding import PartitionSpec as P

LOOK_RG = 15
LOOK_AZ = 5
EPS = 1e-05
SCALE = 1.0 / (LOOK_AZ * LOOK_RG)
DATES = 8
PAIRS = 16
ITEMS = 8
RG = 1920
LCOL = 128
ROWS = 320
CHUNKS = ((0, 0, 5), (8, 0, 4), (8, 4, 5))
HALF = 16

VMEM = pl.BlockSpec(memory_space=pltpu.VMEM)
SMEM = pl.BlockSpec(memory_space=pltpu.SMEM)
HBM = pl.BlockSpec(memory_space=pltpu.HBM)
ANYWHERE = pl.BlockSpec(memory_space=pl.ANY)


def cut_kernel(chunk, images, *rest):
    to1, to2, to3, own, sem = rest[-5:]
    first, low, high = chunk
    group = lax.axis_index("date")
    copies = []
    for step, out in ((1, to1), (3, to3), (2, to2), (0, own)):
        taker = lax.rem(group + step, 4)
        tiles = pl.ds(lax.rem(taker, 2) * HALF + first, ITEMS)
        lines = pl.ds(lax.div(taker, 2) * LOOK_AZ + low, high - low)
        for date in range(2):
            copies.append(
                pltpu.make_async_copy(
                    images.at[date, tiles, lines], out.at[:, date], sem.at[len(copies)]
                )
            )
            copies[-1].start()
    for copy in copies:
        copy.wait()


def cut(images, chunk, after=None):
    _, low, high = chunk
    block = jax.ShapeDtypeStruct((ITEMS, 2, high - low, 2, RG), jnp.bfloat16)
    operands = (images,) + (() if after is None else (after,))
    return pl.pallas_call(
        functools.partial(cut_kernel, chunk),
        out_shape=[block] * 4,
        in_specs=[HBM, ANYWHERE][: len(operands)],
        out_specs=[VMEM] * 4,
        scratch_shapes=[pltpu.SemaphoreType.DMA((8,))],
        compiler_params=pltpu.CompilerParams(vmem_limit_bytes=8 << 20),
    )(*operands)


def meet(to1, to2, to3, own):
    def ring(step):
        return [(i, (i + step) % 4) for i in range(4)]

    three = lax.ppermute(to1, "date", ring(1))
    one = lax.ppermute(to3, "date", ring(3))
    two = lax.ppermute(to2, "date", ring(2))
    return own, one, two, three


def add_lines(epochs, blocks, box, img, hi, lo):
    group = lax.axis_index("date")
    lines = blocks[0].shape[2]
    for step, block in enumerate(blocks):
        base = lax.rem(group + step, 4) * 2
        for date in range(2):
            for line in range(lines):
                pixels = jnp.swapaxes(block[:, date, line], 0, 1).reshape(16, RG)
                img[base + date, line] = pixels.astype(jnp.float32)

    def split(values, row):
        upper = values.astype(jnp.bfloat16)
        hi[pl.ds(row, 16), :] = upper
        lo[pl.ds(row, 16), :] = (values - upper.astype(jnp.float32)).astype(jnp.bfloat16)

    def power(half, carry):
        total = []
        for date in range(2):
            acc = jnp.zeros((ITEMS, RG), jnp.float32)
            for line in range(lines):
                re = img[2 * half + date, line, 0:8, :]
                im = img[2 * half + date, line, 8:16, :]
                acc = acc + (re * re + im * im)
            total.append(acc)
        split(jnp.concatenate(total, axis=0), pl.multiple_of(half * 16, 16))
        return carry

    lax.fori_loop(0, DATES // 2, power, 0)

    def cross(k, carry):
        a, b = epochs[0, k], epochs[1, k]
        acc_re = jnp.zeros((ITEMS, RG), jnp.float32)
        acc_im = jnp.zeros((ITEMS, RG), jnp.float32)
        for line in range(lines):
            re_a, im_a = img[a, line, 0:8, :], img[a, line, 8:16, :]
            re_b, im_b = img[b, line, 0:8, :], img[b, line, 8:16, :]
            acc_re = acc_re + (re_a * re_b + im_a * im_b)
            acc_im = acc_im + (im_a * re_b - re_a * im_b)
        split(jnp.concatenate([acc_re, acc_im], axis=0), pl.multiple_of(64 + k * 16, 16))
        return carry

    lax.fori_loop(0, PAIRS, cross, 0)
    return jnp.dot(hi[...], box[...], preferred_element_type=jnp.float32) + jnp.dot(
        lo[...], box[...], preferred_element_type=jnp.float32
    )


def coherence(epochs, part, sums, out):
    start = lax.rem(lax.axis_index("date"), 2) * HALF + part * ITEMS
    for owner in range(4):
        rows = []
        for kk in range(4):
            k = owner * 4 + kk
            power_a = sums[pl.ds(pl.multiple_of(epochs[0, k] * 8, 8), 8), :]
            power_b = sums[pl.ds(pl.multiple_of(epochs[1, k] * 8, 8), 8), :]
            weight = lax.rsqrt((power_a + EPS) * (power_b + EPS))
            rows.append(sums[64 + k * 16 : 72 + k * 16, :] * weight)
            rows.append(sums[72 + k * 16 : 80 + k * 16, :] * weight)
        out[owner, pl.ds(start, ITEMS)] = jnp.swapaxes(jnp.stack(rows, axis=0), 0, 1)


def whole_kernel(epochs, own, one, two, three, box, table, out, img, hi, lo, sums):
    del table
    sums[...] = add_lines(epochs, (own, one, two, three), box, img, hi, lo) * SCALE
    coherence(epochs, 0, sums, out)


def most_kernel(epochs, own, one, two, three, box, after, later, img, hi, lo, sums):
    del after, sums
    later[...] = add_lines(epochs, (own, one, two, three), box, img, hi, lo)


def last_kernel(epochs, own, one, two, three, box, most, given, out, img, hi, lo, sums):
    del given
    total = add_lines(epochs, (own, one, two, three), box, img, hi, lo)
    sums[...] = (total + most[...]) * SCALE
    coherence(epochs, 1, sums, out)


def looks(kernel, epochs, operands, out_shape, lines, aliases={}):
    work = lines * ITEMS * RG * (PAIRS * 8 + DATES * 4) + 4 * ROWS * RG * LCOL
    return pl.pallas_call(
        kernel,
        out_shape=out_shape,
        grid_spec=pltpu.PrefetchScalarGridSpec(
            num_scalar_prefetch=1,
            grid=(),
            in_specs=[VMEM if x.ndim > 1 else SMEM for x in operands],
            out_specs=jax.tree.map(lambda _: VMEM, out_shape),
            scratch_shapes=[
                pltpu.VMEM((DATES, lines, 16, RG), jnp.float32),
                pltpu.VMEM((ROWS, RG), jnp.bfloat16),
                pltpu.VMEM((ROWS, RG), jnp.bfloat16),
                pltpu.VMEM((ROWS, LCOL), jnp.float32),
            ],
        ),
        input_output_aliases=aliases,
        cost_estimate=pl.CostEstimate(
            flops=work, bytes_accessed=DATES * lines * 16 * RG * 2, transcendentals=0
        ),
        compiler_params=pltpu.CompilerParams(vmem_limit_bytes=24 << 20),
    )(epochs, *operands)


def place_kernel(table, got, out, rows):
    half = lax.div(lax.axis_index("tile"), HALF)
    for burst in range(32):
        position = table[burst]
        valid = jnp.where(position < table[32], 1.0, 0.0).astype(jnp.float32)
        base = pl.multiple_of(position * 16, 16)
        rows[pl.ds(base, 8), :] = got[half, burst] * valid
        rows[pl.ds(base + 8, 8), :] = got[2 + half, burst] * valid
    for plane in range(8):
        for part in range(8):
            out[plane // 2, plane % 2, part * 8 : part * 8 + 8, :] = rows[
                pl.ds(part * 64 + plane, 8, stride=8), :
            ]


def on_device(complex_images, segment_position_map, usable_position_total, interferogram_epochs):
    images = complex_images[:, 0].transpose(0, 1, 3, 2, 4)
    epochs = interferogram_epochs.T
    table = jnp.concatenate([segment_position_map[0], usable_position_total])
    box = (
        jnp.arange(RG)[:, None] // LOOK_RG == jnp.arange(LCOL)[None, :]
    ).astype(jnp.bfloat16)

    first = meet(*cut(images, CHUNKS[0]))
    second = meet(*cut(images, CHUNKS[1], first[3]))

    shape = jax.ShapeDtypeStruct((4, 32, 8, LCOL), jnp.float32)
    partial = jax.ShapeDtypeStruct((ROWS, LCOL), jnp.float32)
    gamma = looks(whole_kernel, epochs, (*first, box, table), shape, 5)
    third = meet(*cut(images, CHUNKS[2], gamma))
    most = looks(most_kernel, epochs, (*second, box, gamma), partial, 4)
    gamma = looks(last_kernel, epochs, (*third, box, most, gamma), shape, 1, {7: 0})
    got = lax.all_to_all(
        gamma.reshape(128, 8, LCOL), ("date", "tile"), split_axis=0, concat_axis=0, tiled=True
    ).reshape(4, 32, 8, LCOL)
    return pl.pallas_call(
        place_kernel,
        out_shape=jax.ShapeDtypeStruct((4, 2, 64, LCOL), jnp.float32),
        grid_spec=pltpu.PrefetchScalarGridSpec(
            num_scalar_prefetch=1,
            grid=(),
            in_specs=[VMEM],
            out_specs=VMEM,
            scratch_shapes=[pltpu.VMEM((512, LCOL), jnp.float32)],
        ),
        compiler_params=pltpu.CompilerParams(vmem_limit_bytes=4 << 20),
    )(table, got)


def solution(mesh):
    in_specs = (P("date", "tile", None, None, None, None), P("tile", None), P("tile"), P())
    out_specs = P("date", None, None, "tile")
    return jax.shard_map(
        on_device, mesh=mesh, in_specs=in_specs, out_specs=out_specs, check_vma=False
    )
```
